32 devices in a mesh: groups: 2 (over x), dom: 2 (over core), seq: 8 (over z, y).
Axes of the slice: x: 2, y: 2, z: 4, core: 2. Of those that a mesh axis runs over, the one named last changes fastest.
Arguments:
- latents: bfloat16 [16, 512, 1536], P(('groups', 'dom'), 'seq'), parts along dimension 0, may hold values from -6 to 6
- queries: bfloat16 [16, 512, 1536], P(('groups', 'dom'), 'seq'), parts along dimension 0, may hold values from -64 to 64
- keys: bfloat16 [16, 512, 1536], P(('groups', 'dom'), 'seq'), parts along dimension 0, may hold values from -64 to 64
- values: bfloat16 [16, 512, 1536], P(('groups', 'dom'), 'seq'), parts along dimension 0, may hold values from -6 to 6
- out_weight: bfloat16 [1536, 1536], replicated, may hold values from -0.15625 to 0.15625
- step_index: int32 [2], P('groups'), parts along dimension 0, may hold values from 1 to 27
- embed_weight: bfloat16 [1536, 1024], P('seq'), may hold values from -0.15625 to 0.15625
- norm_gain: float32 [1024], replicated, may hold values from 0.1 to 1.9
- up_weight: bfloat16 [1024, 4096], P(None, 'seq'), may hold values from -0.1875 to 0.1875
- head_weight: float32 [4096], replicated, may hold values from -0.09375 to 0.09375
- prev_logw: float32 [16], P(('groups', 'dom')), parts along dimension 0, may hold values from -20 to 320
- ancestors: int32 [16], P(('groups', 'dom')), parts along dimension 0, may hold values from 0 to 7
Outputs:
- resampled: bfloat16 [16, 512, 1536], P(('groups', 'dom'), 'seq'), parts along dimension 0
- log_weights: float32 [16], P(('groups', 'dom')), parts along dimension 0
The draws below stay inside these ranges and needn't reach their ends.
There are 2 independent parts, one for each index of `groups`. The reference program is written for one: setup_inputs(seed, part) draws one part's arguments, and reference() takes and returns one part's arrays. A program takes and returns all parts, laid end to end along the dimension named above; an argument that names none is the same for every part. Nothing has to cross between parts.
Inputs may be any that keep to these rules, and one draw needn't show every extreme that they name: `ancestors`: index of a particle of the same group.
All inputs are finite; a program needn't handle non-finite values.
Results may differ from the reference program's by a relative error of at most 0.0014.
Values may be sent and summed in bfloat16 or wider, within the bound.
A program may use at most 128 MiB of HBM per device.

```python
import math
import jax
import jax.numpy as jnp
from jax import lax

D = 1536
HEADS = 24
RW = 1024
RH = 4096
STEPS = 28
P_SIZE = 8
TOKENS = 512


def query_key_pair(key):
    base = jax.random.fold_in(key, 11)
    first_key, second_key = jax.random.split(base)
    key_rows = jnp.clip(jax.random.normal(first_key, (P_SIZE, TOKENS, D), jnp.float32), -6.0, 6.0)
    query_rows = jnp.clip(jax.random.normal(second_key, (P_SIZE, TOKENS, D), jnp.float32), -6.0, 6.0)
    return (query_rows, key_rows)


def draw_queries(key, part):
    return query_key_pair(key)[0].astype(jnp.bfloat16)


def draw_keys(key, part):
    return query_key_pair(key)[1].astype(jnp.bfloat16)


def draw_prev_logw(key, part):
    base = jax.random.fold_in(key, 23)
    drawn = jnp.clip(2.0 * jax.random.normal(base, (P_SIZE,), jnp.float32), -20.0, 20.0)
    return drawn


def set_ends(result, own_key, least, high):
    place = [jax.random.randint(jax.random.fold_in(own_key, axis), (), 0, length) for axis, length in enumerate(result.shape)]
    main_axis = result.shape.index(max(result.shape))
    next_to = place[:main_axis] + [(place[main_axis] + 1) % result.shape[main_axis]] + place[main_axis + 1:]
    return result.at[tuple(place)].set(least).at[tuple(next_to)].set(high)


def shard_levels(own_key, extent, cuts, low, top_value):
    def one(axis_at, parts):
        draws = jax.random.uniform(jax.random.fold_in(jax.random.fold_in(own_key, 6), axis_at), (parts,), jnp.float32, low / len(cuts), top_value / len(cuts))
        return jnp.repeat(jnp.exp(draws), extent[axis_at] // parts).reshape((-1,) + (1,) * (len(extent) - axis_at - 1))

    factor_of = one(*cuts[0])
    for cut in cuts[1:]:
        factor_of = factor_of * one(*cut)
    return factor_of


def centred(stream_key, extent, deviation, limit, shards=(), kind=jnp.bfloat16):
    result = jax.random.normal(stream_key, extent, jnp.float32) * deviation
    if len(shards) > 0:
        result = shard_levels(stream_key, extent, shards, -0.22, 0.18) * result
    return jnp.clip(result, min=-limit, max=limit).astype(kind)


def setup_inputs(seed: int = 0, part: int = 0) -> dict:
    arg_keys = jax.random.split(jax.random.key(seed), 13)
    part_keys = jax.random.split(jax.random.fold_in(arg_keys[12], part), 13)
    return {
        "latents": centred(part_keys[0], (P_SIZE, TOKENS, D), 1.0, 6.0, ((0, 2), (1, 8))),
        "queries": draw_queries(jax.random.fold_in(jax.random.fold_in(arg_keys[12], part), 71), part),
        "keys": draw_keys(jax.random.fold_in(jax.random.fold_in(arg_keys[12], part), 71), part),
        "values": centred(part_keys[3], (P_SIZE, TOKENS, D), 1.0, 6.0, ((0, 2), (1, 8))),
        "out_weight": centred(arg_keys[4], (D, D), D ** -0.5, 0.15625),
        "step_index": jax.random.randint(part_keys[5], (1,), 1, STEPS).astype(jnp.int32),
        "embed_weight": centred(arg_keys[6], (D, RW), D ** -0.5, 0.15625, ((0, 8),)),
        "norm_gain": jnp.clip(1.0 + 0.18 * jax.random.normal(arg_keys[7], (RW,), jnp.float32), 0.1, 1.9),
        "up_weight": centred(arg_keys[8], (RW, RH), RW ** -0.5, 0.1875, ((1, 8),)),
        "head_weight": centred(arg_keys[9], (RH,), RH ** -0.5, 0.09375, (), jnp.float32),
        "prev_logw": draw_prev_logw(jax.random.fold_in(jax.random.fold_in(arg_keys[12], part), 71), part),
        "ancestors": set_ends(jax.random.randint(part_keys[11], (P_SIZE,), 0, P_SIZE), jax.random.fold_in(part_keys[11], 1), 0, P_SIZE - 1).astype(jnp.int32),
    }


potential_scale = 4.0
norm_eps = 1e-05

def particle_attention(triple):
    query_rows, key_rows, value_rows = triple
    head_width = D // HEADS
    query_heads = query_rows.reshape(TOKENS, HEADS, head_width).astype(jnp.float32)
    key_heads = key_rows.reshape(TOKENS, HEADS, head_width).astype(jnp.float32)
    value_heads = value_rows.reshape(TOKENS, HEADS, head_width).astype(jnp.float32)
    scores = jnp.einsum('qhd,khd->hqk', query_heads, key_heads) * (1.0 / math.sqrt(head_width))
    highest = lax.optimization_barrier(jnp.max(scores, axis=-1, keepdims=True))
    expanded = jnp.exp(scores - highest)
    soft_weights = (expanded / lax.optimization_barrier(jnp.sum(expanded, axis=-1, keepdims=True))).astype(jnp.bfloat16)
    soft_weights = lax.optimization_barrier(soft_weights).astype(jnp.float32)
    attended = jnp.einsum('hqk,khd->qhd', soft_weights, value_heads)
    return attended.reshape(TOKENS, D).astype(jnp.bfloat16)

def reference(latents, queries, keys, values, out_weight, step_index, embed_weight, norm_gain, up_weight, head_weight, prev_logw, ancestors):
    attended = lax.map(particle_attention, (queries, keys, values))
    flat = latents.reshape(P_SIZE * TOKENS, D).astype(jnp.float32)
    velocity = flat + jnp.dot(attended.reshape(P_SIZE * TOKENS, D), out_weight, preferred_element_type=jnp.float32)
    sigma = step_index[0].astype(jnp.float32) / STEPS
    clean = (flat - sigma * velocity).astype(jnp.bfloat16)
    stepped = (flat - velocity / STEPS).astype(jnp.bfloat16)
    embedded = jnp.dot(clean, embed_weight, preferred_element_type=jnp.float32)
    centre = lax.optimization_barrier(jnp.mean(embedded, axis=1, keepdims=True))
    centered = embedded - centre
    variance = lax.optimization_barrier(jnp.mean(centered * centered, axis=1, keepdims=True))
    features = jax.nn.gelu(centered * lax.rsqrt(variance + norm_eps) * norm_gain[None, :]).astype(jnp.bfloat16)
    hidden = jax.nn.gelu(jnp.dot(features, up_weight, preferred_element_type=jnp.float32))
    token_score = lax.optimization_barrier(jnp.sum(hidden * head_weight[None, :], axis=1))
    reward = lax.optimization_barrier(jnp.sum(token_score.reshape(P_SIZE, TOKENS), axis=1)) / math.sqrt(TOKENS)
    logits = prev_logw + potential_scale * reward
    highest = jnp.max(logits)
    log_weights = logits - (highest + jnp.log(jnp.sum(jnp.exp(logits - highest))))
    resampled = jnp.take(stepped.reshape(P_SIZE, TOKENS, D), ancestors, axis=0)
    return (resampled, log_weights)
```

```python
import functools
import math

import jax
import jax.numpy as jnp
from jax import lax
from jax.experimental import pallas as pl
from jax.experimental.pallas import tpu as pltpu
from jax.sharding import PartitionSpec as P

HEADS = 24
STEPS = 28
LANES = 128
MESH = pl.DeviceIdType.MESH

potential_scale = 4.0
norm_eps = 1e-05


def attend_plain(qb, kb, vb, ob, row, rows, column, head_width):
    cols = pl.ds(column, head_width)
    rescale = math.log2(math.e) / math.sqrt(head_width)
    scores = lax.dot_general(
        qb[pl.ds(row, rows), cols],
        kb[:, cols],
        (((1,), (1,)), ((), ())),
        preferred_element_type=jnp.float32,
    )
    highest = jnp.max(scores, axis=-1, keepdims=True)
    expanded = jnp.exp2((scores - highest) * rescale)
    total = jnp.sum(expanded, axis=-1, keepdims=True)
    mixed = jnp.dot(
        expanded.astype(jnp.bfloat16), vb[:, cols], preferred_element_type=jnp.float32
    )
    ob[pl.ds(row, rows), cols] = (mixed / total).astype(ob.dtype)


def attend_pair(qb, kb, vb, ob, row, rows, column, head_width):
    cols = pl.ds(pl.multiple_of(column, LANES), LANES)
    rescale = math.log2(math.e) / math.sqrt(head_width)
    query = qb[pl.ds(row, rows), cols]
    key = kb[:, cols]
    value = vb[:, cols]
    query_low = lax.broadcasted_iota(jnp.int32, query.shape, 1) < head_width
    value_low = lax.broadcasted_iota(jnp.int32, value.shape, 1) < head_width
    results = []
    for head in range(2):
        own_query = query_low if head == 0 else jnp.logical_not(query_low)
        own_value = value_low if head == 0 else jnp.logical_not(value_low)
        scores = lax.dot_general(
            jnp.where(own_query, query, jnp.zeros_like(query)),
            key,
            (((1,), (1,)), ((), ())),
            preferred_element_type=jnp.float32,
        )
        highest = jnp.max(scores, axis=-1, keepdims=True)
        expanded = jnp.exp2((scores - highest) * rescale).astype(jnp.bfloat16)
        results.append(
            jnp.dot(
                expanded,
                jnp.where(own_value, value, jnp.ones_like(value)),
                preferred_element_type=jnp.float32,
            )
        )
    first, second = results
    low = lax.broadcasted_iota(jnp.int32, first.shape, 1) < head_width
    mixed = jnp.where(low, first, second)
    total = pltpu.roll(jnp.where(low, second, first), head_width, 1)
    ob[pl.ds(row, rows), cols] = (mixed / total).astype(ob.dtype)


def piece(ref, item, groups, cols, start, width):
    if groups == 0:
        return ref.at[item]
    offset = pl.multiple_of((item % groups) * cols + start, LANES)
    return ref.at[item // groups, :, pl.ds(offset, width)]


def weight_exchange(
    n, fan, group_count, dom_count, embed_ref, up_ref, embed_full, up_full,
    shard_own, line_send, line_recv, fan_send, fan_recv, group_send, group_recv, dom_send, dom_recv,
):
    me = lax.axis_index("seq")
    my_group = lax.axis_index("groups")
    my_dom = lax.axis_index("dom")
    share_count = group_count * dom_count
    embed_rows, embed_cols = embed_ref.shape
    up_rows, up_cols = up_ref.shape
    embed_part = embed_cols // share_count
    up_part = up_rows // share_count

    def share(which, owner, group, dom, own=False):
        part = group * dom_count + dom
        if which == 0:
            columns = pl.ds(pl.multiple_of(part * embed_part, LANES), embed_part)
            if own:
                return embed_ref.at[:, columns]
            return embed_full.at[
                pl.ds(pl.multiple_of(owner * embed_rows, 16), embed_rows), columns
            ]
        rows = pl.ds(pl.multiple_of(part * up_part, 16), up_part)
        if own:
            return up_ref.at[rows, :]
        return up_full.at[rows, pl.ds(pl.multiple_of(owner * up_cols, LANES), up_cols)]

    def shard_copy(which):
        if which == 0:
            target = embed_full.at[pl.ds(pl.multiple_of(me * embed_rows, 16), embed_rows), :]
            return pltpu.make_async_copy(embed_ref, target, shard_own.at[0])
        target = up_full.at[:, pl.ds(pl.multiple_of(me * up_cols, LANES), up_cols)]
        return pltpu.make_async_copy(up_ref, target, shard_own.at[1])

    place = lax.div(me, fan)
    lane = lax.rem(me, fan)
    length = n // fan
    signs = (1, -1)

    def line_copy(which, direction, step, incoming):
        sign = signs[direction]
        origin = place - sign * (step if incoming else step - 1)
        owner = lax.rem(origin + n, length) * fan + lane
        to = lax.rem(place + sign + n, length) * fan + lane
        return pltpu.make_async_remote_copy(
            src_ref=share(which, owner, my_group, my_dom, own=step == 1 and not incoming),
            dst_ref=share(which, owner, my_group, my_dom),
            send_sem=line_send.at[which, direction, step - 1],
            recv_sem=line_recv.at[which, direction, step - 1],
            device_id={"seq": to},
            device_id_type=MESH,
        )

    def receives(direction, step):
        return place >= step if direction == 0 else place + step < length

    def sends(direction, step):
        if direction == 0:
            return jnp.logical_and(place >= step - 1, place + 1 < length)
        return jnp.logical_and(place + step - 1 < length, place >= 1)

    def fan_copy(which, spot, shift, incoming, own=False):
        to = lax.rem(lane + shift, fan)
        source = lax.rem(lane - shift + fan, fan) if incoming else lane
        owner = spot * fan + source
        return pltpu.make_async_remote_copy(
            src_ref=share(which, owner, my_group, my_dom, own=own),
            dst_ref=share(which, owner, my_group, my_dom),
            send_sem=fan_send.at[which, shift, spot],
            recv_sem=fan_recv.at[which, shift, spot],
            device_id={"seq": place * fan + to},
            device_id_type=MESH,
        )

    def group_copy(which, owner, shift, incoming):
        other = lax.rem(my_group + shift, group_count)
        source = lax.rem(my_group - shift + group_count, group_count) if incoming else my_group
        return pltpu.make_async_remote_copy(
            src_ref=share(which, owner, source, my_dom),
            dst_ref=share(which, owner, source, my_dom),
            send_sem=group_send.at[which, shift, owner],
            recv_sem=group_recv.at[which, shift, owner],
            device_id={"groups": other},
            device_id_type=MESH,
        )

    def dom_copy(which, owner, shift, group_shift, incoming):
        other = lax.rem(my_dom + shift, dom_count)
        source = lax.rem(my_dom - shift + dom_count, dom_count) if incoming else my_dom
        group = lax.rem(my_group - group_shift + group_count, group_count)
        return pltpu.make_async_remote_copy(
            src_ref=share(which, owner, group, source),
            dst_ref=share(which, owner, group, source),
            send_sem=dom_send.at[which, shift, group_shift, owner],
            recv_sem=dom_recv.at[which, shift, group_shift, owner],
            device_id={"dom": other},
            device_id_type=MESH,
        )

    def spread(which, owner):
        for shift in range(1, group_count):
            group_copy(which, owner, shift, False).start()
        for shift in range(1, dom_count):
            dom_copy(which, owner, shift, 0, False).start()

    def each_arrival(step, action):
        for direction in range(2):

            @pl.when(receives(direction, step))
            def _(direction=direction):
                for which in range(2):
                    action(which, direction, place - signs[direction] * step)

    def line_start():
        for which in range(2):
            for direction in range(2):

                @pl.when(sends(direction, 1))
                def _(which=which, direction=direction):
                    line_copy(which, direction, 1, False).start()

            for shift in range(1, fan):
                fan_copy(which, place, shift, False, own=True).start()
            shard_copy(which).start()

    def line_step(step):
        def action(which, direction, spot):
            line_copy(which, direction, step, True).wait_recv()
            if step + 1 < length:

                @pl.when(sends(direction, step + 1))
                def _():
                    line_copy(which, direction, step + 1, False).start()

            for shift in range(1, fan):
                fan_copy(which, spot, shift, False).start()
            spread(which, spot * fan + lane)

        each_arrival(step, action)

    def fan_step(step):
        def action(which, direction, spot):
            for shift in range(1, fan):
                fan_copy(which, spot, shift, True).wait_recv()
                spread(which, spot * fan + lax.rem(lane - shift + fan, fan))

        if step == 0:
            for which in range(2):
                action(which, 0, place)
        else:
            each_arrival(step, action)

    def group_block(which, owner):
        for group_shift in range(1, group_count):
            group_copy(which, owner, group_shift, True).wait_recv()
            for shift in range(1, dom_count):
                dom_copy(which, owner, shift, group_shift, False).start()

    def group_step(step):
        def action(which, direction, spot):
            if step > 0:
                group_block(which, spot * fan + lane)
            for shift in range(1, fan):
                group_block(which, spot * fan + lax.rem(lane - shift + fan, fan))

        if step == 0:
            for which in range(2):
                action(which, 0, place)
        else:
            each_arrival(step, action)

    def weight_step(step):
        if 1 <= step < length:
            line_step(step)
        if 0 <= step - 1 < length:
            fan_step(step - 1)
        if 0 <= step - 2 < length:
            group_step(step - 2)

    weight_steps = length + 2

    def finish_weights(parts=(0, 1)):
        for which in parts:
            shard_copy(which).wait()
            for direction in range(2):
                for step in range(1, length):

                    @pl.when(sends(direction, step))
                    def _(which=which, direction=direction, step=step):
                        line_copy(which, direction, step, False).wait_send()

            @pl.loop(0, length)
            def _(spot, which=which):
                for shift in range(1, fan):
                    fan_copy(which, spot, shift, False).wait_send()

            @pl.loop(1, n)
            def _(step, which=which):
                owner = lax.rem(me + step, n)
                for shift in range(1, group_count):
                    group_copy(which, owner, shift, False).wait_send()
                for shift in range(1, dom_count):
                    for group_shift in range(group_count):
                        dom_copy(which, owner, shift, group_shift, True).wait_recv()
                        dom_copy(which, owner, shift, group_shift, False).wait_send()

    return line_start, weight_step, finish_weights, weight_steps


def attention_kernel(
    n, fan, group_count, dom_count, groups, cols, width, head_width, row_block,
    q_ref, k_ref, v_ref, embed_ref, up_ref, o_ref, embed_full, up_full,
    qb, kb, vb, ob, send_sem, recv_sem, own_sem, back_send, back_recv, back_own,
    shard_own, line_send, line_recv, fan_send, fan_recv, group_send, group_recv, dom_send, dom_recv,
):
    me = lax.axis_index("seq")
    my_group = lax.axis_index("groups")
    my_dom = lax.axis_index("dom")
    tokens = q_ref.shape[1]
    total_tokens = n * tokens
    chunks = cols // width
    inputs = ((q_ref, qb), (k_ref, kb), (v_ref, vb))

    barrier = pltpu.get_barrier_semaphore()

    @pl.loop(1, n)
    def _(step):
        pl.semaphore_signal(
            barrier, inc=1, device_id={"seq": lax.rem(me + step, n)}, device_id_type=MESH
        )

    for step in range(1, group_count):
        peer = {"groups": lax.rem(my_group + step, group_count)}
        pl.semaphore_signal(barrier, inc=1, device_id=peer, device_id_type=MESH)
    for step in range(1, dom_count):
        peer = {"dom": lax.rem(my_dom + step, dom_count)}
        pl.semaphore_signal(barrier, inc=1, device_id=peer, device_id_type=MESH)
    pl.semaphore_wait(barrier, n - 1 + group_count - 1 + dom_count - 1)

    line_start, weight_step, finish_weights, weight_steps = weight_exchange(
        n, fan, group_count, dom_count, embed_ref, up_ref, embed_full, up_full,
        shard_own, line_send, line_recv, fan_send, fan_recv, group_send, group_recv,
        dom_send, dom_recv,
    )

    def rows_of(ref, owner, chunk):
        row = pl.ds(pl.multiple_of(owner * tokens, 16), tokens)
        return ref.at[row, pl.ds(chunk * width, width)]

    def outgoing(index, chunk, target, slot):
        source, buffer = inputs[index]
        return pltpu.make_async_remote_copy(
            src_ref=piece(source, target, groups, cols, chunk * width, width),
            dst_ref=rows_of(buffer, me, chunk),
            send_sem=send_sem.at[index, chunk, target],
            recv_sem=recv_sem.at[index, chunk, slot],
            device_id={"seq": target},
            device_id_type=MESH,
        )

    def own_copy(index, chunk):
        source, buffer = inputs[index]
        return pltpu.make_async_copy(
            piece(source, me, groups, cols, chunk * width, width),
            rows_of(buffer, me, chunk),
            own_sem.at[index, chunk],
        )

    def returned(chunk, target, slot):
        return pltpu.make_async_remote_copy(
            src_ref=rows_of(ob, target, chunk),
            dst_ref=piece(o_ref, me, groups, cols, chunk * width, width),
            send_sem=back_send.at[chunk, target],
            recv_sem=back_recv.at[chunk, slot],
            device_id={"seq": target},
            device_id_type=MESH,
        )

    def own_return(chunk):
        return pltpu.make_async_copy(
            rows_of(ob, me, chunk),
            piece(o_ref, me, groups, cols, chunk * width, width),
            back_own.at[chunk],
        )

    ready = 1
    for chunk in range(chunks):
        if chunk == 0:
            line_start()
        elif ready < weight_steps:
            weight_step(ready)
            ready += 1
        for index in range(3):
            own_copy(index, chunk).start()

            @pl.loop(1, n)
            def _(step, index=index, chunk=chunk):
                outgoing(index, chunk, lax.rem(me + step, n), me).start()

    paired = 2 * head_width == LANES and width % LANES == 0
    unit = LANES if paired else head_width
    blocks = total_tokens // row_block

    for chunk in range(chunks):
        for index in range(3):
            own_copy(index, chunk).wait()

            @pl.loop(1, n)
            def _(step, index=index, chunk=chunk):
                other = lax.rem(me + step, n)
                outgoing(index, chunk, other, other).wait_recv()

        if paired:

            @pl.loop(0, (width // unit) * blocks)
            def _(step, chunk=chunk):
                attend_pair(
                    qb, kb, vb, ob,
                    pl.multiple_of((step % blocks) * row_block, row_block), row_block,
                    chunk * width + (step // blocks) * unit, head_width,
                )
        else:
            for head in range(width // unit):

                @pl.loop(0, blocks)
                def _(step, head=head, chunk=chunk):
                    attend_plain(
                        qb, kb, vb, ob,
                        pl.multiple_of(step * row_block, row_block), row_block,
                        chunk * width + head * unit, head_width,
                    )

        own_return(chunk).start()

        @pl.loop(1, n)
        def _(step, chunk=chunk):
            returned(chunk, lax.rem(me + step, n), me).start()

        if ready < weight_steps and chunk < chunks - 1:
            weight_step(ready)
            ready += 1

    for step in range(ready, weight_steps):
        weight_step(step)
    finish_weights()

    for chunk in range(chunks):
        own_return(chunk).wait()
        for index in range(3):

            @pl.loop(1, n)
            def _(step, index=index, chunk=chunk):
                outgoing(index, chunk, lax.rem(me + step, n), me).wait_send()

        @pl.loop(1, n)
        def _(step, chunk=chunk):
            other = lax.rem(me + step, n)
            returned(chunk, other, other).wait_recv()
            returned(chunk, other, me).wait_send()


def attention(queries, keys, values, embed_weight, up_weight):
    n = lax.axis_size("seq")
    group_count = lax.axis_size("groups")
    dom_count = lax.axis_size("dom")
    fan = 2 if n % 2 == 0 else 1
    particles, tokens, model_width = queries.shape
    head_width = model_width // HEADS
    per_device = particles * HEADS // n
    cols = per_device * head_width
    aligned = model_width % cols == 0 and cols % LANES == 0
    groups = model_width // cols if aligned else 0
    width = 2 * LANES if aligned and cols % (2 * LANES) == 0 else cols
    chunks = cols // width
    total_tokens = n * tokens

    def to_items(array):
        if aligned:
            return array
        split = array.reshape(particles, tokens, HEADS, head_width).transpose(0, 2, 1, 3)
        split = split.reshape(n, per_device, tokens, head_width).transpose(0, 2, 1, 3)
        return split.reshape(n, tokens, cols)

    operands = tuple(to_items(a) for a in (queries, keys, values))
    any_spec = pl.BlockSpec(memory_space=pl.ANY)
    embed_shape = (n * embed_weight.shape[0], embed_weight.shape[1])
    up_shape = (up_weight.shape[0], n * up_weight.shape[1])
    out, embed_full, up_full = pl.pallas_call(
        functools.partial(
            attention_kernel, n, fan, group_count, dom_count, groups, cols, width, head_width,
            min(256, total_tokens),
        ),
        out_shape=(
            jax.ShapeDtypeStruct(operands[0].shape, jnp.bfloat16),
            jax.ShapeDtypeStruct(embed_shape, jnp.bfloat16),
            jax.ShapeDtypeStruct(up_shape, jnp.bfloat16),
        ),
        in_specs=[any_spec] * 5,
        out_specs=(any_spec,) * 3,
        scratch_shapes=[pltpu.VMEM((total_tokens, cols), jnp.bfloat16)] * 4
        + [
            pltpu.SemaphoreType.DMA((3, chunks, n)),
            pltpu.SemaphoreType.DMA((3, chunks, n)),
            pltpu.SemaphoreType.DMA((3, chunks)),
            pltpu.SemaphoreType.DMA((chunks, n)),
            pltpu.SemaphoreType.DMA((chunks, n)),
            pltpu.SemaphoreType.DMA((chunks,)),
            pltpu.SemaphoreType.DMA((2,)),
            pltpu.SemaphoreType.DMA((2, 2, n // fan)),
            pltpu.SemaphoreType.DMA((2, 2, n // fan)),
            pltpu.SemaphoreType.DMA((2, fan, n // fan)),
            pltpu.SemaphoreType.DMA((2, fan, n // fan)),
            pltpu.SemaphoreType.DMA((2, group_count, n)),
            pltpu.SemaphoreType.DMA((2, group_count, n)),
            pltpu.SemaphoreType.DMA((2, dom_count, group_count, n)),
            pltpu.SemaphoreType.DMA((2, dom_count, group_count, n)),
        ],
        compiler_params=pltpu.CompilerParams(
            collective_id=0, has_side_effects=True, vmem_limit_bytes=60 * 1024 * 1024
        ),
        name="attention",
    )(*operands, embed_weight, up_weight)
    if not aligned:
        out = out.reshape(n, tokens, per_device, head_width).transpose(0, 2, 1, 3)
        out = out.reshape(particles, HEADS, tokens, head_width).transpose(0, 2, 1, 3)
    return out.reshape(particles * tokens, model_width), embed_full, up_full


def reward_kernel(n, doms, particles, x_ref, o_ref, held, send_sem, recv_sem):
    me = lax.axis_index("dom") * n + lax.axis_index("seq")
    members = n * doms

    def target(step):
        other = lax.rem(me + step, members)
        return other, {"dom": other // n, "seq": other % n}

    def copy(step, slot):
        other, device = target(step)
        return pltpu.make_async_remote_copy(
            src_ref=x_ref,
            dst_ref=held.at[me],
            send_sem=send_sem.at[other],
            recv_sem=recv_sem.at[slot],
            device_id=device,
            device_id_type=MESH,
        )

    barrier = pltpu.get_barrier_semaphore()

    @pl.loop(1, members)
    def _(step):
        _, device = target(step)
        pl.semaphore_signal(barrier, inc=1, device_id=device, device_id_type=MESH)

    pl.semaphore_wait(barrier, members - 1)

    @pl.loop(1, members)
    def _(step):
        copy(step, me).start()

    held[me] = x_ref[...]

    @pl.loop(1, members)
    def _(step):
        copy(step, lax.rem(me + step, members)).wait_recv()

    logits = []
    for dom in range(doms):
        rewards = jnp.sum(held[dom * n : (dom + 1) * n], axis=0)[:1]
        value = held[dom * n][1:2] + potential_scale * rewards
        used = lax.broadcasted_iota(jnp.int32, value.shape, 1) < particles
        logits.append(jnp.where(used, value, -jnp.inf))
    highest = functools.reduce(jnp.maximum, [jnp.max(v, axis=1, keepdims=True) for v in logits])
    total = sum(jnp.sum(jnp.exp(v - highest), axis=1, keepdims=True) for v in logits)
    own = logits[0]
    for dom in range(1, doms):
        own = jnp.where(lax.axis_index("dom") == dom, logits[dom], own)
    o_ref[...] = jnp.broadcast_to(own - (highest + jnp.log(total)), o_ref.shape)

    @pl.loop(1, members)
    def _(step):
        copy(step, me).wait_send()


def weigh(partial_value, prev_logw, n, doms):
    particles = partial_value.shape[0]
    rows = jnp.stack([partial_value, prev_logw])
    padded = jnp.pad(rows, ((0, 8 - 2), (0, LANES - particles)))
    vmem = pl.BlockSpec(memory_space=pltpu.VMEM)
    out = pl.pallas_call(
        functools.partial(reward_kernel, n, doms, particles),
        out_shape=jax.ShapeDtypeStruct((8, LANES), jnp.float32),
        in_specs=[vmem],
        out_specs=vmem,
        scratch_shapes=[
            pltpu.VMEM((n * doms, 8, LANES), jnp.float32),
            pltpu.SemaphoreType.DMA((n * doms,)),
            pltpu.SemaphoreType.DMA((n * doms,)),
        ],
        compiler_params=pltpu.CompilerParams(collective_id=1, has_side_effects=True),
        name="rewards",
    )(padded)
    return out[0, :particles]


def part_sum(block, rows):
    parts = [
        jnp.sum(block[at : at + rows], axis=0, keepdims=True)
        for at in range(0, block.shape[0], rows)
    ]
    return jnp.concatenate(parts, axis=0)


def fused_kernel(
    n, fan, group_count, dom_count, groups, chunks, head_width, row_block, tile,
    q_ref, k_ref, v_ref, lat_ref, wo_ref, step_ref, embed_ref, gain_ref, up_ref, head_ref,
    prev_ref, anc_ref, out_ref, logw_ref,
    qb, kb, vb, ob, mixed, embed_full, up_full, wo, lat, velocity, clean, embedded, features,
    cand, score, mine, held,
    send_sem, recv_sem, own_sem, back_send, back_recv, back_own,
    shard_own, line_send, line_recv, fan_send, fan_recv, group_send, group_recv, dom_send, dom_recv,
    load_sem, step_send, step_recv, score_send, score_recv,
):
    me = lax.axis_index("seq")
    my_group = lax.axis_index("groups")
    my_dom = lax.axis_index("dom")
    particles, tokens, model_width = q_ref.shape
    rows = particles * tokens
    cols = model_width // groups
    total_tokens = n * tokens
    inputs = ((q_ref, qb), (k_ref, kb), (v_ref, vb))
    members = n * dom_count
    member = my_dom * n + me

    def other_member(step):
        other = lax.rem(member + step, members)
        return other, {"dom": other // n, "seq": other % n}

    loads = (
        pltpu.make_async_copy(wo_ref, wo, load_sem.at[0]),
        pltpu.make_async_copy(lat_ref, lat, load_sem.at[1]),
    )

    barrier = pltpu.get_barrier_semaphore()

    @pl.loop(1, members)
    def _(step):
        _, device = other_member(step)
        pl.semaphore_signal(barrier, inc=1, device_id=device, device_id_type=MESH)

    for step in range(1, group_count):
        peer = {"groups": lax.rem(my_group + step, group_count)}
        pl.semaphore_signal(barrier, inc=1, device_id=peer, device_id_type=MESH)
    for load in loads:
        load.start()
    pl.semaphore_wait(barrier, members - 1 + group_count - 1)

    line_start, weight_step, finish_weights, weight_steps = weight_exchange(
        n, fan, group_count, dom_count, embed_ref, up_ref, embed_full, up_full,
        shard_own, line_send, line_recv, fan_send, fan_recv, group_send, group_recv,
        dom_send, dom_recv,
    )

    def source_of(ref, item, chunk):
        start, width = chunks[chunk]
        offset = pl.multiple_of(groups * start + (item % groups) * width, LANES)
        return ref.at[item // groups, :, pl.ds(offset, width)]

    def mixed_of(item, chunk):
        start, width = chunks[chunk]
        offset = pl.multiple_of(groups * start + (item % groups) * width, LANES)
        row = pl.multiple_of((item // groups) * tokens, 16)
        return mixed.at[pl.ds(row, tokens), pl.ds(offset, width)]

    def rows_of(ref, owner, chunk):
        start, width = chunks[chunk]
        row = pl.ds(pl.multiple_of(owner * tokens, 16), tokens)
        return ref.at[row, pl.ds(start, width)]

    def outgoing(index, chunk, target, slot):
        source, buffer = inputs[index]
        return pltpu.make_async_remote_copy(
            src_ref=source_of(source, target, chunk),
            dst_ref=rows_of(buffer, me, chunk),
            send_sem=send_sem.at[index, chunk, target],
            recv_sem=recv_sem.at[index, chunk, slot],
            device_id={"seq": target},
            device_id_type=MESH,
        )

    def own_copy(index, chunk):
        source, buffer = inputs[index]
        return pltpu.make_async_copy(
            source_of(source, me, chunk), rows_of(buffer, me, chunk), own_sem.at[index, chunk]
        )

    def returned(chunk, target, slot):
        return pltpu.make_async_remote_copy(
            src_ref=rows_of(ob, target, chunk),
            dst_ref=mixed_of(me, chunk),
            send_sem=back_send.at[chunk, target],
            recv_sem=back_recv.at[chunk, slot],
            device_id={"seq": target},
            device_id_type=MESH,
        )

    def own_return(chunk):
        return pltpu.make_async_copy(
            rows_of(ob, me, chunk), mixed_of(me, chunk), back_own.at[chunk]
        )

    count = len(chunks)
    ready = 1
    for chunk in range(count):
        if chunk == 0:
            line_start()
        elif ready < weight_steps:
            weight_step(ready)
            ready += 1
        for index in range(3):
            own_copy(index, chunk).start()

            @pl.loop(1, n)
            def _(step, index=index, chunk=chunk):
                outgoing(index, chunk, lax.rem(me + step, n), me).start()

    blocks = total_tokens // row_block

    for chunk in range(count):
        start, width = chunks[chunk]
        for index in range(3):
            own_copy(index, chunk).wait()

            @pl.loop(1, n)
            def _(step, index=index, chunk=chunk):
                other = lax.rem(me + step, n)
                outgoing(index, chunk, other, other).wait_recv()

        @pl.loop(0, (width // LANES) * blocks)
        def _(step, start=start):
            attend_pair(
                qb, kb, vb, ob,
                pl.multiple_of((step % blocks) * row_block, row_block), row_block,
                start + (step // blocks) * LANES, head_width,
            )

        own_return(chunk).start()

        @pl.loop(1, n)
        def _(step, chunk=chunk):
            returned(chunk, lax.rem(me + step, n), me).start()

        if ready < weight_steps and chunk < count - 1:
            weight_step(ready)
            ready += 1

    for step in range(ready, weight_steps):
        weight_step(step)
    for load in loads:
        load.wait()

    sigma = step_ref[0].astype(jnp.float32) / STEPS

    for chunk in range(count):
        start, width = chunks[chunk]
        inner = pl.ds(groups * start, groups * width)
        own_return(chunk).wait()

        @pl.loop(1, n)
        def _(step, chunk=chunk):
            other = lax.rem(me + step, n)
            returned(chunk, other, other).wait_recv()

        @pl.loop(0, model_width // tile)
        def _(step, chunk=chunk, inner=inner):
            columns = pl.ds(pl.multiple_of(step * tile, tile), tile)
            part = jnp.dot(mixed[:, inner], wo[inner, columns], preferred_element_type=jnp.float32)
            if chunk > 0:
                part = velocity[:, columns] + part
            if chunk < count - 1:
                velocity[:, columns] = part
                return
            flat = lat[:, :, columns].reshape(rows, tile).astype(jnp.float32)
            moved = flat + part
            clean[:, columns] = (flat - sigma * moved).astype(jnp.bfloat16)
            stepped = (flat - moved / STEPS).astype(jnp.bfloat16)
            for item in range(particles):
                cand[my_dom * particles + item, :, columns] = stepped[
                    item * tokens : (item + 1) * tokens
                ]

    finish_weights((0,))

    @pl.loop(0, embedded.shape[1] // tile)
    def _(step):
        columns = pl.ds(pl.multiple_of(step * tile, tile), tile)
        embedded[:, columns] = jnp.dot(
            clean[...], embed_full[:, columns], preferred_element_type=jnp.float32
        )

    def step_copy(shift, incoming):
        source = lax.rem(my_dom - shift + dom_count, dom_count) if incoming else my_dom
        block = cand.at[pl.ds(source * particles, particles)]
        return pltpu.make_async_remote_copy(
            src_ref=block,
            dst_ref=block,
            send_sem=step_send.at[shift],
            recv_sem=step_recv.at[shift],
            device_id={"dom": lax.rem(my_dom + shift, dom_count)},
            device_id_type=MESH,
        )

    for shift in range(1, dom_count):
        step_copy(shift, False).start()

    @pl.loop(0, particles)
    def _(item):
        own_rows = pl.ds(pl.multiple_of(item * tokens, tokens), tokens)
        block = embedded[own_rows, :]
        centered = block - jnp.mean(block, axis=1, keepdims=True)
        variance = jnp.mean(centered * centered, axis=1, keepdims=True)
        normed = centered * lax.rsqrt(variance + norm_eps) * gain_ref[...]
        features[own_rows, :] = jax.nn.gelu(normed).astype(jnp.bfloat16)

    finish_weights((1,))
    score[...] = jnp.zeros_like(score)

    @pl.loop(0, up_full.shape[1] // tile)
    def _(step):
        columns = pl.ds(pl.multiple_of(step * tile, tile), tile)
        hidden = jnp.dot(features[...], up_full[:, columns], preferred_element_type=jnp.float32)
        score[...] += part_sum(jax.nn.gelu(hidden), tokens) * head_ref[:, columns]

    partial_value = jnp.sum(score[...], axis=1, keepdims=True) / math.sqrt(total_tokens)
    lane = lax.broadcasted_iota(jnp.int32, (particles, LANES), 1)
    row = lax.broadcasted_iota(jnp.int32, (particles, LANES), 0)
    before = jnp.zeros((particles, LANES), jnp.float32)
    for item in range(particles):
        before = jnp.where(row == item, prev_ref[item], before)
    half = LANES // 2
    own_block = jnp.where(lane < half, partial_value, before)
    mine[0:particles, :] = own_block
    held[member, 0:particles, :] = own_block

    def score_copy(step, slot):
        other, device = other_member(step)
        return pltpu.make_async_remote_copy(
            src_ref=mine,
            dst_ref=held.at[member],
            send_sem=score_send.at[other],
            recv_sem=score_recv.at[slot],
            device_id=device,
            device_id_type=MESH,
        )

    @pl.loop(1, members)
    def _(step):
        score_copy(step, member).start()

    for shift in range(1, dom_count):
        step_copy(shift, True).wait_recv()
    for item in range(particles):
        out_ref[item] = cand[anc_ref[item]]

    for chunk in range(count):
        for index in range(3):

            @pl.loop(1, n)
            def _(step, index=index, chunk=chunk):
                outgoing(index, chunk, lax.rem(me + step, n), me).wait_send()

        @pl.loop(1, n)
        def _(step, chunk=chunk):
            returned(chunk, lax.rem(me + step, n), me).wait_send()

    for shift in range(1, dom_count):
        step_copy(shift, False).wait_send()

    @pl.loop(1, members)
    def _(step):
        score_copy(step, lax.rem(member + step, members)).wait_recv()

    logits = []
    for dom in range(dom_count):
        reward = jnp.sum(held[dom * n : (dom + 1) * n, 0:particles, :], axis=0)[:, 0:1]
        logits.append(held[dom * n, 0:particles, :][:, half : half + 1] + potential_scale * reward)
    highest = functools.reduce(
        jnp.maximum, [jnp.max(value, axis=0, keepdims=True) for value in logits]
    )
    total = sum(jnp.sum(jnp.exp(value - highest), axis=0, keepdims=True) for value in logits)
    own = logits[0]
    for dom in range(1, dom_count):
        own = jnp.where(my_dom == dom, logits[dom], own)
    logw_ref[0:particles, :] = jnp.broadcast_to(
        own - (highest + jnp.log(total)), (particles, LANES)
    )

    @pl.loop(1, members)
    def _(step):
        score_copy(step, member).wait_send()


def chunk_widths(cols):
    widths = []
    left = cols
    while left > 2 * LANES + LANES:
        widths.append(2 * LANES)
        left -= 2 * LANES
    widths += [LANES] * (left // LANES)
    starts = [sum(widths[:i]) for i in range(len(widths))]
    return tuple(zip(starts, widths))


def fused(
    latents, queries, keys, values, out_weight, step_index, embed_weight, norm_gain, up_weight,
    head_weight, prev_logw, ancestors,
):
    n = lax.axis_size("seq")
    group_count = lax.axis_size("groups")
    dom_count = lax.axis_size("dom")
    fan = 2 if n % 2 == 0 else 1
    particles, tokens, model_width = queries.shape
    head_width = model_width // HEADS
    cols = particles * model_width // n
    groups = model_width // cols
    chunks = chunk_widths(cols)
    count = len(chunks)
    rows = particles * tokens
    total_tokens = n * tokens
    members = n * dom_count
    tile = 512
    embed_shape = (n * embed_weight.shape[0], embed_weight.shape[1])
    up_shape = (up_weight.shape[0], n * up_weight.shape[1])
    hbm = pl.BlockSpec(memory_space=pl.ANY)
    vmem = pl.BlockSpec(memory_space=pltpu.VMEM)
    smem = pl.BlockSpec(memory_space=pltpu.SMEM)
    bf16 = jnp.bfloat16
    dma = pltpu.SemaphoreType.DMA
    resampled, logw = pl.pallas_call(
        functools.partial(
            fused_kernel, n, fan, group_count, dom_count, groups, chunks, head_width,
            min(256, total_tokens), tile,
        ),
        out_shape=(
            jax.ShapeDtypeStruct(latents.shape, bf16),
            jax.ShapeDtypeStruct((8, LANES), jnp.float32),
        ),
        in_specs=[hbm] * 5 + [smem, hbm, vmem, hbm, vmem, smem, smem],
        out_specs=(vmem, vmem),
        scratch_shapes=[pltpu.VMEM((total_tokens, cols), bf16)] * 4
        + [
            pltpu.VMEM((rows, model_width), bf16),
            pltpu.VMEM(embed_shape, bf16),
            pltpu.VMEM(up_shape, bf16),
            pltpu.VMEM(out_weight.shape, bf16),
            pltpu.VMEM(latents.shape, bf16),
            pltpu.VMEM((rows, model_width), jnp.float32),
            pltpu.VMEM((rows, model_width), bf16),
            pltpu.VMEM((rows, embed_shape[1]), jnp.float32),
            pltpu.VMEM((rows, embed_shape[1]), bf16),
            pltpu.VMEM((dom_count * particles, tokens, model_width), bf16),
            pltpu.VMEM((particles, tile), jnp.float32),
            pltpu.VMEM((8, LANES), jnp.float32),
            pltpu.VMEM((members, 8, LANES), jnp.float32),
            dma((3, count, n)),
            dma((3, count, n)),
            dma((3, count)),
            dma((count, n)),
            dma((count, n)),
            dma((count,)),
            dma((2,)),
            dma((2, 2, n // fan)),
            dma((2, 2, n // fan)),
            dma((2, fan, n // fan)),
            dma((2, fan, n // fan)),
            dma((2, group_count, n)),
            dma((2, group_count, n)),
            dma((2, dom_count, group_count, n)),
            dma((2, dom_count, group_count, n)),
            dma((2,)),
            dma((dom_count,)),
            dma((dom_count,)),
            dma((members,)),
            dma((members,)),
        ],
        compiler_params=pltpu.CompilerParams(
            collective_id=0, has_side_effects=True, vmem_limit_bytes=60 * 1024 * 1024
        ),
        name="step",
    )(
        queries, keys, values, latents, out_weight, step_index, embed_weight,
        norm_gain.reshape(1, -1), up_weight, head_weight.reshape(1, -1), prev_logw, ancestors,
    )
    return resampled, logw[:particles, 0]


def tiles_evenly(queries, embed_weight, up_weight):
    n = lax.axis_size("seq")
    particles, tokens, model_width = queries.shape
    if particles * HEADS % n:
        return False
    cols = particles * model_width // n
    if 2 * (model_width // HEADS) != LANES or cols % LANES or model_width % cols:
        return False
    return model_width % 512 == 0 and embed_weight.shape[1] % 512 == 0


def on_device(
    latents,
    queries,
    keys,
    values,
    out_weight,
    step_index,
    embed_weight,
    norm_gain,
    up_weight,
    head_weight,
    prev_logw,
    ancestors,
):
    seq_count = lax.axis_size("seq")
    dom_count = lax.axis_size("dom")
    local_particles, local_tokens, model_width = latents.shape
    local_rows = local_particles * local_tokens
    total_tokens = local_tokens * seq_count
    dom = lax.axis_index("dom")

    if tiles_evenly(queries, embed_weight, up_weight):
        return fused(
            latents, queries, keys, values, out_weight, step_index, embed_weight, norm_gain,
            up_weight, head_weight, prev_logw, ancestors,
        )
    attended, embed_full, up_full = attention(
        queries, keys, values, embed_weight, up_weight
    )
    flat = latents.reshape(local_rows, model_width).astype(jnp.float32)
    velocity = flat + jnp.dot(attended, out_weight, preferred_element_type=jnp.float32)
    sigma = step_index[0].astype(jnp.float32) / STEPS
    clean = (flat - sigma * velocity).astype(jnp.bfloat16)
    stepped = (flat - velocity / STEPS).astype(jnp.bfloat16)
    stepped = stepped.reshape(local_particles, local_tokens, model_width)
    candidates = [stepped]
    for shift in range(1, dom_count):
        pairs = [((to + shift) % dom_count, to) for to in range(dom_count)]
        candidates.append(lax.ppermute(stepped, "dom", pairs))
    embedded = jnp.dot(
        clean,
        embed_full,
        preferred_element_type=jnp.float32,
    )
    centre = jnp.mean(embedded, axis=1, keepdims=True)
    centered = embedded - centre
    variance = jnp.mean(centered * centered, axis=1, keepdims=True)
    features = jax.nn.gelu(centered * lax.rsqrt(variance + norm_eps) * norm_gain[None, :]).astype(
        jnp.bfloat16
    )
    scored = (
        jax.nn.gelu(
            jnp.dot(
                features,
                up_full,
                preferred_element_type=jnp.float32,
            )
        )
        * head_weight[None, :]
    )
    partial_value = jnp.sum(jnp.sum(scored, axis=1).reshape(local_particles, local_tokens), axis=1)
    partial_value = partial_value / math.sqrt(total_tokens)
    log_weights = weigh(partial_value, prev_logw, seq_count, dom_count)
    slot = lax.rem(ancestors // local_particles - dom + dom_count, dom_count)
    row = slot * local_particles + lax.rem(ancestors, local_particles)
    resampled = jnp.take(jnp.concatenate(candidates), row, axis=0, mode="clip")
    return (resampled, log_weights)


def solution(mesh):
    in_specs = (
        P(("groups", "dom"), "seq", None),
        P(("groups", "dom"), "seq", None),
        P(("groups", "dom"), "seq", None),
        P(("groups", "dom"), "seq", None),
        P(),
        P("groups"),
        P("seq", None),
        P(),
        P(None, "seq"),
        P(),
        P(("groups", "dom")),
        P(("groups", "dom")),
    )
    out_specs = (P(("groups", "dom"), "seq", None), P(("groups", "dom")))
    return jax.shard_map(
        on_device, mesh=mesh, in_specs=in_specs, out_specs=out_specs, check_vma=False
    )
```

```python
import functools
import math

import jax
import jax.numpy as jnp
from jax import lax
from jax.experimental import pallas as pl
from jax.experimental.pallas import tpu as pltpu
from jax.sharding import PartitionSpec as P

HEADS = 24
STEPS = 28
LANES = 128
MESH = pl.DeviceIdType.MESH

potential_scale = 4.0
norm_eps = 1e-05


def attend_plain(qb, kb, vb, ob, row, rows, column, head_width):
    cols = pl.ds(column, head_width)
    rescale = math.log2(math.e) / math.sqrt(head_width)
    scores = lax.dot_general(
        qb[pl.ds(row, rows), cols],
        kb[:, cols],
        (((1,), (1,)), ((), ())),
        preferred_element_type=jnp.float32,
    )
    highest = jnp.max(scores, axis=-1, keepdims=True)
    expanded = jnp.exp2((scores - highest) * rescale)
    total = jnp.sum(expanded, axis=-1, keepdims=True)
    mixed = jnp.dot(
        expanded.astype(jnp.bfloat16), vb[:, cols], preferred_element_type=jnp.float32
    )
    ob[pl.ds(row, rows), cols] = (mixed / total).astype(ob.dtype)


def attend_pair(qb, kb, vb, ob, row, rows, column, head_width):
    cols = pl.ds(pl.multiple_of(column, LANES), LANES)
    rescale = math.log2(math.e) / math.sqrt(head_width)
    query = qb[pl.ds(row, rows), cols]
    key = kb[:, cols]
    value = vb[:, cols]
    query_low = lax.broadcasted_iota(jnp.int32, query.shape, 1) < head_width
    value_low = lax.broadcasted_iota(jnp.int32, value.shape, 1) < head_width
    results = []
    for head in range(2):
        own_query = query_low if head == 0 else jnp.logical_not(query_low)
        own_value = value_low if head == 0 else jnp.logical_not(value_low)
        scores = lax.dot_general(
            jnp.where(own_query, query, jnp.zeros_like(query)),
            key,
            (((1,), (1,)), ((), ())),
            preferred_element_type=jnp.float32,
        )
        highest = jnp.max(scores, axis=-1, keepdims=True)
        expanded = jnp.exp2((scores - highest) * rescale).astype(jnp.bfloat16)
        results.append(
            jnp.dot(
                expanded,
                jnp.where(own_value, value, jnp.ones_like(value)),
                preferred_element_type=jnp.float32,
            )
        )
    first, second = results
    low = lax.broadcasted_iota(jnp.int32, first.shape, 1) < head_width
    mixed = jnp.where(low, first, second)
    total = pltpu.roll(jnp.where(low, second, first), head_width, 1)
    ob[pl.ds(row, rows), cols] = (mixed / total).astype(ob.dtype)


def piece(ref, item, groups, cols, start, width):
    if groups == 0:
        return ref.at[item]
    offset = pl.multiple_of((item % groups) * cols + start, LANES)
    return ref.at[item // groups, :, pl.ds(offset, width)]


def weight_exchange(
    n, fan, group_count, dom_count, embed_ref, up_ref, embed_full, up_full,
    shard_own, line_send, line_recv, fan_send, fan_recv, group_send, group_recv, dom_send, dom_recv,
):
    me = lax.axis_index("seq")
    my_group = lax.axis_index("groups")
    my_dom = lax.axis_index("dom")
    share_count = group_count * dom_count
    embed_rows, embed_cols = embed_ref.shape
    up_rows, up_cols = up_ref.shape
    embed_part = embed_cols // share_count
    up_part = up_rows // share_count

    def share(which, owner, group, dom, own=False):
        part = group * dom_count + dom
        if which == 0:
            columns = pl.ds(pl.multiple_of(part * embed_part, LANES), embed_part)
            if own:
                return embed_ref.at[:, columns]
            return embed_full.at[
                pl.ds(pl.multiple_of(owner * embed_rows, 16), embed_rows), columns
            ]
        rows = pl.ds(pl.multiple_of(part * up_part, 16), up_part)
        if own:
            return up_ref.at[rows, :]
        return up_full.at[rows, pl.ds(pl.multiple_of(owner * up_cols, LANES), up_cols)]

    def shard_copy(which):
        if which == 0:
            target = embed_full.at[pl.ds(pl.multiple_of(me * embed_rows, 16), embed_rows), :]
            return pltpu.make_async_copy(embed_ref, target, shard_own.at[0])
        target = up_full.at[:, pl.ds(pl.multiple_of(me * up_cols, LANES), up_cols)]
        return pltpu.make_async_copy(up_ref, target, shard_own.at[1])

    place = lax.div(me, fan)
    lane = lax.rem(me, fan)
    length = n // fan
    signs = (1, -1)

    def line_copy(which, direction, step, incoming):
        sign = signs[direction]
        origin = place - sign * (step if incoming else step - 1)
        owner = lax.rem(origin + n, length) * fan + lane
        to = lax.rem(place + sign + n, length) * fan + lane
        return pltpu.make_async_remote_copy(
            src_ref=share(which, owner, my_group, my_dom, own=step == 1 and not incoming),
            dst_ref=share(which, owner, my_group, my_dom),
            send_sem=line_send.at[which, direction, step - 1],
            recv_sem=line_recv.at[which, direction, step - 1],
            device_id={"seq": to},
            device_id_type=MESH,
        )

    def receives(direction, step):
        return place >= step if direction == 0 else place + step < length

    def sends(direction, step):
        if direction == 0:
            return jnp.logical_and(place >= step - 1, place + 1 < length)
        return jnp.logical_and(place + step - 1 < length, place >= 1)

    def fan_copy(which, spot, shift, incoming, own=False):
        to = lax.rem(lane + shift, fan)
        source = lax.rem(lane - shift + fan, fan) if incoming else lane
        owner = spot * fan + source
        return pltpu.make_async_remote_copy(
            src_ref=share(which, owner, my_group, my_dom, own=own),
            dst_ref=share(which, owner, my_group, my_dom),
            send_sem=fan_send.at[which, shift, spot],
            recv_sem=fan_recv.at[which, shift, spot],
            device_id={"seq": place * fan + to},
            device_id_type=MESH,
        )

    def group_copy(which, owner, shift, incoming):
        other = lax.rem(my_group + shift, group_count)
        source = lax.rem(my_group - shift + group_count, group_count) if incoming else my_group
        return pltpu.make_async_remote_copy(
            src_ref=share(which, owner, source, my_dom),
            dst_ref=share(which, owner, source, my_dom),
            send_sem=group_send.at[which, shift, owner],
            recv_sem=group_recv.at[which, shift, owner],
            device_id={"groups": other},
            device_id_type=MESH,
        )

    def dom_copy(which, owner, shift, group_shift, incoming):
        other = lax.rem(my_dom + shift, dom_count)
        source = lax.rem(my_dom - shift + dom_count, dom_count) if incoming else my_dom
        group = lax.rem(my_group - group_shift + group_count, group_count)
        return pltpu.make_async_remote_copy(
            src_ref=share(which, owner, group, source),
            dst_ref=share(which, owner, group, source),
            send_sem=dom_send.at[which, shift, group_shift, owner],
            recv_sem=dom_recv.at[which, shift, group_shift, owner],
            device_id={"dom": other},
            device_id_type=MESH,
        )

    def spread(which, owner):
        for shift in range(1, group_count):
            group_copy(which, owner, shift, False).start()
        for shift in range(1, dom_count):
            dom_copy(which, owner, shift, 0, False).start()

    def each_arrival(step, action):
        for direction in range(2):

            @pl.when(receives(direction, step))
            def _(direction=direction):
                for which in range(2):
                    action(which, direction, place - signs[direction] * step)

    def line_start():
        for which in range(2):
            for direction in range(2):

                @pl.when(sends(direction, 1))
                def _(which=which, direction=direction):
                    line_copy(which, direction, 1, False).start()

            for shift in range(1, fan):
                fan_copy(which, place, shift, False, own=True).start()
            shard_copy(which).start()

    def line_step(step):
        def action(which, direction, spot):
            line_copy(which, direction, step, True).wait_recv()
            if step + 1 < length:

                @pl.when(sends(direction, step + 1))
                def _():
                    line_copy(which, direction, step + 1, False).start()

            for shift in range(1, fan):
                fan_copy(which, spot, shift, False).start()
            spread(which, spot * fan + lane)

        each_arrival(step, action)

    def fan_step(step):
        def action(which, direction, spot):
            for shift in range(1, fan):
                fan_copy(which, spot, shift, True).wait_recv()
                spread(which, spot * fan + lax.rem(lane - shift + fan, fan))

        if step == 0:
            for which in range(2):
                action(which, 0, place)
        else:
            each_arrival(step, action)

    def group_block(which, owner):
        for group_shift in range(1, group_count):
            group_copy(which, owner, group_shift, True).wait_recv()
            for shift in range(1, dom_count):
                dom_copy(which, owner, shift, group_shift, False).start()

    def group_step(step):
        def action(which, direction, spot):
            if step > 0:
                group_block(which, spot * fan + lane)
            for shift in range(1, fan):
                group_block(which, spot * fan + lax.rem(lane - shift + fan, fan))

        if step == 0:
            for which in range(2):
                action(which, 0, place)
        else:
            each_arrival(step, action)

    def move_step(step):
        if 1 <= step < length:
            line_step(step)
        if 0 <= step - 1 < length:
            fan_step(step - 1)


    def finish_weights(parts=(0, 1)):
        for which in parts:
            shard_copy(which).wait()
            for direction in range(2):
                for step in range(1, length):

                    @pl.when(sends(direction, step))
                    def _(which=which, direction=direction, step=step):
                        line_copy(which, direction, step, False).wait_send()

            @pl.loop(0, length)
            def _(spot, which=which):
                for shift in range(1, fan):
                    fan_copy(which, spot, shift, False).wait_send()

            @pl.loop(1, n)
            def _(step, which=which):
                owner = lax.rem(me + step, n)
                for shift in range(1, group_count):
                    group_copy(which, owner, shift, False).wait_send()
                for shift in range(1, dom_count):
                    for group_shift in range(group_count):
                        dom_copy(which, owner, shift, group_shift, True).wait_recv()
                        dom_copy(which, owner, shift, group_shift, False).wait_send()

    return line_start, move_step, group_step, finish_weights, length


def take(semaphore, region):
    pltpu.make_async_copy(region, region, semaphore).wait()


def shared_weight_exchange(
    n, fan, group_count, dom_count, embed_ref, up_ref, embed_full, up_full,
    shard_own, line_send, line_recv, fan_send, fan_recv, group_send, group_recv, dom_send, dom_recv,
):
    me = lax.axis_index("seq")
    my_group = lax.axis_index("groups")
    my_dom = lax.axis_index("dom")
    share_count = group_count * dom_count
    embed_rows, embed_cols = embed_ref.shape
    up_rows, up_cols = up_ref.shape
    embed_part = embed_cols // share_count
    up_part = up_rows // share_count

    def share(which, owner, group, dom, own=False):
        part = group * dom_count + dom
        if which == 0:
            columns = pl.ds(pl.multiple_of(part * embed_part, LANES), embed_part)
            if own:
                return embed_ref.at[:, columns]
            return embed_full.at[
                pl.ds(pl.multiple_of(owner * embed_rows, 16), embed_rows), columns
            ]
        rows = pl.ds(pl.multiple_of(part * up_part, 16), up_part)
        if own:
            return up_ref.at[rows, :]
        return up_full.at[rows, pl.ds(pl.multiple_of(owner * up_cols, LANES), up_cols)]

    def shard_copy(which):
        if which == 0:
            target = embed_full.at[pl.ds(pl.multiple_of(me * embed_rows, 16), embed_rows), :]
            return pltpu.make_async_copy(embed_ref, target, shard_own.at[0])
        target = up_full.at[:, pl.ds(pl.multiple_of(me * up_cols, LANES), up_cols)]
        return pltpu.make_async_copy(up_ref, target, shard_own.at[1])

    place = lax.div(me, fan)
    lane = lax.rem(me, fan)
    length = n // fan
    signs = (1, -1)

    def line_copy(which, direction, step, incoming):
        sign = signs[direction]
        origin = place - sign * (step if incoming else step - 1)
        owner = lax.rem(origin + n, length) * fan + lane
        to = lax.rem(place + sign + n, length) * fan + lane
        return pltpu.make_async_remote_copy(
            src_ref=share(which, owner, my_group, my_dom, own=step == 1 and not incoming),
            dst_ref=share(which, owner, my_group, my_dom),
            send_sem=line_send.at[which, direction, step - 1],
            recv_sem=line_recv.at[which, direction, step - 1],
            device_id={"seq": to},
            device_id_type=MESH,
        )

    def receives(direction, step):
        return place >= step if direction == 0 else place + step < length

    def sends(direction, step):
        if direction == 0:
            return jnp.logical_and(place >= step - 1, place + 1 < length)
        return jnp.logical_and(place + step - 1 < length, place >= 1)

    def fan_copy(which, spot, shift, incoming, own=False):
        to = lax.rem(lane + shift, fan)
        source = lax.rem(lane - shift + fan, fan) if incoming else lane
        owner = spot * fan + source
        return pltpu.make_async_remote_copy(
            src_ref=share(which, owner, my_group, my_dom, own=own),
            dst_ref=share(which, owner, my_group, my_dom),
            send_sem=fan_send.at[which, shift - 1],
            recv_sem=fan_recv.at[which, shift - 1, spot],
            device_id={"seq": place * fan + to},
            device_id_type=MESH,
        )

    def group_copy(which, owner, shift, incoming):
        other = lax.rem(my_group + shift, group_count)
        source = lax.rem(my_group - shift + group_count, group_count) if incoming else my_group
        return pltpu.make_async_remote_copy(
            src_ref=share(which, owner, source, my_dom),
            dst_ref=share(which, owner, source, my_dom),
            send_sem=group_send.at[which, shift - 1],
            recv_sem=group_recv.at[which, shift - 1, owner],
            device_id={"groups": other},
            device_id_type=MESH,
        )

    def dom_copy(which, owner, shift, group_shift, incoming):
        other = lax.rem(my_dom + shift, dom_count)
        source = lax.rem(my_dom - shift + dom_count, dom_count) if incoming else my_dom
        group = lax.rem(my_group - group_shift + group_count, group_count)
        return pltpu.make_async_remote_copy(
            src_ref=share(which, owner, group, source),
            dst_ref=share(which, owner, group, source),
            send_sem=dom_send.at[which, shift - 1],
            recv_sem=dom_recv.at[which, shift - 1],
            device_id={"dom": other},
            device_id_type=MESH,
        )

    def spread(which, owner):
        for shift in range(1, group_count):
            group_copy(which, owner, shift, False).start()
        for shift in range(1, dom_count):
            dom_copy(which, owner, shift, 0, False).start()

    def each_arrival(step, action):
        for direction in range(2):

            @pl.when(receives(direction, step))
            def _(direction=direction):
                for which in range(2):
                    action(which, direction, place - signs[direction] * step)

    def line_start():
        for which in range(2):
            for direction in range(2):

                @pl.when(sends(direction, 1))
                def _(which=which, direction=direction):
                    line_copy(which, direction, 1, False).start()

            for shift in range(1, fan):
                fan_copy(which, place, shift, False, own=True).start()
            shard_copy(which).start()

    def line_step(step):
        def action(which, direction, spot):
            line_copy(which, direction, step, True).wait_recv()
            if step + 1 < length:

                @pl.when(sends(direction, step + 1))
                def _():
                    line_copy(which, direction, step + 1, False).start()

            for shift in range(1, fan):
                fan_copy(which, spot, shift, False).start()
            spread(which, spot * fan + lane)

        each_arrival(step, action)

    def fan_step(step):
        def action(which, direction, spot):
            for shift in range(1, fan):
                fan_copy(which, spot, shift, True).wait_recv()
                spread(which, spot * fan + lax.rem(lane - shift + fan, fan))

        if step == 0:
            for which in range(2):
                action(which, 0, place)
        else:
            each_arrival(step, action)

    def group_block(which, owner):
        for group_shift in range(1, group_count):
            group_copy(which, owner, group_shift, True).wait_recv()
            for shift in range(1, dom_count):
                dom_copy(which, owner, shift, group_shift, False).start()

    def group_step(step):
        def action(which, direction, spot):
            if step > 0:
                group_block(which, spot * fan + lane)
            for shift in range(1, fan):
                group_block(which, spot * fan + lax.rem(lane - shift + fan, fan))

        if step == 0:
            for which in range(2):
                action(which, 0, place)
        else:
            each_arrival(step, action)

    def move_step(step):
        if 1 <= step < length:
            line_step(step)
        if 0 <= step - 1 < length:
            fan_step(step - 1)


    def parts_of(which, amount):
        if which == 0:
            wide = math.gcd(amount, share_count)
            return embed_full.at[0 : amount // wide * embed_rows, 0 : wide * embed_part]
        wide = math.gcd(amount, share_count)
        return up_full.at[0 : wide * up_part, 0 : amount // wide * up_cols]

    def finish_weights(parts=(0, 1)):
        for which in parts:
            shard_copy(which).wait()
            for direction in range(2):
                for step in range(1, length):

                    @pl.when(sends(direction, step))
                    def _(which=which, direction=direction, step=step):
                        line_copy(which, direction, step, False).wait_send()

            for shift in range(1, fan):
                take(fan_send.at[which, shift - 1], parts_of(which, length))
            for shift in range(1, group_count):
                take(group_send.at[which, shift - 1], parts_of(which, n - 1))
            for shift in range(1, dom_count):
                take(dom_recv.at[which, shift - 1], parts_of(which, (n - 1) * group_count))
                take(dom_send.at[which, shift - 1], parts_of(which, (n - 1) * group_count))

    return line_start, move_step, group_step, finish_weights, length


def attention_kernel(
    n, fan, group_count, dom_count, groups, cols, width, head_width, row_block,
    q_ref, k_ref, v_ref, embed_ref, up_ref, o_ref, embed_full, up_full,
    qb, kb, vb, ob, send_sem, recv_sem, own_sem, back_send, back_recv, back_own,
    shard_own, line_send, line_recv, fan_send, fan_recv, group_send, group_recv, dom_send, dom_recv,
):
    me = lax.axis_index("seq")
    my_group = lax.axis_index("groups")
    my_dom = lax.axis_index("dom")
    tokens = q_ref.shape[1]
    total_tokens = n * tokens
    chunks = cols // width
    inputs = ((q_ref, qb), (k_ref, kb), (v_ref, vb))

    barrier = pltpu.get_barrier_semaphore()

    @pl.loop(1, n)
    def _(step):
        pl.semaphore_signal(
            barrier, inc=1, device_id={"seq": lax.rem(me + step, n)}, device_id_type=MESH
        )

    for step in range(1, group_count):
        peer = {"groups": lax.rem(my_group + step, group_count)}
        pl.semaphore_signal(barrier, inc=1, device_id=peer, device_id_type=MESH)
    for step in range(1, dom_count):
        peer = {"dom": lax.rem(my_dom + step, dom_count)}
        pl.semaphore_signal(barrier, inc=1, device_id=peer, device_id_type=MESH)
    pl.semaphore_wait(barrier, n - 1 + group_count - 1 + dom_count - 1)

    line_start, move_step, group_step, finish_weights, length = weight_exchange(
        n, fan, group_count, dom_count, embed_ref, up_ref, embed_full, up_full,
        shard_own, line_send, line_recv, fan_send, fan_recv, group_send, group_recv,
        dom_send, dom_recv,
    )

    def rows_of(ref, owner, chunk):
        row = pl.ds(pl.multiple_of(owner * tokens, 16), tokens)
        return ref.at[row, pl.ds(chunk * width, width)]

    def outgoing(index, chunk, target, slot):
        source, buffer = inputs[index]
        return pltpu.make_async_remote_copy(
            src_ref=piece(source, target, groups, cols, chunk * width, width),
            dst_ref=rows_of(buffer, me, chunk),
            send_sem=send_sem.at[index, chunk, target],
            recv_sem=recv_sem.at[index, chunk, slot],
            device_id={"seq": target},
            device_id_type=MESH,
        )

    def own_copy(index, chunk):
        source, buffer = inputs[index]
        return pltpu.make_async_copy(
            piece(source, me, groups, cols, chunk * width, width),
            rows_of(buffer, me, chunk),
            own_sem.at[index, chunk],
        )

    def returned(chunk, target, slot):
        return pltpu.make_async_remote_copy(
            src_ref=rows_of(ob, target, chunk),
            dst_ref=piece(o_ref, me, groups, cols, chunk * width, width),
            send_sem=back_send.at[chunk, target],
            recv_sem=back_recv.at[chunk, slot],
            device_id={"seq": target},
            device_id_type=MESH,
        )

    def own_return(chunk):
        return pltpu.make_async_copy(
            rows_of(ob, me, chunk),
            piece(o_ref, me, groups, cols, chunk * width, width),
            back_own.at[chunk],
        )

    weight_steps = length + 2

    def weight_step(step):
        move_step(step)
        if 0 <= step - 2 < length:
            group_step(step - 2)

    ready = 1
    for chunk in range(chunks):
        if chunk == 0:
            line_start()
        elif ready < weight_steps:
            weight_step(ready)
            ready += 1
        for index in range(3):
            own_copy(index, chunk).start()

            @pl.loop(1, n)
            def _(step, index=index, chunk=chunk):
                outgoing(index, chunk, lax.rem(me + step, n), me).start()

    paired = 2 * head_width == LANES and width % LANES == 0
    unit = LANES if paired else head_width
    blocks = total_tokens // row_block

    for chunk in range(chunks):
        for index in range(3):
            own_copy(index, chunk).wait()

            @pl.loop(1, n)
            def _(step, index=index, chunk=chunk):
                other = lax.rem(me + step, n)
                outgoing(index, chunk, other, other).wait_recv()

        if paired:

            @pl.loop(0, (width // unit) * blocks)
            def _(step, chunk=chunk):
                attend_pair(
                    qb, kb, vb, ob,
                    pl.multiple_of((step % blocks) * row_block, row_block), row_block,
                    chunk * width + (step // blocks) * unit, head_width,
                )
        else:
            for head in range(width // unit):

                @pl.loop(0, blocks)
                def _(step, head=head, chunk=chunk):
                    attend_plain(
                        qb, kb, vb, ob,
                        pl.multiple_of(step * row_block, row_block), row_block,
                        chunk * width + head * unit, head_width,
                    )

        own_return(chunk).start()

        @pl.loop(1, n)
        def _(step, chunk=chunk):
            returned(chunk, lax.rem(me + step, n), me).start()

        if ready < weight_steps and chunk < chunks - 1:
            weight_step(ready)
            ready += 1

    for step in range(ready, weight_steps):
        weight_step(step)
    finish_weights()

    for chunk in range(chunks):
        own_return(chunk).wait()
        for index in range(3):

            @pl.loop(1, n)
            def _(step, index=index, chunk=chunk):
                outgoing(index, chunk, lax.rem(me + step, n), me).wait_send()

        @pl.loop(1, n)
        def _(step, chunk=chunk):
            other = lax.rem(me + step, n)
            returned(chunk, other, other).wait_recv()
            returned(chunk, other, me).wait_send()


def attention(queries, keys, values, embed_weight, up_weight):
    n = lax.axis_size("seq")
    group_count = lax.axis_size("groups")
    dom_count = lax.axis_size("dom")
    fan = 2 if n % 2 == 0 else 1
    particles, tokens, model_width = queries.shape
    head_width = model_width // HEADS
    per_device = particles * HEADS // n
    cols = per_device * head_width
    aligned = model_width % cols == 0 and cols % LANES == 0
    groups = model_width // cols if aligned else 0
    width = 2 * LANES if aligned and cols % (2 * LANES) == 0 else cols
    chunks = cols // width
    total_tokens = n * tokens

    def to_items(array):
        if aligned:
            return array
        split = array.reshape(particles, tokens, HEADS, head_width).transpose(0, 2, 1, 3)
        split = split.reshape(n, per_device, tokens, head_width).transpose(0, 2, 1, 3)
        return split.reshape(n, tokens, cols)

    operands = tuple(to_items(a) for a in (queries, keys, values))
    any_spec = pl.BlockSpec(memory_space=pl.ANY)
    embed_shape = (n * embed_weight.shape[0], embed_weight.shape[1])
    up_shape = (up_weight.shape[0], n * up_weight.shape[1])
    out, embed_full, up_full = pl.pallas_call(
        functools.partial(
            attention_kernel, n, fan, group_count, dom_count, groups, cols, width, head_width,
            min(256, total_tokens),
        ),
        out_shape=(
            jax.ShapeDtypeStruct(operands[0].shape, jnp.bfloat16),
            jax.ShapeDtypeStruct(embed_shape, jnp.bfloat16),
            jax.ShapeDtypeStruct(up_shape, jnp.bfloat16),
        ),
        in_specs=[any_spec] * 5,
        out_specs=(any_spec,) * 3,
        scratch_shapes=[pltpu.VMEM((total_tokens, cols), jnp.bfloat16)] * 4
        + [
            pltpu.SemaphoreType.DMA((3, chunks, n)),
            pltpu.SemaphoreType.DMA((3, chunks, n)),
            pltpu.SemaphoreType.DMA((3, chunks)),
            pltpu.SemaphoreType.DMA((chunks, n)),
            pltpu.SemaphoreType.DMA((chunks, n)),
            pltpu.SemaphoreType.DMA((chunks,)),
            pltpu.SemaphoreType.DMA((2,)),
            pltpu.SemaphoreType.DMA((2, 2, n // fan)),
            pltpu.SemaphoreType.DMA((2, 2, n // fan)),
            pltpu.SemaphoreType.DMA((2, fan, n // fan)),
            pltpu.SemaphoreType.DMA((2, fan, n // fan)),
            pltpu.SemaphoreType.DMA((2, group_count, n)),
            pltpu.SemaphoreType.DMA((2, group_count, n)),
            pltpu.SemaphoreType.DMA((2, dom_count, group_count, n)),
            pltpu.SemaphoreType.DMA((2, dom_count, group_count, n)),
        ],
        compiler_params=pltpu.CompilerParams(
            collective_id=0, has_side_effects=True, vmem_limit_bytes=60 * 1024 * 1024
        ),
        name="attention",
    )(*operands, embed_weight, up_weight)
    if not aligned:
        out = out.reshape(n, tokens, per_device, head_width).transpose(0, 2, 1, 3)
        out = out.reshape(particles, HEADS, tokens, head_width).transpose(0, 2, 1, 3)
    return out.reshape(particles * tokens, model_width), embed_full, up_full


def reward_kernel(n, doms, particles, x_ref, o_ref, held, send_sem, recv_sem):
    me = lax.axis_index("dom") * n + lax.axis_index("seq")
    members = n * doms

    def target(step):
        other = lax.rem(me + step, members)
        return other, {"dom": other // n, "seq": other % n}

    def copy(step, slot):
        other, device = target(step)
        return pltpu.make_async_remote_copy(
            src_ref=x_ref,
            dst_ref=held.at[me],
            send_sem=send_sem.at[other],
            recv_sem=recv_sem.at[slot],
            device_id=device,
            device_id_type=MESH,
        )

    barrier = pltpu.get_barrier_semaphore()

    @pl.loop(1, members)
    def _(step):
        _, device = target(step)
        pl.semaphore_signal(barrier, inc=1, device_id=device, device_id_type=MESH)

    pl.semaphore_wait(barrier, members - 1)

    @pl.loop(1, members)
    def _(step):
        copy(step, me).start()

    held[me] = x_ref[...]

    @pl.loop(1, members)
    def _(step):
        copy(step, lax.rem(me + step, members)).wait_recv()

    logits = []
    for dom in range(doms):
        rewards = jnp.sum(held[dom * n : (dom + 1) * n], axis=0)[:1]
        value = held[dom * n][1:2] + potential_scale * rewards
        used = lax.broadcasted_iota(jnp.int32, value.shape, 1) < particles
        logits.append(jnp.where(used, value, -jnp.inf))
    highest = functools.reduce(jnp.maximum, [jnp.max(v, axis=1, keepdims=True) for v in logits])
    total = sum(jnp.sum(jnp.exp(v - highest), axis=1, keepdims=True) for v in logits)
    own = logits[0]
    for dom in range(1, doms):
        own = jnp.where(lax.axis_index("dom") == dom, logits[dom], own)
    o_ref[...] = jnp.broadcast_to(own - (highest + jnp.log(total)), o_ref.shape)

    @pl.loop(1, members)
    def _(step):
        copy(step, me).wait_send()


def weigh(partial_value, prev_logw, n, doms):
    particles = partial_value.shape[0]
    rows = jnp.stack([partial_value, prev_logw])
    padded = jnp.pad(rows, ((0, 8 - 2), (0, LANES - particles)))
    vmem = pl.BlockSpec(memory_space=pltpu.VMEM)
    out = pl.pallas_call(
        functools.partial(reward_kernel, n, doms, particles),
        out_shape=jax.ShapeDtypeStruct((8, LANES), jnp.float32),
        in_specs=[vmem],
        out_specs=vmem,
        scratch_shapes=[
            pltpu.VMEM((n * doms, 8, LANES), jnp.float32),
            pltpu.SemaphoreType.DMA((n * doms,)),
            pltpu.SemaphoreType.DMA((n * doms,)),
        ],
        compiler_params=pltpu.CompilerParams(collective_id=1, has_side_effects=True),
        name="rewards",
    )(padded)
    return out[0, :particles]


def part_sum(block, rows):
    parts = [
        jnp.sum(block[at : at + rows], axis=0, keepdims=True)
        for at in range(0, block.shape[0], rows)
    ]
    return jnp.concatenate(parts, axis=0)


def fused_kernel(
    n, fan, group_count, dom_count, rounds, groups, chunks, head_width, row_block, tile,
    q_ref, k_ref, v_ref, lat_ref, wo_ref, step_in, embed_ref, gain_in, up_ref, head_in,
    prev_in, anc_in, out_ref, logw_ref,
    step_ref, gain_ref, head_ref, prev_ref, anc_ref, picked,
    qb, kb, vb, ob, mixed, embed_full, up_full, wo, lat, velocity, clean, embedded, features,
    cand, score, mine, held,
    send_sem, recv_sem, back_send, back_recv,
    shard_own, line_send, line_recv, fan_send, fan_recv, group_send, group_recv, dom_send, dom_recv,
    load_sem, step_send, step_recv, score_send, score_recv,
):
    me = lax.axis_index("seq")
    my_group = lax.axis_index("groups")
    my_dom = lax.axis_index("dom")
    particles, tokens, model_width = q_ref.shape
    rows = particles * tokens
    share = particles // rounds
    share_rows = share * tokens
    total_tokens = n * tokens
    inputs = ((q_ref, qb), (k_ref, kb), (v_ref, vb))
    members = n * dom_count
    member = my_dom * n + me

    def other_member(step):
        other = lax.rem(member + step, members)
        return other, {"dom": other // n, "seq": other % n}

    small = (
        (wo_ref, wo), (lat_ref, lat), (step_in, step_ref), (gain_in, gain_ref),
        (head_in, head_ref), (prev_in, prev_ref), (anc_in, anc_ref),
    )
    loads = [
        pltpu.make_async_copy(source, target, load_sem.at[at])
        for at, (source, target) in enumerate(small)
    ]

    barrier = pltpu.get_barrier_semaphore()

    @pl.loop(1, members)
    def _(step):
        _, device = other_member(step)
        pl.semaphore_signal(barrier, inc=1, device_id=device, device_id_type=MESH)

    for step in range(1, group_count):
        peer = {"groups": lax.rem(my_group + step, group_count)}
        pl.semaphore_signal(barrier, inc=1, device_id=peer, device_id_type=MESH)
    for load in loads:
        load.start()
    pl.semaphore_wait(barrier, members - 1 + group_count - 1)

    line_start, move_step, group_step, finish_weights, length = shared_weight_exchange(
        n, fan, group_count, dom_count, embed_ref, up_ref, embed_full, up_full,
        shard_own, line_send, line_recv, fan_send, fan_recv, group_send, group_recv,
        dom_send, dom_recv,
    )

    cols = model_width // groups

    def source_of(ref, item, chunk):
        turn, start, width = chunks[chunk]
        offset = pl.multiple_of(groups * start + (item % groups) * width, LANES)
        return ref.at[turn * share + item // groups, :, pl.ds(offset, width)]

    def mixed_of(item, chunk):
        turn, start, width = chunks[chunk]
        offset = pl.multiple_of(groups * start + (item % groups) * width, LANES)
        row = pl.multiple_of((turn * share + item // groups) * tokens, 16)
        return mixed.at[pl.ds(row, tokens), pl.ds(offset, width)]

    def rows_of(ref, owner, chunk):
        turn, start, width = chunks[chunk]
        row = pl.ds(pl.multiple_of(owner * tokens, 16), tokens)
        return ref.at[row, pl.ds(turn * cols + start, width)]

    def outgoing(index, chunk, target):
        source, buffer = inputs[index]
        return pltpu.make_async_remote_copy(
            src_ref=source_of(source, target, chunk),
            dst_ref=rows_of(buffer, me, chunk),
            send_sem=send_sem.at[index, chunk],
            recv_sem=recv_sem.at[index, chunk],
            device_id={"seq": target},
            device_id_type=MESH,
        )

    def own_copy(index, chunk):
        source, buffer = inputs[index]
        return pltpu.make_async_copy(
            source_of(source, me, chunk), rows_of(buffer, me, chunk), recv_sem.at[index, chunk]
        )

    def returned(chunk, target):
        return pltpu.make_async_remote_copy(
            src_ref=rows_of(ob, target, chunk),
            dst_ref=mixed_of(me, chunk),
            send_sem=back_send.at[chunk],
            recv_sem=back_recv.at[chunk],
            device_id={"seq": target},
            device_id_type=MESH,
        )

    def own_return(chunk):
        return pltpu.make_async_copy(
            rows_of(ob, me, chunk), mixed_of(me, chunk), back_recv.at[chunk]
        )

    count = len(chunks)
    blocks = total_tokens // row_block

    def issue(chunk):
        for index in range(3):
            own_copy(index, chunk).start()

            @pl.loop(1, n)
            def _(step, index=index):
                outgoing(index, chunk, lax.rem(me + step, n)).start()

    def attend(chunk):
        turn, start, width = chunks[chunk]
        first = turn * cols + start

        @pl.loop(0, (width // LANES) * blocks)
        def _(step):
            attend_pair(
                qb, kb, vb, ob,
                pl.multiple_of((step % blocks) * row_block, row_block), row_block,
                first + (step // blocks) * LANES, head_width,
            )

    def arrive(chunk):
        turn, start, width = chunks[chunk]
        for index in range(3):
            buffer = inputs[index][1]
            first = turn * cols + start
            take(recv_sem.at[index, chunk], buffer.at[:, first : first + width])

    def give_back(chunk):
        own_return(chunk).start()

        @pl.loop(1, n)
        def _(step):
            returned(chunk, lax.rem(me + step, n)).start()

    def project(chunk):
        if chunk == 0:
            for load in loads:
                load.wait()
        sigma = step_ref[0].astype(jnp.float32) / STEPS
        turn, start, width = chunks[chunk]
        inner = pl.ds(groups * start, groups * width)
        own_rows = pl.ds(turn * share_rows, share_rows)
        final = chunk + 1 == count or chunks[chunk + 1][0] != turn
        take(back_recv.at[chunk], mixed.at[own_rows, inner])

        @pl.loop(0, model_width // tile)
        def _(step):
            columns = pl.ds(pl.multiple_of(step * tile, tile), tile)
            part = jnp.dot(
                mixed[own_rows, inner], wo[inner, columns], preferred_element_type=jnp.float32
            )
            if start > 0:
                part = velocity[own_rows, columns] + part
            if not final:
                velocity[own_rows, columns] = part
                return
            for item in range(share):
                at = slice(item * tokens, (item + 1) * tokens)
                spot = turn * share + item
                flat = lat[spot, :, columns].astype(jnp.float32)
                moved = flat + part[at]
                clean[spot * tokens : (spot + 1) * tokens, columns] = (
                    flat - sigma * moved
                ).astype(jnp.bfloat16)
                cand[my_dom * particles + spot, :, columns] = (flat - moved / STEPS).astype(
                    jnp.bfloat16
                )

    def step_copy(turn, shift, incoming):
        source = lax.rem(my_dom - shift + dom_count, dom_count) if incoming else my_dom
        block = cand.at[pl.ds(source * particles + turn * share, share)]
        return pltpu.make_async_remote_copy(
            src_ref=block,
            dst_ref=block,
            send_sem=step_send.at[turn, shift - 1],
            recv_sem=step_recv.at[turn, shift - 1],
            device_id={"dom": lax.rem(my_dom + shift, dom_count)},
            device_id_type=MESH,
        )

    def embed(turn):
        if turn == 0:
            finish_weights((0,))
        own_rows = pl.ds(turn * share_rows, share_rows)

        @pl.loop(0, embedded.shape[1] // tile)
        def _(step):
            columns = pl.ds(pl.multiple_of(step * tile, tile), tile)
            embedded[own_rows, columns] = jnp.dot(
                clean[own_rows, :], embed_full[:, columns], preferred_element_type=jnp.float32
            )

        for shift in range(1, dom_count):
            step_copy(turn, shift, False).start()

        @pl.loop(turn * share, (turn + 1) * share)
        def _(item):
            item_rows = pl.ds(pl.multiple_of(item * tokens, tokens), tokens)
            block = embedded[item_rows, :]
            centered = block - jnp.mean(block, axis=1, keepdims=True)
            variance = jnp.mean(centered * centered, axis=1, keepdims=True)
            normed = centered * lax.rsqrt(variance + norm_eps) * gain_ref[...]
            features[item_rows, :] = jax.nn.gelu(normed).astype(jnp.bfloat16)

    def judge(turn):
        if turn == 0:
            finish_weights((1,))
        own_rows = pl.ds(turn * share_rows, share_rows)

        @pl.loop(0, up_full.shape[1] // tile)
        def _(step):
            columns = pl.ds(pl.multiple_of(step * tile, tile), tile)
            hidden = jnp.dot(
                features[own_rows, :], up_full[:, columns], preferred_element_type=jnp.float32
            )
            score[turn * share : (turn + 1) * share, :] += (
                part_sum(jax.nn.gelu(hidden), tokens) * head_ref[:, columns]
            )

    actions = {
        "issue": issue, "arrive": arrive, "attend": attend, "return": give_back,
        "move": move_step, "group": group_step, "line": lambda _: line_start(),
        "project": project, "embed": embed, "judge": judge,
    }
    score[...] = jnp.zeros_like(score)
    for name, at in plan(chunks, length):
        actions[name](at)

    partial_value = jnp.sum(score[...], axis=1, keepdims=True) / math.sqrt(total_tokens)
    lane = lax.broadcasted_iota(jnp.int32, (particles, LANES), 1)
    row = lax.broadcasted_iota(jnp.int32, (particles, LANES), 0)
    before = jnp.zeros((particles, LANES), jnp.float32)
    for item in range(particles):
        before = jnp.where(row == item, prev_ref[item], before)
    half = LANES // 2
    own_block = jnp.where(lane < half, partial_value, before)
    mine[0:particles, :] = own_block
    held[member, 0:particles, :] = own_block

    def score_copy(step):
        _, device = other_member(step)
        return pltpu.make_async_remote_copy(
            src_ref=mine,
            dst_ref=held.at[member],
            send_sem=score_send.at[0],
            recv_sem=score_recv.at[0],
            device_id=device,
            device_id_type=MESH,
        )

    @pl.loop(1, members)
    def _(step):
        score_copy(step).start()

    for turn in range(rounds):
        for shift in range(1, dom_count):
            step_copy(turn, shift, True).wait_recv()
    for item in range(particles):
        picked[item] = cand[anc_ref[item]]
    write = pltpu.make_async_copy(picked, out_ref, load_sem.at[0])
    write.start()

    for chunk in range(count):
        sent = qb.at[0 : (n - 1) * tokens, 0 : chunks[chunk][2]]
        for index in range(3):
            take(send_sem.at[index, chunk], sent)
        take(back_send.at[chunk], sent)

    for turn in range(rounds):
        for shift in range(1, dom_count):
            step_copy(turn, shift, False).wait_send()

    take(score_recv.at[0], held.at[0 : members - 1])

    logits = []
    for dom in range(dom_count):
        reward = jnp.sum(held[dom * n : (dom + 1) * n, 0:particles, :], axis=0)[:, 0:1]
        logits.append(held[dom * n, 0:particles, :][:, half : half + 1] + potential_scale * reward)
    highest = functools.reduce(
        jnp.maximum, [jnp.max(value, axis=0, keepdims=True) for value in logits]
    )
    total = sum(jnp.sum(jnp.exp(value - highest), axis=0, keepdims=True) for value in logits)
    own = logits[0]
    for dom in range(1, dom_count):
        own = jnp.where(my_dom == dom, logits[dom], own)
    logw_ref[0:particles, :] = jnp.broadcast_to(
        own - (highest + jnp.log(total)), (particles, LANES)
    )

    take(score_send.at[0], held.at[0 : members - 1])
    write.wait()


def plan(chunks, length):
    count = len(chunks)
    steps = [("line", 0), ("issue", 0), ("move", 1)] + [("issue", at) for at in range(1, count)][:1]
    moved, grouped, projected = 1, 0, 0
    for chunk in range(count):
        steps += [("arrive", chunk), ("attend", chunk), ("return", chunk)]
        if moved < length:
            moved += 1
            steps.append(("move", moved))
        if chunk + 2 < count:
            steps.append(("issue", chunk + 2))
        if chunk + 2 == count:
            steps += [("move", step) for step in range(moved + 1, length + 1)]
            moved = length
            steps += [("group", step) for step in range(length)]
            grouped = length
            while chunks[projected][0] < chunks[-1][0]:
                steps.append(("project", projected))
                projected += 1
    steps += [("move", step) for step in range(moved + 1, length + 1)]
    steps += [("group", step) for step in range(grouped, length)]
    for chunk in range(projected):
        turn = chunks[chunk][0]
        if chunks[chunk + 1][0] > turn:
            steps += [("embed", turn), ("judge", turn)]
    steps += [("project", chunk) for chunk in range(projected, count)]
    return steps + [("embed", chunks[-1][0]), ("judge", chunks[-1][0])]


def chunk_list(rounds, cols):
    chunks = []
    for turn in range(rounds):
        widths = [2 * LANES] * (cols // (2 * LANES)) + [LANES] * (cols % (2 * LANES) // LANES)
        if turn == 0:
            widths.reverse()
        start = 0
        for width in widths:
            chunks.append((turn, start, width))
            start += width
    return tuple(chunks)


def fused(
    latents, queries, keys, values, out_weight, step_index, embed_weight, norm_gain, up_weight,
    head_weight, prev_logw, ancestors,
):
    n = lax.axis_size("seq")
    group_count = lax.axis_size("groups")
    dom_count = lax.axis_size("dom")
    fan = 2 if n % 2 == 0 else 1
    particles, tokens, model_width = queries.shape
    head_width = model_width // HEADS
    rounds = round_count(n, particles, model_width)
    cols = particles * model_width // (n * rounds)
    groups = model_width // cols
    chunks = chunk_list(rounds, cols)
    count = len(chunks)
    rows = particles * tokens
    total_tokens = n * tokens
    members = n * dom_count
    fan_steps, group_steps, dom_steps = (max(x - 1, 1) for x in (fan, group_count, dom_count))
    tile = 512
    embed_shape = (n * embed_weight.shape[0], embed_weight.shape[1])
    up_shape = (up_weight.shape[0], n * up_weight.shape[1])
    hbm = pl.BlockSpec(memory_space=pl.ANY)
    vmem = pl.BlockSpec(memory_space=pltpu.VMEM)
    bf16 = jnp.bfloat16
    dma = pltpu.SemaphoreType.DMA
    resampled, logw = pl.pallas_call(
        functools.partial(
            fused_kernel, n, fan, group_count, dom_count, rounds, groups, chunks, head_width,
            min(256, total_tokens), tile,
        ),
        out_shape=(
            jax.ShapeDtypeStruct(latents.shape, bf16),
            jax.ShapeDtypeStruct((8, LANES), jnp.float32),
        ),
        in_specs=[hbm] * 12,
        out_specs=(hbm, vmem),
        scratch_shapes=[
            pltpu.SMEM(step_index.shape, jnp.int32),
            pltpu.VMEM((1, norm_gain.shape[0]), jnp.float32),
            pltpu.VMEM((1, head_weight.shape[0]), jnp.float32),
            pltpu.SMEM(prev_logw.shape, jnp.float32),
            pltpu.SMEM(ancestors.shape, jnp.int32),
            pltpu.VMEM(latents.shape, bf16),
        ]
        + [pltpu.VMEM((total_tokens, rounds * cols), bf16)] * 4
        + [
            pltpu.VMEM((rows, model_width), bf16),
            pltpu.VMEM(embed_shape, bf16),
            pltpu.VMEM(up_shape, bf16),
            pltpu.VMEM(out_weight.shape, bf16),
            pltpu.VMEM(latents.shape, bf16),
            pltpu.VMEM((rows, model_width), jnp.float32),
            pltpu.VMEM((rows, model_width), bf16),
            pltpu.VMEM((rows, embed_shape[1]), jnp.float32),
            pltpu.VMEM((rows, embed_shape[1]), bf16),
            pltpu.VMEM((dom_count * particles, tokens, model_width), bf16),
            pltpu.VMEM((particles, tile), jnp.float32),
            pltpu.VMEM((8, LANES), jnp.float32),
            pltpu.VMEM((members, 8, LANES), jnp.float32),
            dma((3, count)),
            dma((3, count)),
            dma((count,)),
            dma((count,)),
            dma((2,)),
            dma((2, 2, max(n // fan - 1, 1))),
            dma((2, 2, max(n // fan - 1, 1))),
            dma((2, fan_steps)),
            dma((2, fan_steps, n // fan)),
            dma((2, group_steps)),
            dma((2, group_steps, n)),
            dma((2, dom_steps)),
            dma((2, dom_steps)),
            dma((7,)),
            dma((rounds, dom_steps)),
            dma((rounds, dom_steps)),
            dma((1,)),
            dma((1,)),
        ],
        compiler_params=pltpu.CompilerParams(
            collective_id=0, has_side_effects=True, vmem_limit_bytes=60 * 1024 * 1024
        ),
        name="step",
    )(
        queries, keys, values, latents, out_weight, step_index, embed_weight,
        norm_gain.reshape(1, -1), up_weight, head_weight.reshape(1, -1), prev_logw, ancestors,
    )
    return resampled, logw[:particles, 0]


def round_count(n, particles, model_width):
    for rounds in (2, 1):
        if particles % rounds or (particles * HEADS) % (n * rounds):
            continue
        cols = particles * model_width // (n * rounds)
        if cols % LANES == 0 and model_width % cols == 0:
            return rounds
    return 0


def tiles_evenly(queries, embed_weight, up_weight):
    n = lax.axis_size("seq")
    particles, tokens, model_width = queries.shape
    if 2 * (model_width // HEADS) != LANES or not round_count(n, particles, model_width):
        return False
    return model_width % 512 == 0 and embed_weight.shape[1] % 512 == 0


def on_device(
    latents,
    queries,
    keys,
    values,
    out_weight,
    step_index,
    embed_weight,
    norm_gain,
    up_weight,
    head_weight,
    prev_logw,
    ancestors,
):
    seq_count = lax.axis_size("seq")
    dom_count = lax.axis_size("dom")
    local_particles, local_tokens, model_width = latents.shape
    local_rows = local_particles * local_tokens
    total_tokens = local_tokens * seq_count
    dom = lax.axis_index("dom")

    if tiles_evenly(queries, embed_weight, up_weight):
        return fused(
            latents, queries, keys, values, out_weight, step_index, embed_weight, norm_gain,
            up_weight, head_weight, prev_logw, ancestors,
        )
    attended, embed_full, up_full = attention(
        queries, keys, values, embed_weight, up_weight
    )
    flat = latents.reshape(local_rows, model_width).astype(jnp.float32)
    velocity = flat + jnp.dot(attended, out_weight, preferred_element_type=jnp.float32)
    sigma = step_index[0].astype(jnp.float32) / STEPS
    clean = (flat - sigma * velocity).astype(jnp.bfloat16)
    stepped = (flat - velocity / STEPS).astype(jnp.bfloat16)
    stepped = stepped.reshape(local_particles, local_tokens, model_width)
    candidates = [stepped]
    for shift in range(1, dom_count):
        pairs = [((to + shift) % dom_count, to) for to in range(dom_count)]
        candidates.append(lax.ppermute(stepped, "dom", pairs))
    embedded = jnp.dot(
        clean,
        embed_full,
        preferred_element_type=jnp.float32,
    )
    centre = jnp.mean(embedded, axis=1, keepdims=True)
    centered = embedded - centre
    variance = jnp.mean(centered * centered, axis=1, keepdims=True)
    features = jax.nn.gelu(centered * lax.rsqrt(variance + norm_eps) * norm_gain[None, :]).astype(
        jnp.bfloat16
    )
    scored = (
        jax.nn.gelu(
            jnp.dot(
                features,
                up_full,
                preferred_element_type=jnp.float32,
            )
        )
        * head_weight[None, :]
    )
    partial_value = jnp.sum(jnp.sum(scored, axis=1).reshape(local_particles, local_tokens), axis=1)
    partial_value = partial_value / math.sqrt(total_tokens)
    log_weights = weigh(partial_value, prev_logw, seq_count, dom_count)
    slot = lax.rem(ancestors // local_particles - dom + dom_count, dom_count)
    row = slot * local_particles + lax.rem(ancestors, local_particles)
    resampled = jnp.take(jnp.concatenate(candidates), row, axis=0, mode="clip")
    return (resampled, log_weights)


def solution(mesh):
    in_specs = (
        P(("groups", "dom"), "seq", None),
        P(("groups", "dom"), "seq", None),
        P(("groups", "dom"), "seq", None),
        P(("groups", "dom"), "seq", None),
        P(),
        P("groups"),
        P("seq", None),
        P(),
        P(None, "seq"),
        P(),
        P(("groups", "dom")),
        P(("groups", "dom")),
    )
    out_specs = (P(("groups", "dom"), "seq", None), P(("groups", "dom")))
    return jax.shard_map(
        on_device, mesh=mesh, in_specs=in_specs, out_specs=out_specs, check_vma=False
    )
```

```python
import functools
import math

import jax
import jax.numpy as jnp
from jax import lax
from jax.experimental import pallas as pl
from jax.experimental.pallas import tpu as pltpu
from jax.sharding import PartitionSpec as P

HEADS = 24
STEPS = 28
LANES = 128
MESH = pl.DeviceIdType.MESH

potential_scale = 4.0
norm_eps = 1e-05


def attend_plain(qb, kb, vb, ob, row, rows, column, head_width):
    cols = pl.ds(column, head_width)
    rescale = math.log2(math.e) / math.sqrt(head_width)
    scores = lax.dot_general(
        qb[pl.ds(row, rows), cols],
        kb[:, cols],
        (((1,), (1,)), ((), ())),
        preferred_element_type=jnp.float32,
    )
    highest = jnp.max(scores, axis=-1, keepdims=True)
    expanded = jnp.exp2((scores - highest) * rescale)
    total = jnp.sum(expanded, axis=-1, keepdims=True)
    mixed = jnp.dot(
        expanded.astype(jnp.bfloat16), vb[:, cols], preferred_element_type=jnp.float32
    )
    ob[pl.ds(row, rows), cols] = (mixed / total).astype(ob.dtype)


def attend_pair(qb, kb, vb, ob, row, rows, column, head_width):
    cols = pl.ds(pl.multiple_of(column, LANES), LANES)
    rescale = math.log2(math.e) / math.sqrt(head_width)
    query = qb[pl.ds(row, rows), cols]
    key = kb[:, cols]
    value = vb[:, cols]
    query_low = lax.broadcasted_iota(jnp.int32, query.shape, 1) < head_width
    value_low = lax.broadcasted_iota(jnp.int32, value.shape, 1) < head_width
    results = []
    for head in range(2):
        own_query = query_low if head == 0 else jnp.logical_not(query_low)
        own_value = value_low if head == 0 else jnp.logical_not(value_low)
        scores = lax.dot_general(
            jnp.where(own_query, query, jnp.zeros_like(query)),
            key,
            (((1,), (1,)), ((), ())),
            preferred_element_type=jnp.float32,
        )
        highest = jnp.max(scores, axis=-1, keepdims=True)
        expanded = jnp.exp2((scores - highest) * rescale).astype(jnp.bfloat16)
        results.append(
            jnp.dot(
                expanded,
                jnp.where(own_value, value, jnp.ones_like(value)),
                preferred_element_type=jnp.float32,
            )
        )
    first, second = results
    low = lax.broadcasted_iota(jnp.int32, first.shape, 1) < head_width
    mixed = jnp.where(low, first, second)
    total = pltpu.roll(jnp.where(low, second, first), head_width, 1)
    ob[pl.ds(row, rows), cols] = (mixed / total).astype(ob.dtype)


def piece(ref, item, groups, cols, start, width):
    if groups == 0:
        return ref.at[item]
    offset = pl.multiple_of((item % groups) * cols + start, LANES)
    return ref.at[item // groups, :, pl.ds(offset, width)]


def weight_exchange(
    n, fan, group_count, dom_count, embed_ref, up_ref, embed_full, up_full,
    shard_own, line_send, line_recv, fan_send, fan_recv, group_send, group_recv, dom_send, dom_recv,
):
    me = lax.axis_index("seq")
    my_group = lax.axis_index("groups")
    my_dom = lax.axis_index("dom")
    share_count = group_count * dom_count
    embed_rows, embed_cols = embed_ref.shape
    up_rows, up_cols = up_ref.shape
    embed_part = embed_cols // share_count
    up_part = up_rows // share_count

    def share(which, owner, group, dom, own=False):
        part = group * dom_count + dom
        if which == 0:
            columns = pl.ds(pl.multiple_of(part * embed_part, LANES), embed_part)
            if own:
                return embed_ref.at[:, columns]
            return embed_full.at[
                pl.ds(pl.multiple_of(owner * embed_rows, 16), embed_rows), columns
            ]
        rows = pl.ds(pl.multiple_of(part * up_part, 16), up_part)
        if own:
            return up_ref.at[rows, :]
        return up_full.at[rows, pl.ds(pl.multiple_of(owner * up_cols, LANES), up_cols)]

    def shard_copy(which):
        if which == 0:
            target = embed_full.at[pl.ds(pl.multiple_of(me * embed_rows, 16), embed_rows), :]
            return pltpu.make_async_copy(embed_ref, target, shard_own.at[0])
        target = up_full.at[:, pl.ds(pl.multiple_of(me * up_cols, LANES), up_cols)]
        return pltpu.make_async_copy(up_ref, target, shard_own.at[1])

    place = lax.div(me, fan)
    lane = lax.rem(me, fan)
    length = n // fan
    signs = (1, -1)

    def line_copy(which, direction, step, incoming):
        sign = signs[direction]
        origin = place - sign * (step if incoming else step - 1)
        owner = lax.rem(origin + n, length) * fan + lane
        to = lax.rem(place + sign + n, length) * fan + lane
        return pltpu.make_async_remote_copy(
            src_ref=share(which, owner, my_group, my_dom, own=step == 1 and not incoming),
            dst_ref=share(which, owner, my_group, my_dom),
            send_sem=line_send.at[which, direction, step - 1],
            recv_sem=line_recv.at[which, direction, step - 1],
            device_id={"seq": to},
            device_id_type=MESH,
        )

    def receives(direction, step):
        return place >= step if direction == 0 else place + step < length

    def sends(direction, step):
        if direction == 0:
            return jnp.logical_and(place >= step - 1, place + 1 < length)
        return jnp.logical_and(place + step - 1 < length, place >= 1)

    def fan_copy(which, spot, shift, incoming, own=False):
        to = lax.rem(lane + shift, fan)
        source = lax.rem(lane - shift + fan, fan) if incoming else lane
        owner = spot * fan + source
        return pltpu.make_async_remote_copy(
            src_ref=share(which, owner, my_group, my_dom, own=own),
            dst_ref=share(which, owner, my_group, my_dom),
            send_sem=fan_send.at[which, shift, spot],
            recv_sem=fan_recv.at[which, shift, spot],
            device_id={"seq": place * fan + to},
            device_id_type=MESH,
        )

    def group_copy(which, owner, shift, incoming):
        other = lax.rem(my_group + shift, group_count)
        source = lax.rem(my_group - shift + group_count, group_count) if incoming else my_group
        return pltpu.make_async_remote_copy(
            src_ref=share(which, owner, source, my_dom),
            dst_ref=share(which, owner, source, my_dom),
            send_sem=group_send.at[which, shift, owner],
            recv_sem=group_recv.at[which, shift, owner],
            device_id={"groups": other},
            device_id_type=MESH,
        )

    def dom_copy(which, owner, shift, group_shift, incoming):
        other = lax.rem(my_dom + shift, dom_count)
        source = lax.rem(my_dom - shift + dom_count, dom_count) if incoming else my_dom
        group = lax.rem(my_group - group_shift + group_count, group_count)
        return pltpu.make_async_remote_copy(
            src_ref=share(which, owner, group, source),
            dst_ref=share(which, owner, group, source),
            send_sem=dom_send.at[which, shift, group_shift, owner],
            recv_sem=dom_recv.at[which, shift, group_shift, owner],
            device_id={"dom": other},
            device_id_type=MESH,
        )

    def spread(which, owner):
        for shift in range(1, group_count):
            group_copy(which, owner, shift, False).start()
        for shift in range(1, dom_count):
            dom_copy(which, owner, shift, 0, False).start()

    def each_arrival(step, action):
        for direction in range(2):

            @pl.when(receives(direction, step))
            def _(direction=direction):
                for which in range(2):
                    action(which, direction, place - signs[direction] * step)

    def line_start():
        for which in range(2):
            for direction in range(2):

                @pl.when(sends(direction, 1))
                def _(which=which, direction=direction):
                    line_copy(which, direction, 1, False).start()

            for shift in range(1, fan):
                fan_copy(which, place, shift, False, own=True).start()
            shard_copy(which).start()

    def line_step(step):
        def action(which, direction, spot):
            line_copy(which, direction, step, True).wait_recv()
            if step + 1 < length:

                @pl.when(sends(direction, step + 1))
                def _():
                    line_copy(which, direction, step + 1, False).start()

            for shift in range(1, fan):
                fan_copy(which, spot, shift, False).start()
            spread(which, spot * fan + lane)

        each_arrival(step, action)

    def fan_step(step):
        def action(which, direction, spot):
            for shift in range(1, fan):
                fan_copy(which, spot, shift, True).wait_recv()
                spread(which, spot * fan + lax.rem(lane - shift + fan, fan))

        if step == 0:
            for which in range(2):
                action(which, 0, place)
        else:
            each_arrival(step, action)

    def group_block(which, owner):
        for group_shift in range(1, group_count):
            group_copy(which, owner, group_shift, True).wait_recv()
            for shift in range(1, dom_count):
                dom_copy(which, owner, shift, group_shift, False).start()

    def group_step(step):
        def action(which, direction, spot):
            if step > 0:
                group_block(which, spot * fan + lane)
            for shift in range(1, fan):
                group_block(which, spot * fan + lax.rem(lane - shift + fan, fan))

        if step == 0:
            for which in range(2):
                action(which, 0, place)
        else:
            each_arrival(step, action)

    def move_step(step):
        if 1 <= step < length:
            line_step(step)
        if 0 <= step - 1 < length:
            fan_step(step - 1)


    def finish_weights(parts=(0, 1)):
        for which in parts:
            shard_copy(which).wait()
            for direction in range(2):
                for step in range(1, length):

                    @pl.when(sends(direction, step))
                    def _(which=which, direction=direction, step=step):
                        line_copy(which, direction, step, False).wait_send()

            @pl.loop(0, length)
            def _(spot, which=which):
                for shift in range(1, fan):
                    fan_copy(which, spot, shift, False).wait_send()

            @pl.loop(1, n)
            def _(step, which=which):
                owner = lax.rem(me + step, n)
                for shift in range(1, group_count):
                    group_copy(which, owner, shift, False).wait_send()
                for shift in range(1, dom_count):
                    for group_shift in range(group_count):
                        dom_copy(which, owner, shift, group_shift, True).wait_recv()
                        dom_copy(which, owner, shift, group_shift, False).wait_send()

    return line_start, move_step, group_step, finish_weights, length


def take(semaphore, region):
    pltpu.make_async_copy(region, region, semaphore).wait()


def shared_weight_exchange(
    n, fan, group_count, dom_count, embed_ref, up_ref, embed_full, up_full,
    shard_own, line_send, line_recv, fan_send, fan_recv, group_send, group_recv, dom_send, dom_recv,
):
    me = lax.axis_index("seq")
    my_group = lax.axis_index("groups")
    my_dom = lax.axis_index("dom")
    share_count = group_count * dom_count
    embed_rows, embed_cols = embed_ref.shape
    up_rows, up_cols = up_ref.shape
    embed_part = embed_cols // share_count
    up_part = up_rows // share_count

    def share(which, owner, group, dom, own=False):
        part = group * dom_count + dom
        if which == 0:
            columns = pl.ds(pl.multiple_of(part * embed_part, LANES), embed_part)
            if own:
                return embed_ref.at[:, columns]
            return embed_full.at[
                pl.ds(pl.multiple_of(owner * embed_rows, 16), embed_rows), columns
            ]
        rows = pl.ds(pl.multiple_of(part * up_part, 16), up_part)
        if own:
            return up_ref.at[rows, :]
        return up_full.at[rows, pl.ds(pl.multiple_of(owner * up_cols, LANES), up_cols)]

    def shard_copy(which):
        if which == 0:
            target = embed_full.at[pl.ds(pl.multiple_of(me * embed_rows, 16), embed_rows), :]
            return pltpu.make_async_copy(embed_ref, target, shard_own.at[0])
        target = up_full.at[:, pl.ds(pl.multiple_of(me * up_cols, LANES), up_cols)]
        return pltpu.make_async_copy(up_ref, target, shard_own.at[1])

    place = lax.div(me, fan)
    lane = lax.rem(me, fan)
    length = n // fan
    signs = (1, -1)

    def line_copy(which, direction, step, incoming):
        sign = signs[direction]
        origin = place - sign * (step if incoming else step - 1)
        owner = lax.rem(origin + n, length) * fan + lane
        to = lax.rem(place + sign + n, length) * fan + lane
        return pltpu.make_async_remote_copy(
            src_ref=share(which, owner, my_group, my_dom, own=step == 1 and not incoming),
            dst_ref=share(which, owner, my_group, my_dom),
            send_sem=line_send.at[which, direction, step - 1],
            recv_sem=line_recv.at[which, direction, step - 1],
            device_id={"seq": to},
            device_id_type=MESH,
        )

    def receives(direction, step):
        return place >= step if direction == 0 else place + step < length

    def sends(direction, step):
        if direction == 0:
            return jnp.logical_and(place >= step - 1, place + 1 < length)
        return jnp.logical_and(place + step - 1 < length, place >= 1)

    def fan_copy(which, spot, shift, incoming, own=False):
        to = lax.rem(lane + shift, fan)
        source = lax.rem(lane - shift + fan, fan) if incoming else lane
        owner = spot * fan + source
        return pltpu.make_async_remote_copy(
            src_ref=share(which, owner, my_group, my_dom, own=own),
            dst_ref=share(which, owner, my_group, my_dom),
            send_sem=fan_send.at[which, shift - 1],
            recv_sem=fan_recv.at[which, shift - 1, spot],
            device_id={"seq": place * fan + to},
            device_id_type=MESH,
        )

    def group_copy(which, owner, shift, incoming):
        other = lax.rem(my_group + shift, group_count)
        source = lax.rem(my_group - shift + group_count, group_count) if incoming else my_group
        return pltpu.make_async_remote_copy(
            src_ref=share(which, owner, source, my_dom),
            dst_ref=share(which, owner, source, my_dom),
            send_sem=group_send.at[which, shift - 1],
            recv_sem=group_recv.at[which, shift - 1, owner],
            device_id={"groups": other},
            device_id_type=MESH,
        )

    def dom_copy(which, owner, shift, group_shift, incoming):
        other = lax.rem(my_dom + shift, dom_count)
        source = lax.rem(my_dom - shift + dom_count, dom_count) if incoming else my_dom
        group = lax.rem(my_group - group_shift + group_count, group_count)
        return pltpu.make_async_remote_copy(
            src_ref=share(which, owner, group, source),
            dst_ref=share(which, owner, group, source),
            send_sem=dom_send.at[which, shift - 1],
            recv_sem=dom_recv.at[which, shift - 1],
            device_id={"dom": other},
            device_id_type=MESH,
        )

    def spread(which, owner):
        for shift in range(1, group_count):
            group_copy(which, owner, shift, False).start()
        for shift in range(1, dom_count):
            dom_copy(which, owner, shift, 0, False).start()

    def each_arrival(step, action):
        for direction in range(2):

            @pl.when(receives(direction, step))
            def _(direction=direction):
                for which in range(2):
                    action(which, direction, place - signs[direction] * step)

    def line_start():
        for which in range(2):
            for direction in range(2):

                @pl.when(sends(direction, 1))
                def _(which=which, direction=direction):
                    line_copy(which, direction, 1, False).start()

            for shift in range(1, fan):
                fan_copy(which, place, shift, False, own=True).start()
            shard_copy(which).start()

    def line_step(step):
        def action(which, direction, spot):
            line_copy(which, direction, step, True).wait_recv()
            if step + 1 < length:

                @pl.when(sends(direction, step + 1))
                def _():
                    line_copy(which, direction, step + 1, False).start()

            for shift in range(1, fan):
                fan_copy(which, spot, shift, False).start()
            spread(which, spot * fan + lane)

        each_arrival(step, action)

    def fan_step(step):
        def action(which, direction, spot):
            for shift in range(1, fan):
                fan_copy(which, spot, shift, True).wait_recv()
                spread(which, spot * fan + lax.rem(lane - shift + fan, fan))

        if step == 0:
            for which in range(2):
                action(which, 0, place)
        else:
            each_arrival(step, action)

    def group_block(which, owner):
        for group_shift in range(1, group_count):
            group_copy(which, owner, group_shift, True).wait_recv()
            for shift in range(1, dom_count):
                dom_copy(which, owner, shift, group_shift, False).start()

    def group_step(step):
        def action(which, direction, spot):
            if step > 0:
                group_block(which, spot * fan + lane)
            for shift in range(1, fan):
                group_block(which, spot * fan + lax.rem(lane - shift + fan, fan))

        if step == 0:
            for which in range(2):
                action(which, 0, place)
        else:
            each_arrival(step, action)

    def parts_of(which, amount):
        if which == 0:
            wide = math.gcd(amount, share_count)
            return embed_full.at[0 : amount // wide * embed_rows, 0 : wide * embed_part]
        wide = math.gcd(amount, share_count)
        return up_full.at[0 : wide * up_part, 0 : amount // wide * up_cols]

    def finish_weights(parts=(0, 1)):
        for which in parts:
            shard_copy(which).wait()
            for direction in range(2):
                for step in range(1, length):

                    @pl.when(sends(direction, step))
                    def _(which=which, direction=direction, step=step):
                        line_copy(which, direction, step, False).wait_send()

            for shift in range(1, fan):
                take(fan_send.at[which, shift - 1], parts_of(which, length))
            for shift in range(1, group_count):
                take(group_send.at[which, shift - 1], parts_of(which, n - 1))
            for shift in range(1, dom_count):
                take(dom_recv.at[which, shift - 1], parts_of(which, (n - 1) * group_count))
                take(dom_send.at[which, shift - 1], parts_of(which, (n - 1) * group_count))

    return line_start, line_step, fan_step, group_step, finish_weights, length


def attention_kernel(
    n, fan, group_count, dom_count, groups, cols, width, head_width, row_block,
    q_ref, k_ref, v_ref, embed_ref, up_ref, o_ref, embed_full, up_full,
    qb, kb, vb, ob, send_sem, recv_sem, own_sem, back_send, back_recv, back_own,
    shard_own, line_send, line_recv, fan_send, fan_recv, group_send, group_recv, dom_send, dom_recv,
):
    me = lax.axis_index("seq")
    my_group = lax.axis_index("groups")
    my_dom = lax.axis_index("dom")
    tokens = q_ref.shape[1]
    total_tokens = n * tokens
    chunks = cols // width
    inputs = ((q_ref, qb), (k_ref, kb), (v_ref, vb))

    barrier = pltpu.get_barrier_semaphore()

    @pl.loop(1, n)
    def _(step):
        pl.semaphore_signal(
            barrier, inc=1, device_id={"seq": lax.rem(me + step, n)}, device_id_type=MESH
        )

    for step in range(1, group_count):
        peer = {"groups": lax.rem(my_group + step, group_count)}
        pl.semaphore_signal(barrier, inc=1, device_id=peer, device_id_type=MESH)
    for step in range(1, dom_count):
        peer = {"dom": lax.rem(my_dom + step, dom_count)}
        pl.semaphore_signal(barrier, inc=1, device_id=peer, device_id_type=MESH)
    pl.semaphore_wait(barrier, n - 1 + group_count - 1 + dom_count - 1)

    line_start, move_step, group_step, finish_weights, length = weight_exchange(
        n, fan, group_count, dom_count, embed_ref, up_ref, embed_full, up_full,
        shard_own, line_send, line_recv, fan_send, fan_recv, group_send, group_recv,
        dom_send, dom_recv,
    )

    def rows_of(ref, owner, chunk):
        row = pl.ds(pl.multiple_of(owner * tokens, 16), tokens)
        return ref.at[row, pl.ds(chunk * width, width)]

    def outgoing(index, chunk, target, slot):
        source, buffer = inputs[index]
        return pltpu.make_async_remote_copy(
            src_ref=piece(source, target, groups, cols, chunk * width, width),
            dst_ref=rows_of(buffer, me, chunk),
            send_sem=send_sem.at[index, chunk, target],
            recv_sem=recv_sem.at[index, chunk, slot],
            device_id={"seq": target},
            device_id_type=MESH,
        )

    def own_copy(index, chunk):
        source, buffer = inputs[index]
        return pltpu.make_async_copy(
            piece(source, me, groups, cols, chunk * width, width),
            rows_of(buffer, me, chunk),
            own_sem.at[index, chunk],
        )

    def returned(chunk, target, slot):
        return pltpu.make_async_remote_copy(
            src_ref=rows_of(ob, target, chunk),
            dst_ref=piece(o_ref, me, groups, cols, chunk * width, width),
            send_sem=back_send.at[chunk, target],
            recv_sem=back_recv.at[chunk, slot],
            device_id={"seq": target},
            device_id_type=MESH,
        )

    def own_return(chunk):
        return pltpu.make_async_copy(
            rows_of(ob, me, chunk),
            piece(o_ref, me, groups, cols, chunk * width, width),
            back_own.at[chunk],
        )

    weight_steps = length + 2

    def weight_step(step):
        move_step(step)
        if 0 <= step - 2 < length:
            group_step(step - 2)

    ready = 1
    for chunk in range(chunks):
        if chunk == 0:
            line_start()
        elif ready < weight_steps:
            weight_step(ready)
            ready += 1
        for index in range(3):
            own_copy(index, chunk).start()

            @pl.loop(1, n)
            def _(step, index=index, chunk=chunk):
                outgoing(index, chunk, lax.rem(me + step, n), me).start()

    paired = 2 * head_width == LANES and width % LANES == 0
    unit = LANES if paired else head_width
    blocks = total_tokens // row_block

    for chunk in range(chunks):
        for index in range(3):
            own_copy(index, chunk).wait()

            @pl.loop(1, n)
            def _(step, index=index, chunk=chunk):
                other = lax.rem(me + step, n)
                outgoing(index, chunk, other, other).wait_recv()

        if paired:

            @pl.loop(0, (width // unit) * blocks)
            def _(step, chunk=chunk):
                attend_pair(
                    qb, kb, vb, ob,
                    pl.multiple_of((step % blocks) * row_block, row_block), row_block,
                    chunk * width + (step // blocks) * unit, head_width,
                )
        else:
            for head in range(width // unit):

                @pl.loop(0, blocks)
                def _(step, head=head, chunk=chunk):
                    attend_plain(
                        qb, kb, vb, ob,
                        pl.multiple_of(step * row_block, row_block), row_block,
                        chunk * width + head * unit, head_width,
                    )

        own_return(chunk).start()

        @pl.loop(1, n)
        def _(step, chunk=chunk):
            returned(chunk, lax.rem(me + step, n), me).start()

        if ready < weight_steps and chunk < chunks - 1:
            weight_step(ready)
            ready += 1

    for step in range(ready, weight_steps):
        weight_step(step)
    finish_weights()

    for chunk in range(chunks):
        own_return(chunk).wait()
        for index in range(3):

            @pl.loop(1, n)
            def _(step, index=index, chunk=chunk):
                outgoing(index, chunk, lax.rem(me + step, n), me).wait_send()

        @pl.loop(1, n)
        def _(step, chunk=chunk):
            other = lax.rem(me + step, n)
            returned(chunk, other, other).wait_recv()
            returned(chunk, other, me).wait_send()


def attention(queries, keys, values, embed_weight, up_weight):
    n = lax.axis_size("seq")
    group_count = lax.axis_size("groups")
    dom_count = lax.axis_size("dom")
    fan = 2 if n % 2 == 0 else 1
    particles, tokens, model_width = queries.shape
    head_width = model_width // HEADS
    per_device = particles * HEADS // n
    cols = per_device * head_width
    aligned = model_width % cols == 0 and cols % LANES == 0
    groups = model_width // cols if aligned else 0
    width = 2 * LANES if aligned and cols % (2 * LANES) == 0 else cols
    chunks = cols // width
    total_tokens = n * tokens

    def to_items(array):
        if aligned:
            return array
        split = array.reshape(particles, tokens, HEADS, head_width).transpose(0, 2, 1, 3)
        split = split.reshape(n, per_device, tokens, head_width).transpose(0, 2, 1, 3)
        return split.reshape(n, tokens, cols)

    operands = tuple(to_items(a) for a in (queries, keys, values))
    any_spec = pl.BlockSpec(memory_space=pl.ANY)
    embed_shape = (n * embed_weight.shape[0], embed_weight.shape[1])
    up_shape = (up_weight.shape[0], n * up_weight.shape[1])
    out, embed_full, up_full = pl.pallas_call(
        functools.partial(
            attention_kernel, n, fan, group_count, dom_count, groups, cols, width, head_width,
            min(256, total_tokens),
        ),
        out_shape=(
            jax.ShapeDtypeStruct(operands[0].shape, jnp.bfloat16),
            jax.ShapeDtypeStruct(embed_shape, jnp.bfloat16),
            jax.ShapeDtypeStruct(up_shape, jnp.bfloat16),
        ),
        in_specs=[any_spec] * 5,
        out_specs=(any_spec,) * 3,
        scratch_shapes=[pltpu.VMEM((total_tokens, cols), jnp.bfloat16)] * 4
        + [
            pltpu.SemaphoreType.DMA((3, chunks, n)),
            pltpu.SemaphoreType.DMA((3, chunks, n)),
            pltpu.SemaphoreType.DMA((3, chunks)),
            pltpu.SemaphoreType.DMA((chunks, n)),
            pltpu.SemaphoreType.DMA((chunks, n)),
            pltpu.SemaphoreType.DMA((chunks,)),
            pltpu.SemaphoreType.DMA((2,)),
            pltpu.SemaphoreType.DMA((2, 2, n // fan)),
            pltpu.SemaphoreType.DMA((2, 2, n // fan)),
            pltpu.SemaphoreType.DMA((2, fan, n // fan)),
            pltpu.SemaphoreType.DMA((2, fan, n // fan)),
            pltpu.SemaphoreType.DMA((2, group_count, n)),
            pltpu.SemaphoreType.DMA((2, group_count, n)),
            pltpu.SemaphoreType.DMA((2, dom_count, group_count, n)),
            pltpu.SemaphoreType.DMA((2, dom_count, group_count, n)),
        ],
        compiler_params=pltpu.CompilerParams(
            collective_id=0, has_side_effects=True, vmem_limit_bytes=60 * 1024 * 1024
        ),
        name="attention",
    )(*operands, embed_weight, up_weight)
    if not aligned:
        out = out.reshape(n, tokens, per_device, head_width).transpose(0, 2, 1, 3)
        out = out.reshape(particles, HEADS, tokens, head_width).transpose(0, 2, 1, 3)
    return out.reshape(particles * tokens, model_width), embed_full, up_full


def reward_kernel(n, doms, particles, x_ref, o_ref, held, send_sem, recv_sem):
    me = lax.axis_index("dom") * n + lax.axis_index("seq")
    members = n * doms

    def target(step):
        other = lax.rem(me + step, members)
        return other, {"dom": other // n, "seq": other % n}

    def copy(step, slot):
        other, device = target(step)
        return pltpu.make_async_remote_copy(
            src_ref=x_ref,
            dst_ref=held.at[me],
            send_sem=send_sem.at[other],
            recv_sem=recv_sem.at[slot],
            device_id=device,
            device_id_type=MESH,
        )

    barrier = pltpu.get_barrier_semaphore()

    @pl.loop(1, members)
    def _(step):
        _, device = target(step)
        pl.semaphore_signal(barrier, inc=1, device_id=device, device_id_type=MESH)

    pl.semaphore_wait(barrier, members - 1)

    @pl.loop(1, members)
    def _(step):
        copy(step, me).start()

    held[me] = x_ref[...]

    @pl.loop(1, members)
    def _(step):
        copy(step, lax.rem(me + step, members)).wait_recv()

    logits = []
    for dom in range(doms):
        rewards = jnp.sum(held[dom * n : (dom + 1) * n], axis=0)[:1]
        value = held[dom * n][1:2] + potential_scale * rewards
        used = lax.broadcasted_iota(jnp.int32, value.shape, 1) < particles
        logits.append(jnp.where(used, value, -jnp.inf))
    highest = functools.reduce(jnp.maximum, [jnp.max(v, axis=1, keepdims=True) for v in logits])
    total = sum(jnp.sum(jnp.exp(v - highest), axis=1, keepdims=True) for v in logits)
    own = logits[0]
    for dom in range(1, doms):
        own = jnp.where(lax.axis_index("dom") == dom, logits[dom], own)
    o_ref[...] = jnp.broadcast_to(own - (highest + jnp.log(total)), o_ref.shape)

    @pl.loop(1, members)
    def _(step):
        copy(step, me).wait_send()


def weigh(partial_value, prev_logw, n, doms):
    particles = partial_value.shape[0]
    rows = jnp.stack([partial_value, prev_logw])
    padded = jnp.pad(rows, ((0, 8 - 2), (0, LANES - particles)))
    vmem = pl.BlockSpec(memory_space=pltpu.VMEM)
    out = pl.pallas_call(
        functools.partial(reward_kernel, n, doms, particles),
        out_shape=jax.ShapeDtypeStruct((8, LANES), jnp.float32),
        in_specs=[vmem],
        out_specs=vmem,
        scratch_shapes=[
            pltpu.VMEM((n * doms, 8, LANES), jnp.float32),
            pltpu.SemaphoreType.DMA((n * doms,)),
            pltpu.SemaphoreType.DMA((n * doms,)),
        ],
        compiler_params=pltpu.CompilerParams(collective_id=1, has_side_effects=True),
        name="rewards",
    )(padded)
    return out[0, :particles]


def part_sum(block, rows):
    parts = [
        jnp.sum(block[at : at + rows], axis=0, keepdims=True)
        for at in range(0, block.shape[0], rows)
    ]
    return jnp.concatenate(parts, axis=0)


def fused_kernel(
    n, fan, group_count, dom_count, rounds, groups, chunks, head_width, row_block, tile,
    q_ref, k_ref, v_ref, lat_ref, wo_ref, step_in, embed_ref, gain_in, up_ref, head_in,
    prev_in, anc_in, out_ref, logw_ref,
    step_ref, gain_ref, head_ref, prev_ref, anc_ref, picked,
    qb, kb, vb, ob, mixed, embed_full, up_full, wo, lat, velocity, clean, embedded, features,
    cand, score, mine, held,
    send_sem, recv_sem, back_send, back_recv,
    shard_own, line_send, line_recv, fan_send, fan_recv, group_send, group_recv, dom_send, dom_recv,
    load_sem, step_send, step_recv, score_send, score_recv,
):
    me = lax.axis_index("seq")
    my_group = lax.axis_index("groups")
    my_dom = lax.axis_index("dom")
    particles, tokens, model_width = q_ref.shape
    rows = particles * tokens
    share = particles // rounds
    share_rows = share * tokens
    total_tokens = n * tokens
    inputs = ((q_ref, qb), (k_ref, kb), (v_ref, vb))
    members = n * dom_count
    member = my_dom * n + me

    def other_member(step):
        other = lax.rem(member + step, members)
        return other, {"dom": other // n, "seq": other % n}

    small = (
        (wo_ref, wo), (lat_ref, lat), (step_in, step_ref), (gain_in, gain_ref),
        (head_in, head_ref), (prev_in, prev_ref), (anc_in, anc_ref),
    )
    loads = [
        pltpu.make_async_copy(source, target, load_sem.at[at])
        for at, (source, target) in enumerate(small)
    ]

    barrier = pltpu.get_barrier_semaphore()

    @pl.loop(1, members)
    def _(step):
        _, device = other_member(step)
        pl.semaphore_signal(barrier, inc=1, device_id=device, device_id_type=MESH)

    for step in range(1, group_count):
        peer = {"groups": lax.rem(my_group + step, group_count)}
        pl.semaphore_signal(barrier, inc=1, device_id=peer, device_id_type=MESH)
    for load in loads:
        load.start()
    pl.semaphore_wait(barrier, members - 1 + group_count - 1)

    line_start, line_step, fan_step, group_step, finish_weights, length = shared_weight_exchange(
        n, fan, group_count, dom_count, embed_ref, up_ref, embed_full, up_full,
        shard_own, line_send, line_recv, fan_send, fan_recv, group_send, group_recv,
        dom_send, dom_recv,
    )

    cols = model_width // groups

    def source_of(ref, item, chunk):
        turn, start, width = chunks[chunk]
        offset = pl.multiple_of(groups * start + (item % groups) * width, LANES)
        return ref.at[turn * share + item // groups, :, pl.ds(offset, width)]

    def mixed_of(item, chunk):
        turn, start, width = chunks[chunk]
        offset = pl.multiple_of(groups * start + (item % groups) * width, LANES)
        row = pl.multiple_of((turn * share + item // groups) * tokens, 16)
        return mixed.at[pl.ds(row, tokens), pl.ds(offset, width)]

    def rows_of(ref, owner, chunk):
        turn, start, width = chunks[chunk]
        row = pl.ds(pl.multiple_of(owner * tokens, 16), tokens)
        return ref.at[row, pl.ds(turn * cols + start, width)]

    def outgoing(index, chunk, target):
        source, buffer = inputs[index]
        return pltpu.make_async_remote_copy(
            src_ref=source_of(source, target, chunk),
            dst_ref=rows_of(buffer, me, chunk),
            send_sem=send_sem.at[index, chunk],
            recv_sem=recv_sem.at[index, chunk],
            device_id={"seq": target},
            device_id_type=MESH,
        )

    def own_copy(index, chunk):
        source, buffer = inputs[index]
        return pltpu.make_async_copy(
            source_of(source, me, chunk), rows_of(buffer, me, chunk), recv_sem.at[index, chunk]
        )

    def returned(chunk, target):
        return pltpu.make_async_remote_copy(
            src_ref=rows_of(ob, target, chunk),
            dst_ref=mixed_of(me, chunk),
            send_sem=back_send.at[chunk],
            recv_sem=back_recv.at[chunk],
            device_id={"seq": target},
            device_id_type=MESH,
        )

    def own_return(chunk):
        return pltpu.make_async_copy(
            rows_of(ob, me, chunk), mixed_of(me, chunk), back_recv.at[chunk]
        )

    count = len(chunks)
    blocks = total_tokens // row_block

    def issue(chunk):
        for index in range(3):
            own_copy(index, chunk).start()

            @pl.loop(1, n)
            def _(step, index=index):
                outgoing(index, chunk, lax.rem(me + step, n)).start()

    def attend(chunk):
        turn, start, width = chunks[chunk]
        first = turn * cols + start

        @pl.loop(0, (width // LANES) * blocks)
        def _(step):
            attend_pair(
                qb, kb, vb, ob,
                pl.multiple_of((step % blocks) * row_block, row_block), row_block,
                first + (step // blocks) * LANES, head_width,
            )

    def arrive(chunk):
        turn, start, width = chunks[chunk]
        for index in range(3):
            buffer = inputs[index][1]
            first = turn * cols + start
            take(recv_sem.at[index, chunk], buffer.at[:, first : first + width])

    def give_back(chunk):
        own_return(chunk).start()

        @pl.loop(1, n)
        def _(step):
            returned(chunk, lax.rem(me + step, n)).start()

    def project(chunk):
        if chunk == 0:
            for load in loads:
                load.wait()
        sigma = step_ref[0].astype(jnp.float32) / STEPS
        turn, start, width = chunks[chunk]
        inner = pl.ds(groups * start, groups * width)
        own_rows = pl.ds(turn * share_rows, share_rows)
        final = chunk + 1 == count or chunks[chunk + 1][0] != turn
        take(back_recv.at[chunk], mixed.at[own_rows, inner])

        @pl.loop(0, model_width // tile, unroll=model_width // tile)
        def _(step):
            columns = pl.ds(pl.multiple_of(step * tile, tile), tile)
            part = jnp.dot(
                mixed[own_rows, inner], wo[inner, columns], preferred_element_type=jnp.float32
            )
            if start > 0:
                part = velocity[own_rows, columns] + part
            if not final:
                velocity[own_rows, columns] = part
                return
            for item in range(share):
                at = slice(item * tokens, (item + 1) * tokens)
                spot = turn * share + item
                flat = lat[spot, :, columns].astype(jnp.float32)
                moved = flat + part[at]
                clean[spot * tokens : (spot + 1) * tokens, columns] = (
                    flat - sigma * moved
                ).astype(jnp.bfloat16)
                cand[my_dom * particles + spot, :, columns] = (flat - moved / STEPS).astype(
                    jnp.bfloat16
                )

    def step_copy(turn, shift, incoming):
        source = lax.rem(my_dom - shift + dom_count, dom_count) if incoming else my_dom
        block = cand.at[pl.ds(source * particles + turn * share, share)]
        return pltpu.make_async_remote_copy(
            src_ref=block,
            dst_ref=block,
            send_sem=step_send.at[turn, shift - 1],
            recv_sem=step_recv.at[turn, shift - 1],
            device_id={"dom": lax.rem(my_dom + shift, dom_count)},
            device_id_type=MESH,
        )

    def embed(turn):
        if turn == 0:
            finish_weights((0,))
        own_rows = pl.ds(turn * share_rows, share_rows)

        @pl.loop(0, embedded.shape[1] // tile, unroll=embedded.shape[1] // tile)
        def _(step):
            columns = pl.ds(pl.multiple_of(step * tile, tile), tile)
            embedded[own_rows, columns] = jnp.dot(
                clean[own_rows, :], embed_full[:, columns], preferred_element_type=jnp.float32
            )

        for shift in range(1, dom_count):
            step_copy(turn, shift, False).start()

        @pl.loop(turn * share, (turn + 1) * share)
        def _(item):
            item_rows = pl.ds(pl.multiple_of(item * tokens, tokens), tokens)
            block = embedded[item_rows, :]
            centered = block - jnp.mean(block, axis=1, keepdims=True)
            variance = jnp.mean(centered * centered, axis=1, keepdims=True)
            normed = centered * lax.rsqrt(variance + norm_eps) * gain_ref[...]
            features[item_rows, :] = jax.nn.gelu(normed).astype(jnp.bfloat16)

    def judge(turn):
        if turn == 0:
            finish_weights((1,))
        own_rows = pl.ds(turn * share_rows, share_rows)

        @pl.loop(0, up_full.shape[1] // tile, unroll=min(8, up_full.shape[1] // tile))
        def _(step):
            columns = pl.ds(pl.multiple_of(step * tile, tile), tile)
            hidden = jnp.dot(
                features[own_rows, :], up_full[:, columns], preferred_element_type=jnp.float32
            )
            score[turn * share : (turn + 1) * share, :] += (
                part_sum(jax.nn.gelu(hidden), tokens) * head_ref[:, columns]
            )

    actions = {
        "issue": issue, "arrive": arrive, "attend": attend, "return": give_back,
        "line": line_step, "fan": fan_step, "group": group_step, "start": lambda _: line_start(),
        "project": project, "embed": embed, "judge": judge,
    }
    score[...] = jnp.zeros_like(score)
    for name, at in plan(chunks, length):
        actions[name](at)

    partial_value = jnp.sum(score[...], axis=1, keepdims=True) / math.sqrt(total_tokens)
    lane = lax.broadcasted_iota(jnp.int32, (particles, LANES), 1)
    row = lax.broadcasted_iota(jnp.int32, (particles, LANES), 0)
    before = jnp.zeros((particles, LANES), jnp.float32)
    for item in range(particles):
        before = jnp.where(row == item, prev_ref[item], before)
    half = LANES // 2
    own_block = jnp.where(lane < half, partial_value, before)
    mine[0:particles, :] = own_block
    held[member, 0:particles, :] = own_block

    def score_copy(step):
        _, device = other_member(step)
        return pltpu.make_async_remote_copy(
            src_ref=mine,
            dst_ref=held.at[member],
            send_sem=score_send.at[0],
            recv_sem=score_recv.at[0],
            device_id=device,
            device_id_type=MESH,
        )

    @pl.loop(1, members)
    def _(step):
        score_copy(step).start()

    for turn in range(rounds):
        for shift in range(1, dom_count):
            step_copy(turn, shift, True).wait_recv()
    for item in range(particles):
        picked[item] = cand[anc_ref[item]]
    write = pltpu.make_async_copy(picked, out_ref, load_sem.at[0])
    write.start()

    for chunk in range(count):
        sent = qb.at[0 : (n - 1) * tokens, 0 : chunks[chunk][2]]
        for index in range(3):
            take(send_sem.at[index, chunk], sent)
        take(back_send.at[chunk], sent)

    for turn in range(rounds):
        for shift in range(1, dom_count):
            step_copy(turn, shift, False).wait_send()

    take(score_recv.at[0], held.at[0 : members - 1])

    logits = []
    for dom in range(dom_count):
        reward = jnp.sum(held[dom * n : (dom + 1) * n, 0:particles, :], axis=0)[:, 0:1]
        logits.append(held[dom * n, 0:particles, :][:, half : half + 1] + potential_scale * reward)
    highest = functools.reduce(
        jnp.maximum, [jnp.max(value, axis=0, keepdims=True) for value in logits]
    )
    total = sum(jnp.sum(jnp.exp(value - highest), axis=0, keepdims=True) for value in logits)
    own = logits[0]
    for dom in range(1, dom_count):
        own = jnp.where(my_dom == dom, logits[dom], own)
    logw_ref[0:particles, :] = jnp.broadcast_to(
        own - (highest + jnp.log(total)), (particles, LANES)
    )

    take(score_send.at[0], held.at[0 : members - 1])
    write.wait()


def plan(chunks, length):
    count = len(chunks)
    last = chunks[-1][0]
    early = [chunk for chunk in range(count) if chunks[chunk][0] < last]
    late = [chunk for chunk in range(count) if chunks[chunk][0] == last]
    lines = list(range(2, length))
    fans = list(range(1, length))
    steps = [("start", 0), ("issue", 0), ("line", 1), ("fan", 0)]
    if length == 1:
        steps = [("start", 0), ("issue", 0), ("fan", 0)]
    steps += [("issue", chunk) for chunk in range(1, min(2, count))]
    for chunk in range(count):
        if chunk == count - 1:
            steps += [("line", step) for step in lines] + [("fan", step) for step in fans]
            steps += [("group", step) for step in range(length)]
            steps += [("project", part) for part in early]
        elif chunk == 0:
            steps += [("line", step) for step in lines[:1]] + [("fan", step) for step in fans[:1]]
            lines, fans = lines[1:], fans[1:]
        steps += [("arrive", chunk), ("attend", chunk), ("return", chunk)]
        if chunk + 2 < count:
            steps.append(("issue", chunk + 2))
        if chunk < count - 1:
            steps += [("line", step) for step in lines[:1]] + [("fan", step) for step in fans[:1]]
            lines, fans = lines[1:], fans[1:]
    for turn in range(last):
        steps += [("embed", turn), ("judge", turn)]
    return steps + [("project", part) for part in late] + [("embed", last), ("judge", last)]


def chunk_list(rounds, cols):
    chunks = []
    for turn in range(rounds):
        widths = [2 * LANES] * (cols // (2 * LANES)) + [LANES] * (cols % (2 * LANES) // LANES)
        if turn == 0:
            widths.reverse()
        start = 0
        for width in widths:
            chunks.append((turn, start, width))
            start += width
    return tuple(chunks)


def fused(
    latents, queries, keys, values, out_weight, step_index, embed_weight, norm_gain, up_weight,
    head_weight, prev_logw, ancestors,
):
    n = lax.axis_size("seq")
    group_count = lax.axis_size("groups")
    dom_count = lax.axis_size("dom")
    fan = 2 if n % 2 == 0 else 1
    particles, tokens, model_width = queries.shape
    head_width = model_width // HEADS
    rounds = round_count(n, particles, model_width)
    cols = particles * model_width // (n * rounds)
    groups = model_width // cols
    chunks = chunk_list(rounds, cols)
    count = len(chunks)
    rows = particles * tokens
    total_tokens = n * tokens
    members = n * dom_count
    fan_steps, group_steps, dom_steps = (max(x - 1, 1) for x in (fan, group_count, dom_count))
    tile = 512
    embed_shape = (n * embed_weight.shape[0], embed_weight.shape[1])
    up_shape = (up_weight.shape[0], n * up_weight.shape[1])
    hbm = pl.BlockSpec(memory_space=pl.ANY)
    vmem = pl.BlockSpec(memory_space=pltpu.VMEM)
    bf16 = jnp.bfloat16
    dma = pltpu.SemaphoreType.DMA
    resampled, logw = pl.pallas_call(
        functools.partial(
            fused_kernel, n, fan, group_count, dom_count, rounds, groups, chunks, head_width,
            min(256, total_tokens), tile,
        ),
        out_shape=(
            jax.ShapeDtypeStruct(latents.shape, bf16),
            jax.ShapeDtypeStruct((8, LANES), jnp.float32),
        ),
        in_specs=[hbm] * 12,
        out_specs=(hbm, vmem),
        scratch_shapes=[
            pltpu.SMEM(step_index.shape, jnp.int32),
            pltpu.VMEM((1, norm_gain.shape[0]), jnp.float32),
            pltpu.VMEM((1, head_weight.shape[0]), jnp.float32),
            pltpu.SMEM(prev_logw.shape, jnp.float32),
            pltpu.SMEM(ancestors.shape, jnp.int32),
            pltpu.VMEM(latents.shape, bf16),
        ]
        + [pltpu.VMEM((total_tokens, rounds * cols), bf16)] * 4
        + [
            pltpu.VMEM((rows, model_width), bf16),
            pltpu.VMEM(embed_shape, bf16),
            pltpu.VMEM(up_shape, bf16),
            pltpu.VMEM(out_weight.shape, bf16),
            pltpu.VMEM(latents.shape, bf16),
            pltpu.VMEM((rows, model_width), jnp.float32),
            pltpu.VMEM((rows, model_width), bf16),
            pltpu.VMEM((rows, embed_shape[1]), jnp.float32),
            pltpu.VMEM((rows, embed_shape[1]), bf16),
            pltpu.VMEM((dom_count * particles, tokens, model_width), bf16),
            pltpu.VMEM((particles, tile), jnp.float32),
            pltpu.VMEM((8, LANES), jnp.float32),
            pltpu.VMEM((members, 8, LANES), jnp.float32),
            dma((3, count)),
            dma((3, count)),
            dma((count,)),
            dma((count,)),
            dma((2,)),
            dma((2, 2, max(n // fan - 1, 1))),
            dma((2, 2, max(n // fan - 1, 1))),
            dma((2, fan_steps)),
            dma((2, fan_steps, n // fan)),
            dma((2, group_steps)),
            dma((2, group_steps, n)),
            dma((2, dom_steps)),
            dma((2, dom_steps)),
            dma((7,)),
            dma((rounds, dom_steps)),
            dma((rounds, dom_steps)),
            dma((1,)),
            dma((1,)),
        ],
        compiler_params=pltpu.CompilerParams(
            collective_id=0, has_side_effects=True, vmem_limit_bytes=60 * 1024 * 1024
        ),
        name="step",
    )(
        queries, keys, values, latents, out_weight, step_index, embed_weight,
        norm_gain.reshape(1, -1), up_weight, head_weight.reshape(1, -1), prev_logw, ancestors,
    )
    return resampled, logw[:particles, 0]


def round_count(n, particles, model_width):
    for rounds in (2, 1):
        if particles % rounds or (particles * HEADS) % (n * rounds):
            continue
        cols = particles * model_width // (n * rounds)
        if cols % LANES == 0 and model_width % cols == 0:
            return rounds
    return 0


def tiles_evenly(queries, embed_weight, up_weight):
    n = lax.axis_size("seq")
    particles, tokens, model_width = queries.shape
    if 2 * (model_width // HEADS) != LANES or not round_count(n, particles, model_width):
        return False
    return model_width % 512 == 0 and embed_weight.shape[1] % 512 == 0


def on_device(
    latents,
    queries,
    keys,
    values,
    out_weight,
    step_index,
    embed_weight,
    norm_gain,
    up_weight,
    head_weight,
    prev_logw,
    ancestors,
):
    seq_count = lax.axis_size("seq")
    dom_count = lax.axis_size("dom")
    local_particles, local_tokens, model_width = latents.shape
    local_rows = local_particles * local_tokens
    total_tokens = local_tokens * seq_count
    dom = lax.axis_index("dom")

    if tiles_evenly(queries, embed_weight, up_weight):
        return fused(
            latents, queries, keys, values, out_weight, step_index, embed_weight, norm_gain,
            up_weight, head_weight, prev_logw, ancestors,
        )
    attended, embed_full, up_full = attention(
        queries, keys, values, embed_weight, up_weight
    )
    flat = latents.reshape(local_rows, model_width).astype(jnp.float32)
    velocity = flat + jnp.dot(attended, out_weight, preferred_element_type=jnp.float32)
    sigma = step_index[0].astype(jnp.float32) / STEPS
    clean = (flat - sigma * velocity).astype(jnp.bfloat16)
    stepped = (flat - velocity / STEPS).astype(jnp.bfloat16)
    stepped = stepped.reshape(local_particles, local_tokens, model_width)
    candidates = [stepped]
    for shift in range(1, dom_count):
        pairs = [((to + shift) % dom_count, to) for to in range(dom_count)]
        candidates.append(lax.ppermute(stepped, "dom", pairs))
    embedded = jnp.dot(
        clean,
        embed_full,
        preferred_element_type=jnp.float32,
    )
    centre = jnp.mean(embedded, axis=1, keepdims=True)
    centered = embedded - centre
    variance = jnp.mean(centered * centered, axis=1, keepdims=True)
    features = jax.nn.gelu(centered * lax.rsqrt(variance + norm_eps) * norm_gain[None, :]).astype(
        jnp.bfloat16
    )
    scored = (
        jax.nn.gelu(
            jnp.dot(
                features,
                up_full,
                preferred_element_type=jnp.float32,
            )
        )
        * head_weight[None, :]
    )
    partial_value = jnp.sum(jnp.sum(scored, axis=1).reshape(local_particles, local_tokens), axis=1)
    partial_value = partial_value / math.sqrt(total_tokens)
    log_weights = weigh(partial_value, prev_logw, seq_count, dom_count)
    slot = lax.rem(ancestors // local_particles - dom + dom_count, dom_count)
    row = slot * local_particles + lax.rem(ancestors, local_particles)
    resampled = jnp.take(jnp.concatenate(candidates), row, axis=0, mode="clip")
    return (resampled, log_weights)


def solution(mesh):
    in_specs = (
        P(("groups", "dom"), "seq", None),
        P(("groups", "dom"), "seq", None),
        P(("groups", "dom"), "seq", None),
        P(("groups", "dom"), "seq", None),
        P(),
        P("groups"),
        P("seq", None),
        P(),
        P(None, "seq"),
        P(),
        P(("groups", "dom")),
        P(("groups", "dom")),
    )
    out_specs = (P(("groups", "dom"), "seq", None), P(("groups", "dom")))
    return jax.shard_map(
        on_device, mesh=mesh, in_specs=in_specs, out_specs=out_specs, check_vma=False
    )
```

```python
import functools
import math

import jax
import jax.numpy as jnp
from jax import lax
from jax.experimental import pallas as pl
from jax.experimental.pallas import tpu as pltpu
from jax.sharding import PartitionSpec as P

HEADS = 24
STEPS = 28
LANES = 128
MESH = pl.DeviceIdType.MESH

potential_scale = 4.0
norm_eps = 1e-05


def attend_plain(qb, kb, vb, ob, row, rows, column, head_width):
    cols = pl.ds(column, head_width)
    rescale = math.log2(math.e) / math.sqrt(head_width)
    scores = lax.dot_general(
        qb[pl.ds(row, rows), cols],
        kb[:, cols],
        (((1,), (1,)), ((), ())),
        preferred_element_type=jnp.float32,
    )
    highest = jnp.max(scores, axis=-1, keepdims=True)
    expanded = jnp.exp2((scores - highest) * rescale)
    total = jnp.sum(expanded, axis=-1, keepdims=True)
    mixed = jnp.dot(
        expanded.astype(jnp.bfloat16), vb[:, cols], preferred_element_type=jnp.float32
    )
    ob[pl.ds(row, rows), cols] = (mixed / total).astype(ob.dtype)


def attend_pair(qb, kb, vb, ob, row, rows, column, head_width):
    cols = pl.ds(pl.multiple_of(column, LANES), LANES)
    rescale = math.log2(math.e) / math.sqrt(head_width)
    query = qb[pl.ds(row, rows), cols]
    key = kb[:, cols]
    value = vb[:, cols]
    query_low = lax.broadcasted_iota(jnp.int32, query.shape, 1) < head_width
    value_low = lax.broadcasted_iota(jnp.int32, value.shape, 1) < head_width
    results = []
    for head in range(2):
        own_query = query_low if head == 0 else jnp.logical_not(query_low)
        own_value = value_low if head == 0 else jnp.logical_not(value_low)
        scores = lax.dot_general(
            jnp.where(own_query, query, jnp.zeros_like(query)),
            key,
            (((1,), (1,)), ((), ())),
            preferred_element_type=jnp.float32,
        )
        highest = jnp.max(scores, axis=-1, keepdims=True)
        expanded = jnp.exp2((scores - highest) * rescale).astype(jnp.bfloat16)
        results.append(
            jnp.dot(
                expanded,
                jnp.where(own_value, value, jnp.ones_like(value)),
                preferred_element_type=jnp.float32,
            )
        )
    first, second = results
    low = lax.broadcasted_iota(jnp.int32, first.shape, 1) < head_width
    mixed = jnp.where(low, first, second)
    total = pltpu.roll(jnp.where(low, second, first), head_width, 1)
    ob[pl.ds(row, rows), cols] = (mixed / total).astype(ob.dtype)


def piece(ref, item, groups, cols, start, width):
    if groups == 0:
        return ref.at[item]
    offset = pl.multiple_of((item % groups) * cols + start, LANES)
    return ref.at[item // groups, :, pl.ds(offset, width)]


def weight_exchange(
    n, fan, group_count, dom_count, embed_ref, up_ref, embed_full, up_full,
    shard_own, line_send, line_recv, fan_send, fan_recv, group_send, group_recv, dom_send, dom_recv,
):
    me = lax.axis_index("seq")
    my_group = lax.axis_index("groups")
    my_dom = lax.axis_index("dom")
    share_count = group_count * dom_count
    embed_rows, embed_cols = embed_ref.shape
    up_rows, up_cols = up_ref.shape
    embed_part = embed_cols // share_count
    up_part = up_rows // share_count

    def share(which, owner, group, dom, own=False):
        part = group * dom_count + dom
        if which == 0:
            columns = pl.ds(pl.multiple_of(part * embed_part, LANES), embed_part)
            if own:
                return embed_ref.at[:, columns]
            return embed_full.at[
                pl.ds(pl.multiple_of(owner * embed_rows, 16), embed_rows), columns
            ]
        rows = pl.ds(pl.multiple_of(part * up_part, 16), up_part)
        if own:
            return up_ref.at[rows, :]
        return up_full.at[rows, pl.ds(pl.multiple_of(owner * up_cols, LANES), up_cols)]

    def shard_copy(which):
        if which == 0:
            target = embed_full.at[pl.ds(pl.multiple_of(me * embed_rows, 16), embed_rows), :]
            return pltpu.make_async_copy(embed_ref, target, shard_own.at[0])
        target = up_full.at[:, pl.ds(pl.multiple_of(me * up_cols, LANES), up_cols)]
        return pltpu.make_async_copy(up_ref, target, shard_own.at[1])

    place = lax.div(me, fan)
    lane = lax.rem(me, fan)
    length = n // fan
    signs = (1, -1)

    def line_copy(which, direction, step, incoming):
        sign = signs[direction]
        origin = place - sign * (step if incoming else step - 1)
        owner = lax.rem(origin + n, length) * fan + lane
        to = lax.rem(place + sign + n, length) * fan + lane
        return pltpu.make_async_remote_copy(
            src_ref=share(which, owner, my_group, my_dom, own=step == 1 and not incoming),
            dst_ref=share(which, owner, my_group, my_dom),
            send_sem=line_send.at[which, direction, step - 1],
            recv_sem=line_recv.at[which, direction, step - 1],
            device_id={"seq": to},
            device_id_type=MESH,
        )

    def receives(direction, step):
        return place >= step if direction == 0 else place + step < length

    def sends(direction, step):
        if direction == 0:
            return jnp.logical_and(place >= step - 1, place + 1 < length)
        return jnp.logical_and(place + step - 1 < length, place >= 1)

    def fan_copy(which, spot, shift, incoming, own=False):
        to = lax.rem(lane + shift, fan)
        source = lax.rem(lane - shift + fan, fan) if incoming else lane
        owner = spot * fan + source
        return pltpu.make_async_remote_copy(
            src_ref=share(which, owner, my_group, my_dom, own=own),
            dst_ref=share(which, owner, my_group, my_dom),
            send_sem=fan_send.at[which, shift, spot],
            recv_sem=fan_recv.at[which, shift, spot],
            device_id={"seq": place * fan + to},
            device_id_type=MESH,
        )

    def group_copy(which, owner, shift, incoming):
        other = lax.rem(my_group + shift, group_count)
        source = lax.rem(my_group - shift + group_count, group_count) if incoming else my_group
        return pltpu.make_async_remote_copy(
            src_ref=share(which, owner, source, my_dom),
            dst_ref=share(which, owner, source, my_dom),
            send_sem=group_send.at[which, shift, owner],
            recv_sem=group_recv.at[which, shift, owner],
            device_id={"groups": other},
            device_id_type=MESH,
        )

    def dom_copy(which, owner, shift, group_shift, incoming):
        other = lax.rem(my_dom + shift, dom_count)
        source = lax.rem(my_dom - shift + dom_count, dom_count) if incoming else my_dom
        group = lax.rem(my_group - group_shift + group_count, group_count)
        return pltpu.make_async_remote_copy(
            src_ref=share(which, owner, group, source),
            dst_ref=share(which, owner, group, source),
            send_sem=dom_send.at[which, shift, group_shift, owner],
            recv_sem=dom_recv.at[which, shift, group_shift, owner],
            device_id={"dom": other},
            device_id_type=MESH,
        )

    def spread(which, owner):
        for shift in range(1, group_count):
            group_copy(which, owner, shift, False).start()
        for shift in range(1, dom_count):
            dom_copy(which, owner, shift, 0, False).start()

    def each_arrival(step, action):
        for direction in range(2):

            @pl.when(receives(direction, step))
            def _(direction=direction):
                for which in range(2):
                    action(which, direction, place - signs[direction] * step)

    def line_start():
        for which in range(2):
            for direction in range(2):

                @pl.when(sends(direction, 1))
                def _(which=which, direction=direction):
                    line_copy(which, direction, 1, False).start()

            for shift in range(1, fan):
                fan_copy(which, place, shift, False, own=True).start()
            shard_copy(which).start()

    def line_step(step):
        def action(which, direction, spot):
            line_copy(which, direction, step, True).wait_recv()
            if step + 1 < length:

                @pl.when(sends(direction, step + 1))
                def _():
                    line_copy(which, direction, step + 1, False).start()

            for shift in range(1, fan):
                fan_copy(which, spot, shift, False).start()
            spread(which, spot * fan + lane)

        each_arrival(step, action)

    def fan_step(step):
        def action(which, direction, spot):
            for shift in range(1, fan):
                fan_copy(which, spot, shift, True).wait_recv()
                spread(which, spot * fan + lax.rem(lane - shift + fan, fan))

        if step == 0:
            for which in range(2):
                action(which, 0, place)
        else:
            each_arrival(step, action)

    def group_block(which, owner):
        for group_shift in range(1, group_count):
            group_copy(which, owner, group_shift, True).wait_recv()
            for shift in range(1, dom_count):
                dom_copy(which, owner, shift, group_shift, False).start()

    def group_step(step):
        def action(which, direction, spot):
            if step > 0:
                group_block(which, spot * fan + lane)
            for shift in range(1, fan):
                group_block(which, spot * fan + lax.rem(lane - shift + fan, fan))

        if step == 0:
            for which in range(2):
                action(which, 0, place)
        else:
            each_arrival(step, action)

    def move_step(step):
        if 1 <= step < length:
            line_step(step)
        if 0 <= step - 1 < length:
            fan_step(step - 1)


    def finish_weights(parts=(0, 1)):
        for which in parts:
            shard_copy(which).wait()
            for direction in range(2):
                for step in range(1, length):

                    @pl.when(sends(direction, step))
                    def _(which=which, direction=direction, step=step):
                        line_copy(which, direction, step, False).wait_send()

            @pl.loop(0, length)
            def _(spot, which=which):
                for shift in range(1, fan):
                    fan_copy(which, spot, shift, False).wait_send()

            @pl.loop(1, n)
            def _(step, which=which):
                owner = lax.rem(me + step, n)
                for shift in range(1, group_count):
                    group_copy(which, owner, shift, False).wait_send()
                for shift in range(1, dom_count):
                    for group_shift in range(group_count):
                        dom_copy(which, owner, shift, group_shift, True).wait_recv()
                        dom_copy(which, owner, shift, group_shift, False).wait_send()

    return line_start, move_step, group_step, finish_weights, length


def take(semaphore, region):
    pltpu.make_async_copy(region, region, semaphore).wait()


def shared_weight_exchange(
    n, fan, group_count, dom_count, embed_ref, up_ref, embed_full, up_full,
    shard_own, line_send, line_recv, fan_send, fan_recv, group_send, group_recv, dom_send, dom_recv,
):
    me = lax.axis_index("seq")
    my_group = lax.axis_index("groups")
    my_dom = lax.axis_index("dom")
    share_count = group_count * dom_count
    embed_rows, embed_cols = embed_ref.shape
    up_rows, up_cols = up_ref.shape
    embed_part = embed_cols // share_count
    up_part = up_rows // share_count

    def share(which, owner, group, dom, own=False):
        part = group * dom_count + dom
        if which == 0:
            columns = pl.ds(pl.multiple_of(part * embed_part, LANES), embed_part)
            if own:
                return embed_ref.at[:, columns]
            return embed_full.at[
                pl.ds(pl.multiple_of(owner * embed_rows, 16), embed_rows), columns
            ]
        rows = pl.ds(pl.multiple_of(part * up_part, 16), up_part)
        if own:
            return up_ref.at[rows, :]
        return up_full.at[rows, pl.ds(pl.multiple_of(owner * up_cols, LANES), up_cols)]

    def shard_copy(which):
        if which == 0:
            target = embed_full.at[pl.ds(pl.multiple_of(me * embed_rows, 16), embed_rows), :]
            return pltpu.make_async_copy(embed_ref, target, shard_own.at[0])
        target = up_full.at[:, pl.ds(pl.multiple_of(me * up_cols, LANES), up_cols)]
        return pltpu.make_async_copy(up_ref, target, shard_own.at[1])

    place = lax.div(me, fan)
    lane = lax.rem(me, fan)
    length = n // fan
    signs = (1, -1)

    def line_copy(which, direction, step, incoming):
        sign = signs[direction]
        origin = place - sign * (step if incoming else step - 1)
        owner = lax.rem(origin + n, length) * fan + lane
        to = lax.rem(place + sign + n, length) * fan + lane
        return pltpu.make_async_remote_copy(
            src_ref=share(which, owner, my_group, my_dom, own=step == 1 and not incoming),
            dst_ref=share(which, owner, my_group, my_dom),
            send_sem=line_send.at[which, direction, step - 1],
            recv_sem=line_recv.at[which, direction, step - 1],
            device_id={"seq": to},
            device_id_type=MESH,
        )

    def receives(direction, step):
        return place >= step if direction == 0 else place + step < length

    def sends(direction, step):
        if direction == 0:
            return jnp.logical_and(place >= step - 1, place + 1 < length)
        return jnp.logical_and(place + step - 1 < length, place >= 1)

    def fan_copy(which, spot, shift, incoming, own=False):
        to = lax.rem(lane + shift, fan)
        source = lax.rem(lane - shift + fan, fan) if incoming else lane
        owner = spot * fan + source
        return pltpu.make_async_remote_copy(
            src_ref=share(which, owner, my_group, my_dom, own=own),
            dst_ref=share(which, owner, my_group, my_dom),
            send_sem=fan_send.at[which, shift - 1],
            recv_sem=fan_recv.at[which, shift - 1, spot],
            device_id={"seq": place * fan + to},
            device_id_type=MESH,
        )

    def group_copy(which, owner, shift, incoming):
        other = lax.rem(my_group + shift, group_count)
        source = lax.rem(my_group - shift + group_count, group_count) if incoming else my_group
        return pltpu.make_async_remote_copy(
            src_ref=share(which, owner, source, my_dom),
            dst_ref=share(which, owner, source, my_dom),
            send_sem=group_send.at[which, shift - 1],
            recv_sem=group_recv.at[which, shift - 1, owner],
            device_id={"groups": other},
            device_id_type=MESH,
        )

    def dom_copy(which, owner, shift, group_shift, incoming):
        other = lax.rem(my_dom + shift, dom_count)
        source = lax.rem(my_dom - shift + dom_count, dom_count) if incoming else my_dom
        group = lax.rem(my_group - group_shift + group_count, group_count)
        return pltpu.make_async_remote_copy(
            src_ref=share(which, owner, group, source),
            dst_ref=share(which, owner, group, source),
            send_sem=dom_send.at[which, shift - 1],
            recv_sem=dom_recv.at[which, shift - 1],
            device_id={"dom": other},
            device_id_type=MESH,
        )

    def spread(which, owner):
        for shift in range(1, group_count):
            group_copy(which, owner, shift, False).start()
        for shift in range(1, dom_count):
            dom_copy(which, owner, shift, 0, False).start()

    def each_arrival(step, action):
        for direction in range(2):

            @pl.when(receives(direction, step))
            def _(direction=direction):
                for which in range(2):
                    action(which, direction, place - signs[direction] * step)

    def line_start():
        for which in range(2):
            for direction in range(2):

                @pl.when(sends(direction, 1))
                def _(which=which, direction=direction):
                    line_copy(which, direction, 1, False).start()

            for shift in range(1, fan):
                fan_copy(which, place, shift, False, own=True).start()
            shard_copy(which).start()

    def line_step(step):
        def action(which, direction, spot):
            line_copy(which, direction, step, True).wait_recv()
            if step + 1 < length:

                @pl.when(sends(direction, step + 1))
                def _():
                    line_copy(which, direction, step + 1, False).start()

            for shift in range(1, fan):
                fan_copy(which, spot, shift, False).start()
            spread(which, spot * fan + lane)

        each_arrival(step, action)

    def fan_step(step):
        def action(which, direction, spot):
            for shift in range(1, fan):
                fan_copy(which, spot, shift, True).wait_recv()
                spread(which, spot * fan + lax.rem(lane - shift + fan, fan))

        if step == 0:
            for which in range(2):
                action(which, 0, place)
        else:
            each_arrival(step, action)

    def group_block(which, owner):
        for group_shift in range(1, group_count):
            group_copy(which, owner, group_shift, True).wait_recv()
            for shift in range(1, dom_count):
                dom_copy(which, owner, shift, group_shift, False).start()

    def group_step(step):
        def action(which, direction, spot):
            if step > 0:
                group_block(which, spot * fan + lane)
            for shift in range(1, fan):
                group_block(which, spot * fan + lax.rem(lane - shift + fan, fan))

        if step == 0:
            for which in range(2):
                action(which, 0, place)
        else:
            each_arrival(step, action)

    def parts_of(which, amount):
        if which == 0:
            wide = math.gcd(amount, share_count)
            return embed_full.at[0 : amount // wide * embed_rows, 0 : wide * embed_part]
        wide = math.gcd(amount, share_count)
        return up_full.at[0 : wide * up_part, 0 : amount // wide * up_cols]

    def finish_weights(parts=(0, 1)):
        for which in parts:
            shard_copy(which).wait()
            for direction in range(2):
                for step in range(1, length):

                    @pl.when(sends(direction, step))
                    def _(which=which, direction=direction, step=step):
                        line_copy(which, direction, step, False).wait_send()

            for shift in range(1, fan):
                take(fan_send.at[which, shift - 1], parts_of(which, length))
            for shift in range(1, group_count):
                take(group_send.at[which, shift - 1], parts_of(which, n - 1))
            for shift in range(1, dom_count):
                take(dom_recv.at[which, shift - 1], parts_of(which, (n - 1) * group_count))
                take(dom_send.at[which, shift - 1], parts_of(which, (n - 1) * group_count))

    return line_start, line_step, fan_step, group_step, finish_weights, length


def attention_kernel(
    n, fan, group_count, dom_count, groups, cols, width, head_width, row_block,
    q_ref, k_ref, v_ref, embed_ref, up_ref, o_ref, embed_full, up_full,
    qb, kb, vb, ob, send_sem, recv_sem, own_sem, back_send, back_recv, back_own,
    shard_own, line_send, line_recv, fan_send, fan_recv, group_send, group_recv, dom_send, dom_recv,
):
    me = lax.axis_index("seq")
    my_group = lax.axis_index("groups")
    my_dom = lax.axis_index("dom")
    tokens = q_ref.shape[1]
    total_tokens = n * tokens
    chunks = cols // width
    inputs = ((q_ref, qb), (k_ref, kb), (v_ref, vb))

    barrier = pltpu.get_barrier_semaphore()

    @pl.loop(1, n)
    def _(step):
        pl.semaphore_signal(
            barrier, inc=1, device_id={"seq": lax.rem(me + step, n)}, device_id_type=MESH
        )

    for step in range(1, group_count):
        peer = {"groups": lax.rem(my_group + step, group_count)}
        pl.semaphore_signal(barrier, inc=1, device_id=peer, device_id_type=MESH)
    for step in range(1, dom_count):
        peer = {"dom": lax.rem(my_dom + step, dom_count)}
        pl.semaphore_signal(barrier, inc=1, device_id=peer, device_id_type=MESH)
    pl.semaphore_wait(barrier, n - 1 + group_count - 1 + dom_count - 1)

    line_start, move_step, group_step, finish_weights, length = weight_exchange(
        n, fan, group_count, dom_count, embed_ref, up_ref, embed_full, up_full,
        shard_own, line_send, line_recv, fan_send, fan_recv, group_send, group_recv,
        dom_send, dom_recv,
    )

    def rows_of(ref, owner, chunk):
        row = pl.ds(pl.multiple_of(owner * tokens, 16), tokens)
        return ref.at[row, pl.ds(chunk * width, width)]

    def outgoing(index, chunk, target, slot):
        source, buffer = inputs[index]
        return pltpu.make_async_remote_copy(
            src_ref=piece(source, target, groups, cols, chunk * width, width),
            dst_ref=rows_of(buffer, me, chunk),
            send_sem=send_sem.at[index, chunk, target],
            recv_sem=recv_sem.at[index, chunk, slot],
            device_id={"seq": target},
            device_id_type=MESH,
        )

    def own_copy(index, chunk):
        source, buffer = inputs[index]
        return pltpu.make_async_copy(
            piece(source, me, groups, cols, chunk * width, width),
            rows_of(buffer, me, chunk),
            own_sem.at[index, chunk],
        )

    def returned(chunk, target, slot):
        return pltpu.make_async_remote_copy(
            src_ref=rows_of(ob, target, chunk),
            dst_ref=piece(o_ref, me, groups, cols, chunk * width, width),
            send_sem=back_send.at[chunk, target],
            recv_sem=back_recv.at[chunk, slot],
            device_id={"seq": target},
            device_id_type=MESH,
        )

    def own_return(chunk):
        return pltpu.make_async_copy(
            rows_of(ob, me, chunk),
            piece(o_ref, me, groups, cols, chunk * width, width),
            back_own.at[chunk],
        )

    weight_steps = length + 2

    def weight_step(step):
        move_step(step)
        if 0 <= step - 2 < length:
            group_step(step - 2)

    ready = 1
    for chunk in range(chunks):
        if chunk == 0:
            line_start()
        elif ready < weight_steps:
            weight_step(ready)
            ready += 1
        for index in range(3):
            own_copy(index, chunk).start()

            @pl.loop(1, n)
            def _(step, index=index, chunk=chunk):
                outgoing(index, chunk, lax.rem(me + step, n), me).start()

    paired = 2 * head_width == LANES and width % LANES == 0
    unit = LANES if paired else head_width
    blocks = total_tokens // row_block

    for chunk in range(chunks):
        for index in range(3):
            own_copy(index, chunk).wait()

            @pl.loop(1, n)
            def _(step, index=index, chunk=chunk):
                other = lax.rem(me + step, n)
                outgoing(index, chunk, other, other).wait_recv()

        if paired:

            @pl.loop(0, (width // unit) * blocks)
            def _(step, chunk=chunk):
                attend_pair(
                    qb, kb, vb, ob,
                    pl.multiple_of((step % blocks) * row_block, row_block), row_block,
                    chunk * width + (step // blocks) * unit, head_width,
                )
        else:
            for head in range(width // unit):

                @pl.loop(0, blocks)
                def _(step, head=head, chunk=chunk):
                    attend_plain(
                        qb, kb, vb, ob,
                        pl.multiple_of(step * row_block, row_block), row_block,
                        chunk * width + head * unit, head_width,
                    )

        own_return(chunk).start()

        @pl.loop(1, n)
        def _(step, chunk=chunk):
            returned(chunk, lax.rem(me + step, n), me).start()

        if ready < weight_steps and chunk < chunks - 1:
            weight_step(ready)
            ready += 1

    for step in range(ready, weight_steps):
        weight_step(step)
    finish_weights()

    for chunk in range(chunks):
        own_return(chunk).wait()
        for index in range(3):

            @pl.loop(1, n)
            def _(step, index=index, chunk=chunk):
                outgoing(index, chunk, lax.rem(me + step, n), me).wait_send()

        @pl.loop(1, n)
        def _(step, chunk=chunk):
            other = lax.rem(me + step, n)
            returned(chunk, other, other).wait_recv()
            returned(chunk, other, me).wait_send()


def attention(queries, keys, values, embed_weight, up_weight):
    n = lax.axis_size("seq")
    group_count = lax.axis_size("groups")
    dom_count = lax.axis_size("dom")
    fan = 2 if n % 2 == 0 else 1
    particles, tokens, model_width = queries.shape
    head_width = model_width // HEADS
    per_device = particles * HEADS // n
    cols = per_device * head_width
    aligned = model_width % cols == 0 and cols % LANES == 0
    groups = model_width // cols if aligned else 0
    width = 2 * LANES if aligned and cols % (2 * LANES) == 0 else cols
    chunks = cols // width
    total_tokens = n * tokens

    def to_items(array):
        if aligned:
            return array
        split = array.reshape(particles, tokens, HEADS, head_width).transpose(0, 2, 1, 3)
        split = split.reshape(n, per_device, tokens, head_width).transpose(0, 2, 1, 3)
        return split.reshape(n, tokens, cols)

    operands = tuple(to_items(a) for a in (queries, keys, values))
    any_spec = pl.BlockSpec(memory_space=pl.ANY)
    embed_shape = (n * embed_weight.shape[0], embed_weight.shape[1])
    up_shape = (up_weight.shape[0], n * up_weight.shape[1])
    out, embed_full, up_full = pl.pallas_call(
        functools.partial(
            attention_kernel, n, fan, group_count, dom_count, groups, cols, width, head_width,
            min(256, total_tokens),
        ),
        out_shape=(
            jax.ShapeDtypeStruct(operands[0].shape, jnp.bfloat16),
            jax.ShapeDtypeStruct(embed_shape, jnp.bfloat16),
            jax.ShapeDtypeStruct(up_shape, jnp.bfloat16),
        ),
        in_specs=[any_spec] * 5,
        out_specs=(any_spec,) * 3,
        scratch_shapes=[pltpu.VMEM((total_tokens, cols), jnp.bfloat16)] * 4
        + [
            pltpu.SemaphoreType.DMA((3, chunks, n)),
            pltpu.SemaphoreType.DMA((3, chunks, n)),
            pltpu.SemaphoreType.DMA((3, chunks)),
            pltpu.SemaphoreType.DMA((chunks, n)),
            pltpu.SemaphoreType.DMA((chunks, n)),
            pltpu.SemaphoreType.DMA((chunks,)),
            pltpu.SemaphoreType.DMA((2,)),
            pltpu.SemaphoreType.DMA((2, 2, n // fan)),
            pltpu.SemaphoreType.DMA((2, 2, n // fan)),
            pltpu.SemaphoreType.DMA((2, fan, n // fan)),
            pltpu.SemaphoreType.DMA((2, fan, n // fan)),
            pltpu.SemaphoreType.DMA((2, group_count, n)),
            pltpu.SemaphoreType.DMA((2, group_count, n)),
            pltpu.SemaphoreType.DMA((2, dom_count, group_count, n)),
            pltpu.SemaphoreType.DMA((2, dom_count, group_count, n)),
        ],
        compiler_params=pltpu.CompilerParams(
            collective_id=0, has_side_effects=True, vmem_limit_bytes=60 * 1024 * 1024
        ),
        name="attention",
    )(*operands, embed_weight, up_weight)
    if not aligned:
        out = out.reshape(n, tokens, per_device, head_width).transpose(0, 2, 1, 3)
        out = out.reshape(particles, HEADS, tokens, head_width).transpose(0, 2, 1, 3)
    return out.reshape(particles * tokens, model_width), embed_full, up_full


def reward_kernel(n, doms, particles, x_ref, o_ref, held, send_sem, recv_sem):
    me = lax.axis_index("dom") * n + lax.axis_index("seq")
    members = n * doms

    def target(step):
        other = lax.rem(me + step, members)
        return other, {"dom": other // n, "seq": other % n}

    def copy(step, slot):
        other, device = target(step)
        return pltpu.make_async_remote_copy(
            src_ref=x_ref,
            dst_ref=held.at[me],
            send_sem=send_sem.at[other],
            recv_sem=recv_sem.at[slot],
            device_id=device,
            device_id_type=MESH,
        )

    barrier = pltpu.get_barrier_semaphore()

    @pl.loop(1, members)
    def _(step):
        _, device = target(step)
        pl.semaphore_signal(barrier, inc=1, device_id=device, device_id_type=MESH)

    pl.semaphore_wait(barrier, members - 1)

    @pl.loop(1, members)
    def _(step):
        copy(step, me).start()

    held[me] = x_ref[...]

    @pl.loop(1, members)
    def _(step):
        copy(step, lax.rem(me + step, members)).wait_recv()

    logits = []
    for dom in range(doms):
        rewards = jnp.sum(held[dom * n : (dom + 1) * n], axis=0)[:1]
        value = held[dom * n][1:2] + potential_scale * rewards
        used = lax.broadcasted_iota(jnp.int32, value.shape, 1) < particles
        logits.append(jnp.where(used, value, -jnp.inf))
    highest = functools.reduce(jnp.maximum, [jnp.max(v, axis=1, keepdims=True) for v in logits])
    total = sum(jnp.sum(jnp.exp(v - highest), axis=1, keepdims=True) for v in logits)
    own = logits[0]
    for dom in range(1, doms):
        own = jnp.where(lax.axis_index("dom") == dom, logits[dom], own)
    o_ref[...] = jnp.broadcast_to(own - (highest + jnp.log(total)), o_ref.shape)

    @pl.loop(1, members)
    def _(step):
        copy(step, me).wait_send()


def weigh(partial_value, prev_logw, n, doms):
    particles = partial_value.shape[0]
    rows = jnp.stack([partial_value, prev_logw])
    padded = jnp.pad(rows, ((0, 8 - 2), (0, LANES - particles)))
    vmem = pl.BlockSpec(memory_space=pltpu.VMEM)
    out = pl.pallas_call(
        functools.partial(reward_kernel, n, doms, particles),
        out_shape=jax.ShapeDtypeStruct((8, LANES), jnp.float32),
        in_specs=[vmem],
        out_specs=vmem,
        scratch_shapes=[
            pltpu.VMEM((n * doms, 8, LANES), jnp.float32),
            pltpu.SemaphoreType.DMA((n * doms,)),
            pltpu.SemaphoreType.DMA((n * doms,)),
        ],
        compiler_params=pltpu.CompilerParams(collective_id=1, has_side_effects=True),
        name="rewards",
    )(padded)
    return out[0, :particles]


def part_sum(block, rows):
    parts = [
        jnp.sum(block[at : at + rows], axis=0, keepdims=True)
        for at in range(0, block.shape[0], rows)
    ]
    return jnp.concatenate(parts, axis=0)


def fused_kernel(
    n, fan, group_count, dom_count, rounds, groups, chunks, head_width, row_block, tile,
    q_ref, k_ref, v_ref, lat_ref, wo_ref, step_in, embed_ref, gain_in, up_ref, head_in,
    prev_in, anc_in, out_ref, logw_ref,
    step_ref, gain_ref, head_ref, prev_ref, anc_ref, picked,
    qb, kb, vb, ob, mixed, embed_full, up_full, wo, lat, velocity, clean, embedded, features,
    cand, score, mine, held,
    send_sem, recv_sem, back_send, back_recv,
    shard_own, line_send, line_recv, fan_send, fan_recv, group_send, group_recv, dom_send, dom_recv,
    load_sem, step_send, step_recv, score_send, score_recv,
):
    me = lax.axis_index("seq")
    my_group = lax.axis_index("groups")
    my_dom = lax.axis_index("dom")
    particles, tokens, model_width = q_ref.shape
    rows = particles * tokens
    share = particles // rounds
    share_rows = share * tokens
    total_tokens = n * tokens
    inputs = ((q_ref, qb), (k_ref, kb), (v_ref, vb))
    members = n * dom_count
    member = my_dom * n + me

    def other_member(step):
        other = lax.rem(member + step, members)
        return other, {"dom": other // n, "seq": other % n}

    small = (
        (wo_ref, wo), (lat_ref, lat), (step_in, step_ref), (gain_in, gain_ref),
        (head_in, head_ref), (prev_in, prev_ref), (anc_in, anc_ref),
    )
    loads = [
        pltpu.make_async_copy(source, target, load_sem.at[at])
        for at, (source, target) in enumerate(small)
    ]

    barrier = pltpu.get_barrier_semaphore()

    @pl.loop(1, members)
    def _(step):
        _, device = other_member(step)
        pl.semaphore_signal(barrier, inc=1, device_id=device, device_id_type=MESH)

    for step in range(1, group_count):
        peer = {"groups": lax.rem(my_group + step, group_count)}
        pl.semaphore_signal(barrier, inc=1, device_id=peer, device_id_type=MESH)
    for load in loads:
        load.start()
    pl.semaphore_wait(barrier, members - 1 + group_count - 1)

    line_start, line_step, fan_step, group_step, finish_weights, length = shared_weight_exchange(
        n, fan, group_count, dom_count, embed_ref, up_ref, embed_full, up_full,
        shard_own, line_send, line_recv, fan_send, fan_recv, group_send, group_recv,
        dom_send, dom_recv,
    )

    cols = model_width // groups

    def source_of(ref, item, chunk):
        turn, start, width = chunks[chunk]
        offset = pl.multiple_of(groups * start + (item % groups) * width, LANES)
        return ref.at[turn * share + item // groups, :, pl.ds(offset, width)]

    def mixed_of(item, chunk):
        turn, start, width = chunks[chunk]
        offset = pl.multiple_of(groups * start + (item % groups) * width, LANES)
        row = pl.multiple_of((turn * share + item // groups) * tokens, 16)
        return mixed.at[pl.ds(row, tokens), pl.ds(offset, width)]

    def rows_of(ref, owner, chunk):
        turn, start, width = chunks[chunk]
        row = pl.ds(pl.multiple_of(owner * tokens, 16), tokens)
        return ref.at[row, pl.ds(turn * cols + start, width)]

    def outgoing(index, chunk, target):
        source, buffer = inputs[index]
        return pltpu.make_async_remote_copy(
            src_ref=source_of(source, target, chunk),
            dst_ref=rows_of(buffer, me, chunk),
            send_sem=send_sem.at[index, chunk],
            recv_sem=recv_sem.at[index, chunk],
            device_id={"seq": target},
            device_id_type=MESH,
        )

    def own_copy(index, chunk):
        source, buffer = inputs[index]
        return pltpu.make_async_copy(
            source_of(source, me, chunk), rows_of(buffer, me, chunk), recv_sem.at[index, chunk]
        )

    def returned(chunk, target):
        return pltpu.make_async_remote_copy(
            src_ref=rows_of(ob, target, chunk),
            dst_ref=mixed_of(me, chunk),
            send_sem=back_send.at[chunk],
            recv_sem=back_recv.at[chunk],
            device_id={"seq": target},
            device_id_type=MESH,
        )

    def own_return(chunk):
        return pltpu.make_async_copy(
            rows_of(ob, me, chunk), mixed_of(me, chunk), back_recv.at[chunk]
        )

    count = len(chunks)
    blocks = total_tokens // row_block

    def issue(chunk):
        for index in range(3):
            own_copy(index, chunk).start()

            @pl.loop(1, n)
            def _(step, index=index):
                outgoing(index, chunk, lax.rem(me + step, n)).start()

    def attend(chunk):
        turn, start, width = chunks[chunk]
        first = turn * cols + start

        @pl.loop(0, (width // LANES) * blocks)
        def _(step):
            attend_pair(
                qb, kb, vb, ob,
                pl.multiple_of((step % blocks) * row_block, row_block), row_block,
                first + (step // blocks) * LANES, head_width,
            )

    def arrive(chunk):
        turn, start, width = chunks[chunk]
        for index in range(3):
            buffer = inputs[index][1]
            first = turn * cols + start
            take(recv_sem.at[index, chunk], buffer.at[:, first : first + width])

    def give_back(chunk):
        own_return(chunk).start()

        @pl.loop(1, n)
        def _(step):
            returned(chunk, lax.rem(me + step, n)).start()

    def project(chunk):
        if chunk == 0:
            for load in loads:
                load.wait()
        sigma = step_ref[0].astype(jnp.float32) / STEPS
        turn, start, width = chunks[chunk]
        inner = pl.ds(groups * start, groups * width)
        own_rows = pl.ds(turn * share_rows, share_rows)
        final = chunk + 1 == count or chunks[chunk + 1][0] != turn
        take(back_recv.at[chunk], mixed.at[own_rows, inner])

        @pl.loop(0, model_width // tile, unroll=model_width // tile)
        def _(step):
            columns = pl.ds(pl.multiple_of(step * tile, tile), tile)
            part = jnp.dot(
                mixed[own_rows, inner], wo[inner, columns], preferred_element_type=jnp.float32
            )
            if start > 0:
                part = velocity[own_rows, columns] + part
            if not final:
                velocity[own_rows, columns] = part
                return
            for item in range(share):
                at = slice(item * tokens, (item + 1) * tokens)
                spot = turn * share + item
                flat = lat[spot, :, columns].astype(jnp.float32)
                moved = flat + part[at]
                clean[spot * tokens : (spot + 1) * tokens, columns] = (
                    flat - sigma * moved
                ).astype(jnp.bfloat16)
                cand[my_dom * particles + spot, :, columns] = (flat - moved / STEPS).astype(
                    jnp.bfloat16
                )

    def step_copy(turn, shift, incoming):
        source = lax.rem(my_dom - shift + dom_count, dom_count) if incoming else my_dom
        block = cand.at[pl.ds(source * particles + turn * share, share)]
        return pltpu.make_async_remote_copy(
            src_ref=block,
            dst_ref=block,
            send_sem=step_send.at[turn, shift - 1],
            recv_sem=step_recv.at[turn, shift - 1],
            device_id={"dom": lax.rem(my_dom + shift, dom_count)},
            device_id_type=MESH,
        )

    def embed(turn):
        if turn == 0:
            finish_weights((0,))
        own_rows = pl.ds(turn * share_rows, share_rows)

        @pl.loop(0, embedded.shape[1] // tile, unroll=embedded.shape[1] // tile)
        def _(step):
            columns = pl.ds(pl.multiple_of(step * tile, tile), tile)
            embedded[own_rows, columns] = jnp.dot(
                clean[own_rows, :], embed_full[:, columns], preferred_element_type=jnp.float32
            )

        for shift in range(1, dom_count):
            step_copy(turn, shift, False).start()

        @pl.loop(turn * share, (turn + 1) * share, unroll=share)
        def _(item):
            item_rows = pl.ds(pl.multiple_of(item * tokens, tokens), tokens)
            block = embedded[item_rows, :]
            centered = block - jnp.mean(block, axis=1, keepdims=True)
            variance = jnp.mean(centered * centered, axis=1, keepdims=True)
            normed = centered * lax.rsqrt(variance + norm_eps) * gain_ref[...]
            features[item_rows, :] = jax.nn.gelu(normed).astype(jnp.bfloat16)

    def judge(turn):
        if turn == 0:
            finish_weights((1,))
        own_rows = pl.ds(turn * share_rows, share_rows)

        @pl.loop(0, up_full.shape[1] // tile, unroll=min(8, up_full.shape[1] // tile))
        def _(step):
            columns = pl.ds(pl.multiple_of(step * tile, tile), tile)
            hidden = jnp.dot(
                features[own_rows, :], up_full[:, columns], preferred_element_type=jnp.float32
            )
            score[turn * share : (turn + 1) * share, :] += (
                part_sum(jax.nn.gelu(hidden), tokens) * head_ref[:, columns]
            )

    actions = {
        "issue": issue, "arrive": arrive, "attend": attend, "return": give_back,
        "line": line_step, "fan": fan_step, "group": group_step, "start": lambda _: line_start(),
        "project": project, "embed": embed, "judge": judge,
    }
    score[...] = jnp.zeros_like(score)
    for name, at in plan(chunks, length):
        actions[name](at)

    partial_value = jnp.sum(score[...], axis=1, keepdims=True) / math.sqrt(total_tokens)
    lane = lax.broadcasted_iota(jnp.int32, (particles, LANES), 1)
    row = lax.broadcasted_iota(jnp.int32, (particles, LANES), 0)
    before = jnp.zeros((particles, LANES), jnp.float32)
    for item in range(particles):
        before = jnp.where(row == item, prev_ref[item], before)
    half = LANES // 2
    own_block = jnp.where(lane < half, partial_value, before)
    mine[0:particles, :] = own_block
    held[member, 0:particles, :] = own_block

    def score_copy(step):
        _, device = other_member(step)
        return pltpu.make_async_remote_copy(
            src_ref=mine,
            dst_ref=held.at[member],
            send_sem=score_send.at[0],
            recv_sem=score_recv.at[0],
            device_id=device,
            device_id_type=MESH,
        )

    @pl.loop(1, members)
    def _(step):
        score_copy(step).start()

    for turn in range(rounds):
        for shift in range(1, dom_count):
            step_copy(turn, shift, True).wait_recv()
    for item in range(particles):
        picked[item] = cand[anc_ref[item]]
    write = pltpu.make_async_copy(picked, out_ref, load_sem.at[0])
    write.start()

    for chunk in range(count):
        sent = qb.at[0 : (n - 1) * tokens, 0 : chunks[chunk][2]]
        for index in range(3):
            take(send_sem.at[index, chunk], sent)
        take(back_send.at[chunk], sent)

    for turn in range(rounds):
        for shift in range(1, dom_count):
            step_copy(turn, shift, False).wait_send()

    take(score_recv.at[0], held.at[0 : members - 1])

    logits = []
    for dom in range(dom_count):
        reward = jnp.sum(held[dom * n : (dom + 1) * n, 0:particles, :], axis=0)[:, 0:1]
        logits.append(held[dom * n, 0:particles, :][:, half : half + 1] + potential_scale * reward)
    highest = functools.reduce(
        jnp.maximum, [jnp.max(value, axis=0, keepdims=True) for value in logits]
    )
    total = sum(jnp.sum(jnp.exp(value - highest), axis=0, keepdims=True) for value in logits)
    own = logits[0]
    for dom in range(1, dom_count):
        own = jnp.where(my_dom == dom, logits[dom], own)
    result = jnp.broadcast_to(own - (highest + jnp.log(total)), (particles, LANES))
    result = jnp.sum(jnp.where(row == lane, result, 0.0), axis=0, keepdims=True)
    logw_ref[...] = result[:, 0:particles]

    take(score_send.at[0], held.at[0 : members - 1])
    write.wait()


def plan(chunks, length):
    count = len(chunks)
    last = chunks[-1][0]
    early = [chunk for chunk in range(count) if chunks[chunk][0] < last]
    late = [chunk for chunk in range(count) if chunks[chunk][0] == last]
    lines = list(range(2, length))
    fans = list(range(1, length))
    steps = [("start", 0), ("issue", 0), ("line", 1), ("fan", 0)]
    if length == 1:
        steps = [("start", 0), ("issue", 0), ("fan", 0)]
    steps += [("issue", chunk) for chunk in range(1, min(2, count))]
    for chunk in range(count):
        if chunk == count - 1:
            steps += [("line", step) for step in lines] + [("fan", step) for step in fans]
            steps += [("group", step) for step in range(length)]
            steps += [("project", part) for part in early]
        elif chunk == 0:
            steps += [("line", step) for step in lines[:1]] + [("fan", step) for step in fans[:1]]
            lines, fans = lines[1:], fans[1:]
        steps += [("arrive", chunk), ("attend", chunk), ("return", chunk)]
        if chunk + 2 < count:
            steps.append(("issue", chunk + 2))
        if chunk < count - 1:
            steps += [("line", step) for step in lines[:1]] + [("fan", step) for step in fans[:1]]
            lines, fans = lines[1:], fans[1:]
    for turn in range(last):
        steps += [("embed", turn), ("judge", turn)]
    return steps + [("project", part) for part in late] + [("embed", last), ("judge", last)]


def chunk_list(rounds, cols):
    chunks = []
    for turn in range(rounds):
        widths = [2 * LANES] * (cols // (2 * LANES)) + [LANES] * (cols % (2 * LANES) // LANES)
        if turn == 0:
            widths.reverse()
        start = 0
        for width in widths:
            chunks.append((turn, start, width))
            start += width
    return tuple(chunks)


def in_place(array):
    return pltpu.with_memory_space_constraint(array, pltpu.HBM)


def fused(
    latents, queries, keys, values, out_weight, step_index, embed_weight, norm_gain, up_weight,
    head_weight, prev_logw, ancestors,
):
    n = lax.axis_size("seq")
    group_count = lax.axis_size("groups")
    dom_count = lax.axis_size("dom")
    fan = 2 if n % 2 == 0 else 1
    particles, tokens, model_width = queries.shape
    head_width = model_width // HEADS
    rounds = round_count(n, particles, model_width)
    cols = particles * model_width // (n * rounds)
    groups = model_width // cols
    chunks = chunk_list(rounds, cols)
    count = len(chunks)
    rows = particles * tokens
    total_tokens = n * tokens
    members = n * dom_count
    fan_steps, group_steps, dom_steps = (max(x - 1, 1) for x in (fan, group_count, dom_count))
    tile = 512
    embed_shape = (n * embed_weight.shape[0], embed_weight.shape[1])
    up_shape = (up_weight.shape[0], n * up_weight.shape[1])
    hbm = pl.BlockSpec(memory_space=pl.ANY)
    vmem = pl.BlockSpec(memory_space=pltpu.VMEM)
    bf16 = jnp.bfloat16
    dma = pltpu.SemaphoreType.DMA
    resampled, logw = pl.pallas_call(
        functools.partial(
            fused_kernel, n, fan, group_count, dom_count, rounds, groups, chunks, head_width,
            min(256, total_tokens), tile,
        ),
        out_shape=(
            jax.ShapeDtypeStruct(latents.shape, bf16),
            jax.ShapeDtypeStruct((1, particles), jnp.float32),
        ),
        in_specs=[hbm] * 12,
        out_specs=(hbm, vmem),
        scratch_shapes=[
            pltpu.SMEM(step_index.shape, jnp.int32),
            pltpu.VMEM((1, norm_gain.shape[0]), jnp.float32),
            pltpu.VMEM((1, head_weight.shape[0]), jnp.float32),
            pltpu.SMEM(prev_logw.shape, jnp.float32),
            pltpu.SMEM(ancestors.shape, jnp.int32),
            pltpu.VMEM(latents.shape, bf16),
        ]
        + [pltpu.VMEM((total_tokens, rounds * cols), bf16)] * 4
        + [
            pltpu.VMEM((rows, model_width), bf16),
            pltpu.VMEM(embed_shape, bf16),
            pltpu.VMEM(up_shape, bf16),
            pltpu.VMEM(out_weight.shape, bf16),
            pltpu.VMEM(latents.shape, bf16),
            pltpu.VMEM((rows, model_width), jnp.float32),
            pltpu.VMEM((rows, model_width), bf16),
            pltpu.VMEM((rows, embed_shape[1]), jnp.float32),
            pltpu.VMEM((rows, embed_shape[1]), bf16),
            pltpu.VMEM((dom_count * particles, tokens, model_width), bf16),
            pltpu.VMEM((particles, tile), jnp.float32),
            pltpu.VMEM((8, LANES), jnp.float32),
            pltpu.VMEM((members, 8, LANES), jnp.float32),
            dma((3, count)),
            dma((3, count)),
            dma((count,)),
            dma((count,)),
            dma((2,)),
            dma((2, 2, max(n // fan - 1, 1))),
            dma((2, 2, max(n // fan - 1, 1))),
            dma((2, fan_steps)),
            dma((2, fan_steps, n // fan)),
            dma((2, group_steps)),
            dma((2, group_steps, n)),
            dma((2, dom_steps)),
            dma((2, dom_steps)),
            dma((7,)),
            dma((rounds, dom_steps)),
            dma((rounds, dom_steps)),
            dma((1,)),
            dma((1,)),
        ],
        compiler_params=pltpu.CompilerParams(
            collective_id=0, has_side_effects=True, vmem_limit_bytes=44 * 1024 * 1024
        ),
        name="step",
    )(
        *map(
            in_place,
            (queries, keys, values, latents, out_weight),
        ),
        step_index,
        *map(
            in_place,
            (
                embed_weight, norm_gain.reshape(1, -1), up_weight, head_weight.reshape(1, -1),
                prev_logw, ancestors,
            ),
        ),
    )
    return resampled, logw[0]


def round_count(n, particles, model_width):
    for rounds in (2, 1):
        if particles % rounds or (particles * HEADS) % (n * rounds):
            continue
        cols = particles * model_width // (n * rounds)
        if cols % LANES == 0 and model_width % cols == 0:
            return rounds
    return 0


def tiles_evenly(queries, embed_weight, up_weight):
    n = lax.axis_size("seq")
    particles, tokens, model_width = queries.shape
    if 2 * (model_width // HEADS) != LANES or not round_count(n, particles, model_width):
        return False
    return model_width % 512 == 0 and embed_weight.shape[1] % 512 == 0


def on_device(
    latents,
    queries,
    keys,
    values,
    out_weight,
    step_index,
    embed_weight,
    norm_gain,
    up_weight,
    head_weight,
    prev_logw,
    ancestors,
):
    seq_count = lax.axis_size("seq")
    dom_count = lax.axis_size("dom")
    local_particles, local_tokens, model_width = latents.shape
    local_rows = local_particles * local_tokens
    total_tokens = local_tokens * seq_count
    dom = lax.axis_index("dom")

    if tiles_evenly(queries, embed_weight, up_weight):
        return fused(
            latents, queries, keys, values, out_weight, step_index, embed_weight, norm_gain,
            up_weight, head_weight, prev_logw, ancestors,
        )
    attended, embed_full, up_full = attention(
        queries, keys, values, embed_weight, up_weight
    )
    flat = latents.reshape(local_rows, model_width).astype(jnp.float32)
    velocity = flat + jnp.dot(attended, out_weight, preferred_element_type=jnp.float32)
    sigma = step_index[0].astype(jnp.float32) / STEPS
    clean = (flat - sigma * velocity).astype(jnp.bfloat16)
    stepped = (flat - velocity / STEPS).astype(jnp.bfloat16)
    stepped = stepped.reshape(local_particles, local_tokens, model_width)
    candidates = [stepped]
    for shift in range(1, dom_count):
        pairs = [((to + shift) % dom_count, to) for to in range(dom_count)]
        candidates.append(lax.ppermute(stepped, "dom", pairs))
    embedded = jnp.dot(
        clean,
        embed_full,
        preferred_element_type=jnp.float32,
    )
    centre = jnp.mean(embedded, axis=1, keepdims=True)
    centered = embedded - centre
    variance = jnp.mean(centered * centered, axis=1, keepdims=True)
    features = jax.nn.gelu(centered * lax.rsqrt(variance + norm_eps) * norm_gain[None, :]).astype(
        jnp.bfloat16
    )
    scored = (
        jax.nn.gelu(
            jnp.dot(
                features,
                up_full,
                preferred_element_type=jnp.float32,
            )
        )
        * head_weight[None, :]
    )
    partial_value = jnp.sum(jnp.sum(scored, axis=1).reshape(local_particles, local_tokens), axis=1)
    partial_value = partial_value / math.sqrt(total_tokens)
    log_weights = weigh(partial_value, prev_logw, seq_count, dom_count)
    slot = lax.rem(ancestors // local_particles - dom + dom_count, dom_count)
    row = slot * local_particles + lax.rem(ancestors, local_particles)
    resampled = jnp.take(jnp.concatenate(candidates), row, axis=0, mode="clip")
    return (resampled, log_weights)


def solution(mesh):
    in_specs = (
        P(("groups", "dom"), "seq", None),
        P(("groups", "dom"), "seq", None),
        P(("groups", "dom"), "seq", None),
        P(("groups", "dom"), "seq", None),
        P(),
        P("groups"),
        P("seq", None),
        P(),
        P(None, "seq"),
        P(),
        P(("groups", "dom")),
        P(("groups", "dom")),
    )
    out_specs = (P(("groups", "dom"), "seq", None), P(("groups", "dom")))
    return jax.shard_map(
        on_device, mesh=mesh, in_specs=in_specs, out_specs=out_specs, check_vma=False
    )
```

```python
import functools
import math

import jax
import jax.numpy as jnp
from jax import lax
from jax.experimental import pallas as pl
from jax.experimental.pallas import tpu as pltpu
from jax.sharding import PartitionSpec as P

HEADS = 24
STEPS = 28
LANES = 128
MESH = pl.DeviceIdType.MESH

potential_scale = 4.0
norm_eps = 1e-05


def attend_plain(qb, kb, vb, ob, row, rows, column, head_width):
    cols = pl.ds(column, head_width)
    rescale = math.log2(math.e) / math.sqrt(head_width)
    scores = lax.dot_general(
        qb[pl.ds(row, rows), cols],
        kb[:, cols],
        (((1,), (1,)), ((), ())),
        preferred_element_type=jnp.float32,
    )
    highest = jnp.max(scores, axis=-1, keepdims=True)
    expanded = jnp.exp2((scores - highest) * rescale)
    total = jnp.sum(expanded, axis=-1, keepdims=True)
    mixed = jnp.dot(
        expanded.astype(jnp.bfloat16), vb[:, cols], preferred_element_type=jnp.float32
    )
    ob[pl.ds(row, rows), cols] = (mixed / total).astype(ob.dtype)


def attend_pair(qb, kb, vb, ob, row, rows, column, head_width):
    cols = pl.ds(pl.multiple_of(column, LANES), LANES)
    rescale = math.log2(math.e) / math.sqrt(head_width)
    query = qb[pl.ds(row, rows), cols]
    key = kb[:, cols]
    value = vb[:, cols]
    query_low = lax.broadcasted_iota(jnp.int32, query.shape, 1) < head_width
    value_low = lax.broadcasted_iota(jnp.int32, value.shape, 1) < head_width
    results = []
    for head in range(2):
        own_query = query_low if head == 0 else jnp.logical_not(query_low)
        own_value = value_low if head == 0 else jnp.logical_not(value_low)
        scores = lax.dot_general(
            jnp.where(own_query, query, jnp.zeros_like(query)),
            key,
            (((1,), (1,)), ((), ())),
            preferred_element_type=jnp.float32,
        )
        highest = jnp.max(scores, axis=-1, keepdims=True)
        expanded = jnp.exp2((scores - highest) * rescale).astype(jnp.bfloat16)
        results.append(
            jnp.dot(
                expanded,
                jnp.where(own_value, value, jnp.ones_like(value)),
                preferred_element_type=jnp.float32,
            )
        )
    first, second = results
    low = lax.broadcasted_iota(jnp.int32, first.shape, 1) < head_width
    mixed = jnp.where(low, first, second)
    total = pltpu.roll(jnp.where(low, second, first), head_width, 1)
    ob[pl.ds(row, rows), cols] = (mixed / total).astype(ob.dtype)


def piece(ref, item, groups, cols, start, width):
    if groups == 0:
        return ref.at[item]
    offset = pl.multiple_of((item % groups) * cols + start, LANES)
    return ref.at[item // groups, :, pl.ds(offset, width)]


def weight_exchange(
    n, fan, group_count, dom_count, embed_ref, up_ref, embed_full, up_full,
    shard_own, line_send, line_recv, fan_send, fan_recv, group_send, group_recv, dom_send, dom_recv,
):
    me = lax.axis_index("seq")
    my_group = lax.axis_index("groups")
    my_dom = lax.axis_index("dom")
    share_count = group_count * dom_count
    embed_rows, embed_cols = embed_ref.shape
    up_rows, up_cols = up_ref.shape
    embed_part = embed_cols // share_count
    up_part = up_rows // share_count

    def share(which, owner, group, dom, own=False):
        part = group * dom_count + dom
        if which == 0:
            columns = pl.ds(pl.multiple_of(part * embed_part, LANES), embed_part)
            if own:
                return embed_ref.at[:, columns]
            return embed_full.at[
                pl.ds(pl.multiple_of(owner * embed_rows, 16), embed_rows), columns
            ]
        rows = pl.ds(pl.multiple_of(part * up_part, 16), up_part)
        if own:
            return up_ref.at[rows, :]
        return up_full.at[rows, pl.ds(pl.multiple_of(owner * up_cols, LANES), up_cols)]

    def shard_copy(which):
        if which == 0:
            target = embed_full.at[pl.ds(pl.multiple_of(me * embed_rows, 16), embed_rows), :]
            return pltpu.make_async_copy(embed_ref, target, shard_own.at[0])
        target = up_full.at[:, pl.ds(pl.multiple_of(me * up_cols, LANES), up_cols)]
        return pltpu.make_async_copy(up_ref, target, shard_own.at[1])

    place = lax.div(me, fan)
    lane = lax.rem(me, fan)
    length = n // fan
    signs = (1, -1)

    def line_copy(which, direction, step, incoming):
        sign = signs[direction]
        origin = place - sign * (step if incoming else step - 1)
        owner = lax.rem(origin + n, length) * fan + lane
        to = lax.rem(place + sign + n, length) * fan + lane
        return pltpu.make_async_remote_copy(
            src_ref=share(which, owner, my_group, my_dom, own=step == 1 and not incoming),
            dst_ref=share(which, owner, my_group, my_dom),
            send_sem=line_send.at[which, direction, step - 1],
            recv_sem=line_recv.at[which, direction, step - 1],
            device_id={"seq": to},
            device_id_type=MESH,
        )

    def receives(direction, step):
        return place >= step if direction == 0 else place + step < length

    def sends(direction, step):
        if direction == 0:
            return jnp.logical_and(place >= step - 1, place + 1 < length)
        return jnp.logical_and(place + step - 1 < length, place >= 1)

    def fan_copy(which, spot, shift, incoming, own=False):
        to = lax.rem(lane + shift, fan)
        source = lax.rem(lane - shift + fan, fan) if incoming else lane
        owner = spot * fan + source
        return pltpu.make_async_remote_copy(
            src_ref=share(which, owner, my_group, my_dom, own=own),
            dst_ref=share(which, owner, my_group, my_dom),
            send_sem=fan_send.at[which, shift, spot],
            recv_sem=fan_recv.at[which, shift, spot],
            device_id={"seq": place * fan + to},
            device_id_type=MESH,
        )

    def group_copy(which, owner, shift, incoming):
        other = lax.rem(my_group + shift, group_count)
        source = lax.rem(my_group - shift + group_count, group_count) if incoming else my_group
        return pltpu.make_async_remote_copy(
            src_ref=share(which, owner, source, my_dom),
            dst_ref=share(which, owner, source, my_dom),
            send_sem=group_send.at[which, shift, owner],
            recv_sem=group_recv.at[which, shift, owner],
            device_id={"groups": other},
            device_id_type=MESH,
        )

    def dom_copy(which, owner, shift, group_shift, incoming):
        other = lax.rem(my_dom + shift, dom_count)
        source = lax.rem(my_dom - shift + dom_count, dom_count) if incoming else my_dom
        group = lax.rem(my_group - group_shift + group_count, group_count)
        return pltpu.make_async_remote_copy(
            src_ref=share(which, owner, group, source),
            dst_ref=share(which, owner, group, source),
            send_sem=dom_send.at[which, shift, group_shift, owner],
            recv_sem=dom_recv.at[which, shift, group_shift, owner],
            device_id={"dom": other},
            device_id_type=MESH,
        )

    def spread(which, owner):
        for shift in range(1, group_count):
            group_copy(which, owner, shift, False).start()
        for shift in range(1, dom_count):
            dom_copy(which, owner, shift, 0, False).start()

    def each_arrival(step, action):
        for direction in range(2):

            @pl.when(receives(direction, step))
            def _(direction=direction):
                for which in range(2):
                    action(which, direction, place - signs[direction] * step)

    def line_start():
        for which in range(2):
            for direction in range(2):

                @pl.when(sends(direction, 1))
                def _(which=which, direction=direction):
                    line_copy(which, direction, 1, False).start()

            for shift in range(1, fan):
                fan_copy(which, place, shift, False, own=True).start()
            shard_copy(which).start()

    def line_step(step):
        def action(which, direction, spot):
            line_copy(which, direction, step, True).wait_recv()
            if step + 1 < length:

                @pl.when(sends(direction, step + 1))
                def _():
                    line_copy(which, direction, step + 1, False).start()

            for shift in range(1, fan):
                fan_copy(which, spot, shift, False).start()
            spread(which, spot * fan + lane)

        each_arrival(step, action)

    def fan_step(step):
        def action(which, direction, spot):
            for shift in range(1, fan):
                fan_copy(which, spot, shift, True).wait_recv()
                spread(which, spot * fan + lax.rem(lane - shift + fan, fan))

        if step == 0:
            for which in range(2):
                action(which, 0, place)
        else:
            each_arrival(step, action)

    def group_block(which, owner):
        for group_shift in range(1, group_count):
            group_copy(which, owner, group_shift, True).wait_recv()
            for shift in range(1, dom_count):
                dom_copy(which, owner, shift, group_shift, False).start()

    def group_step(step):
        def action(which, direction, spot):
            if step > 0:
                group_block(which, spot * fan + lane)
            for shift in range(1, fan):
                group_block(which, spot * fan + lax.rem(lane - shift + fan, fan))

        if step == 0:
            for which in range(2):
                action(which, 0, place)
        else:
            each_arrival(step, action)

    def move_step(step):
        if 1 <= step < length:
            line_step(step)
        if 0 <= step - 1 < length:
            fan_step(step - 1)


    def finish_weights(parts=(0, 1)):
        for which in parts:
            shard_copy(which).wait()
            for direction in range(2):
                for step in range(1, length):

                    @pl.when(sends(direction, step))
                    def _(which=which, direction=direction, step=step):
                        line_copy(which, direction, step, False).wait_send()

            @pl.loop(0, length)
            def _(spot, which=which):
                for shift in range(1, fan):
                    fan_copy(which, spot, shift, False).wait_send()

            @pl.loop(1, n)
            def _(step, which=which):
                owner = lax.rem(me + step, n)
                for shift in range(1, group_count):
                    group_copy(which, owner, shift, False).wait_send()
                for shift in range(1, dom_count):
                    for group_shift in range(group_count):
                        dom_copy(which, owner, shift, group_shift, True).wait_recv()
                        dom_copy(which, owner, shift, group_shift, False).wait_send()

    return line_start, move_step, group_step, finish_weights, length


def take(semaphore, region):
    pltpu.make_async_copy(region, region, semaphore).wait()


def shared_weight_exchange(
    n, fan, group_count, dom_count, embed_ref, up_ref, embed_full, up_full,
    shard_own, line_send, line_recv, fan_send, fan_recv, group_send, group_recv, dom_send, dom_recv,
):
    me = lax.axis_index("seq")
    my_group = lax.axis_index("groups")
    my_dom = lax.axis_index("dom")
    share_count = group_count * dom_count
    embed_rows, embed_cols = embed_ref.shape
    up_rows, up_cols = up_ref.shape
    embed_part = embed_cols // share_count
    up_part = up_rows // share_count

    def share(which, owner, group, dom, own=False):
        part = group * dom_count + dom
        if which == 0:
            columns = pl.ds(pl.multiple_of(part * embed_part, LANES), embed_part)
            if own:
                return embed_ref.at[:, columns]
            return embed_full.at[
                pl.ds(pl.multiple_of(owner * embed_rows, 16), embed_rows), columns
            ]
        rows = pl.ds(pl.multiple_of(part * up_part, 16), up_part)
        if own:
            return up_ref.at[rows, :]
        return up_full.at[rows, pl.ds(pl.multiple_of(owner * up_cols, LANES), up_cols)]

    def shard_copy(which):
        if which == 0:
            target = embed_full.at[pl.ds(pl.multiple_of(me * embed_rows, 16), embed_rows), :]
            return pltpu.make_async_copy(embed_ref, target, shard_own.at[0])
        target = up_full.at[:, pl.ds(pl.multiple_of(me * up_cols, LANES), up_cols)]
        return pltpu.make_async_copy(up_ref, target, shard_own.at[1])

    place = lax.div(me, fan)
    lane = lax.rem(me, fan)
    length = n // fan
    signs = (1, -1)

    def line_copy(which, direction, step, incoming):
        sign = signs[direction]
        origin = place - sign * (step if incoming else step - 1)
        owner = lax.rem(origin + n, length) * fan + lane
        to = lax.rem(place + sign + n, length) * fan + lane
        return pltpu.make_async_remote_copy(
            src_ref=share(which, owner, my_group, my_dom, own=step == 1 and not incoming),
            dst_ref=share(which, owner, my_group, my_dom),
            send_sem=line_send.at[which, direction, step - 1],
            recv_sem=line_recv.at[which, direction, step - 1],
            device_id={"seq": to},
            device_id_type=MESH,
        )

    def receives(direction, step):
        return place >= step if direction == 0 else place + step < length

    def sends(direction, step):
        if direction == 0:
            return jnp.logical_and(place >= step - 1, place + 1 < length)
        return jnp.logical_and(place + step - 1 < length, place >= 1)

    def fan_copy(which, spot, shift, incoming, own=False):
        to = lax.rem(lane + shift, fan)
        source = lax.rem(lane - shift + fan, fan) if incoming else lane
        owner = spot * fan + source
        return pltpu.make_async_remote_copy(
            src_ref=share(which, owner, my_group, my_dom, own=own),
            dst_ref=share(which, owner, my_group, my_dom),
            send_sem=fan_send.at[which, shift - 1],
            recv_sem=fan_recv.at[which, shift - 1, spot],
            device_id={"seq": place * fan + to},
            device_id_type=MESH,
        )

    def group_copy(which, owner, shift, incoming):
        other = lax.rem(my_group + shift, group_count)
        source = lax.rem(my_group - shift + group_count, group_count) if incoming else my_group
        return pltpu.make_async_remote_copy(
            src_ref=share(which, owner, source, my_dom),
            dst_ref=share(which, owner, source, my_dom),
            send_sem=group_send.at[which, shift - 1],
            recv_sem=group_recv.at[which, shift - 1, owner],
            device_id={"groups": other},
            device_id_type=MESH,
        )

    def dom_copy(which, owner, shift, group_shift, incoming):
        other = lax.rem(my_dom + shift, dom_count)
        source = lax.rem(my_dom - shift + dom_count, dom_count) if incoming else my_dom
        group = lax.rem(my_group - group_shift + group_count, group_count)
        return pltpu.make_async_remote_copy(
            src_ref=share(which, owner, group, source),
            dst_ref=share(which, owner, group, source),
            send_sem=dom_send.at[which, shift - 1],
            recv_sem=dom_recv.at[which, shift - 1],
            device_id={"dom": other},
            device_id_type=MESH,
        )

    def spread(which, owner):
        for shift in range(1, group_count):
            group_copy(which, owner, shift, False).start()
        for shift in range(1, dom_count):
            dom_copy(which, owner, shift, 0, False).start()

    def each_arrival(step, action):
        for direction in range(2):

            @pl.when(receives(direction, step))
            def _(direction=direction):
                for which in range(2):
                    action(which, direction, place - signs[direction] * step)

    def line_start():
        for which in range(2):
            for direction in range(2):

                @pl.when(sends(direction, 1))
                def _(which=which, direction=direction):
                    line_copy(which, direction, 1, False).start()

            for shift in range(1, fan):
                fan_copy(which, place, shift, False, own=True).start()
            shard_copy(which).start()

    def line_step(step):
        def action(which, direction, spot):
            line_copy(which, direction, step, True).wait_recv()
            if step + 1 < length:

                @pl.when(sends(direction, step + 1))
                def _():
                    line_copy(which, direction, step + 1, False).start()

            for shift in range(1, fan):
                fan_copy(which, spot, shift, False).start()
            spread(which, spot * fan + lane)

        each_arrival(step, action)

    def fan_step(step):
        def action(which, direction, spot):
            for shift in range(1, fan):
                fan_copy(which, spot, shift, True).wait_recv()
                spread(which, spot * fan + lax.rem(lane - shift + fan, fan))

        if step == 0:
            for which in range(2):
                action(which, 0, place)
        else:
            each_arrival(step, action)

    def group_block(which, owner):
        for group_shift in range(1, group_count):
            group_copy(which, owner, group_shift, True).wait_recv()
            for shift in range(1, dom_count):
                dom_copy(which, owner, shift, group_shift, False).start()

    def group_step(step):
        def action(which, direction, spot):
            if step > 0:
                group_block(which, spot * fan + lane)
            for shift in range(1, fan):
                group_block(which, spot * fan + lax.rem(lane - shift + fan, fan))

        if step == 0:
            for which in range(2):
                action(which, 0, place)
        else:
            each_arrival(step, action)

    def parts_of(which, amount):
        if which == 0:
            wide = math.gcd(amount, share_count)
            return embed_full.at[0 : amount // wide * embed_rows, 0 : wide * embed_part]
        wide = math.gcd(amount, share_count)
        return up_full.at[0 : wide * up_part, 0 : amount // wide * up_cols]

    def finish_weights(parts=(0, 1)):
        for which in parts:
            shard_copy(which).wait()
            for direction in range(2):
                for step in range(1, length):

                    @pl.when(sends(direction, step))
                    def _(which=which, direction=direction, step=step):
                        line_copy(which, direction, step, False).wait_send()

            for shift in range(1, fan):
                take(fan_send.at[which, shift - 1], parts_of(which, length))
            for shift in range(1, group_count):
                take(group_send.at[which, shift - 1], parts_of(which, n - 1))
            for shift in range(1, dom_count):
                take(dom_recv.at[which, shift - 1], parts_of(which, (n - 1) * group_count))
                take(dom_send.at[which, shift - 1], parts_of(which, (n - 1) * group_count))

    return line_start, line_step, fan_step, group_step, finish_weights, length


def attention_kernel(
    n, fan, group_count, dom_count, groups, cols, width, head_width, row_block,
    q_ref, k_ref, v_ref, embed_ref, up_ref, o_ref, embed_full, up_full,
    qb, kb, vb, ob, send_sem, recv_sem, own_sem, back_send, back_recv, back_own,
    shard_own, line_send, line_recv, fan_send, fan_recv, group_send, group_recv, dom_send, dom_recv,
):
    me = lax.axis_index("seq")
    my_group = lax.axis_index("groups")
    my_dom = lax.axis_index("dom")
    tokens = q_ref.shape[1]
    total_tokens = n * tokens
    chunks = cols // width
    inputs = ((q_ref, qb), (k_ref, kb), (v_ref, vb))

    barrier = pltpu.get_barrier_semaphore()

    @pl.loop(1, n)
    def _(step):
        pl.semaphore_signal(
            barrier, inc=1, device_id={"seq": lax.rem(me + step, n)}, device_id_type=MESH
        )

    for step in range(1, group_count):
        peer = {"groups": lax.rem(my_group + step, group_count)}
        pl.semaphore_signal(barrier, inc=1, device_id=peer, device_id_type=MESH)
    for step in range(1, dom_count):
        peer = {"dom": lax.rem(my_dom + step, dom_count)}
        pl.semaphore_signal(barrier, inc=1, device_id=peer, device_id_type=MESH)
    pl.semaphore_wait(barrier, n - 1 + group_count - 1 + dom_count - 1)

    line_start, move_step, group_step, finish_weights, length = weight_exchange(
        n, fan, group_count, dom_count, embed_ref, up_ref, embed_full, up_full,
        shard_own, line_send, line_recv, fan_send, fan_recv, group_send, group_recv,
        dom_send, dom_recv,
    )

    def rows_of(ref, owner, chunk):
        row = pl.ds(pl.multiple_of(owner * tokens, 16), tokens)
        return ref.at[row, pl.ds(chunk * width, width)]

    def outgoing(index, chunk, target, slot):
        source, buffer = inputs[index]
        return pltpu.make_async_remote_copy(
            src_ref=piece(source, target, groups, cols, chunk * width, width),
            dst_ref=rows_of(buffer, me, chunk),
            send_sem=send_sem.at[index, chunk, target],
            recv_sem=recv_sem.at[index, chunk, slot],
            device_id={"seq": target},
            device_id_type=MESH,
        )

    def own_copy(index, chunk):
        source, buffer = inputs[index]
        return pltpu.make_async_copy(
            piece(source, me, groups, cols, chunk * width, width),
            rows_of(buffer, me, chunk),
            own_sem.at[index, chunk],
        )

    def returned(chunk, target, slot):
        return pltpu.make_async_remote_copy(
            src_ref=rows_of(ob, target, chunk),
            dst_ref=piece(o_ref, me, groups, cols, chunk * width, width),
            send_sem=back_send.at[chunk, target],
            recv_sem=back_recv.at[chunk, slot],
            device_id={"seq": target},
            device_id_type=MESH,
        )

    def own_return(chunk):
        return pltpu.make_async_copy(
            rows_of(ob, me, chunk),
            piece(o_ref, me, groups, cols, chunk * width, width),
            back_own.at[chunk],
        )

    weight_steps = length + 2

    def weight_step(step):
        move_step(step)
        if 0 <= step - 2 < length:
            group_step(step - 2)

    ready = 1
    for chunk in range(chunks):
        if chunk == 0:
            line_start()
        elif ready < weight_steps:
            weight_step(ready)
            ready += 1
        for index in range(3):
            own_copy(index, chunk).start()

            @pl.loop(1, n)
            def _(step, index=index, chunk=chunk):
                outgoing(index, chunk, lax.rem(me + step, n), me).start()

    paired = 2 * head_width == LANES and width % LANES == 0
    unit = LANES if paired else head_width
    blocks = total_tokens // row_block

    for chunk in range(chunks):
        for index in range(3):
            own_copy(index, chunk).wait()

            @pl.loop(1, n)
            def _(step, index=index, chunk=chunk):
                other = lax.rem(me + step, n)
                outgoing(index, chunk, other, other).wait_recv()

        if paired:

            @pl.loop(0, (width // unit) * blocks)
            def _(step, chunk=chunk):
                attend_pair(
                    qb, kb, vb, ob,
                    pl.multiple_of((step % blocks) * row_block, row_block), row_block,
                    chunk * width + (step // blocks) * unit, head_width,
                )
        else:
            for head in range(width // unit):

                @pl.loop(0, blocks)
                def _(step, head=head, chunk=chunk):
                    attend_plain(
                        qb, kb, vb, ob,
                        pl.multiple_of(step * row_block, row_block), row_block,
                        chunk * width + head * unit, head_width,
                    )

        own_return(chunk).start()

        @pl.loop(1, n)
        def _(step, chunk=chunk):
            returned(chunk, lax.rem(me + step, n), me).start()

        if ready < weight_steps and chunk < chunks - 1:
            weight_step(ready)
            ready += 1

    for step in range(ready, weight_steps):
        weight_step(step)
    finish_weights()

    for chunk in range(chunks):
        own_return(chunk).wait()
        for index in range(3):

            @pl.loop(1, n)
            def _(step, index=index, chunk=chunk):
                outgoing(index, chunk, lax.rem(me + step, n), me).wait_send()

        @pl.loop(1, n)
        def _(step, chunk=chunk):
            other = lax.rem(me + step, n)
            returned(chunk, other, other).wait_recv()
            returned(chunk, other, me).wait_send()


def attention(queries, keys, values, embed_weight, up_weight):
    n = lax.axis_size("seq")
    group_count = lax.axis_size("groups")
    dom_count = lax.axis_size("dom")
    fan = 2 if n % 2 == 0 else 1
    particles, tokens, model_width = queries.shape
    head_width = model_width // HEADS
    per_device = particles * HEADS // n
    cols = per_device * head_width
    aligned = model_width % cols == 0 and cols % LANES == 0
    groups = model_width // cols if aligned else 0
    width = 2 * LANES if aligned and cols % (2 * LANES) == 0 else cols
    chunks = cols // width
    total_tokens = n * tokens

    def to_items(array):
        if aligned:
            return array
        split = array.reshape(particles, tokens, HEADS, head_width).transpose(0, 2, 1, 3)
        split = split.reshape(n, per_device, tokens, head_width).transpose(0, 2, 1, 3)
        return split.reshape(n, tokens, cols)

    operands = tuple(to_items(a) for a in (queries, keys, values))
    any_spec = pl.BlockSpec(memory_space=pl.ANY)
    embed_shape = (n * embed_weight.shape[0], embed_weight.shape[1])
    up_shape = (up_weight.shape[0], n * up_weight.shape[1])
    out, embed_full, up_full = pl.pallas_call(
        functools.partial(
            attention_kernel, n, fan, group_count, dom_count, groups, cols, width, head_width,
            min(256, total_tokens),
        ),
        out_shape=(
            jax.ShapeDtypeStruct(operands[0].shape, jnp.bfloat16),
            jax.ShapeDtypeStruct(embed_shape, jnp.bfloat16),
            jax.ShapeDtypeStruct(up_shape, jnp.bfloat16),
        ),
        in_specs=[any_spec] * 5,
        out_specs=(any_spec,) * 3,
        scratch_shapes=[pltpu.VMEM((total_tokens, cols), jnp.bfloat16)] * 4
        + [
            pltpu.SemaphoreType.DMA((3, chunks, n)),
            pltpu.SemaphoreType.DMA((3, chunks, n)),
            pltpu.SemaphoreType.DMA((3, chunks)),
            pltpu.SemaphoreType.DMA((chunks, n)),
            pltpu.SemaphoreType.DMA((chunks, n)),
            pltpu.SemaphoreType.DMA((chunks,)),
            pltpu.SemaphoreType.DMA((2,)),
            pltpu.SemaphoreType.DMA((2, 2, n // fan)),
            pltpu.SemaphoreType.DMA((2, 2, n // fan)),
            pltpu.SemaphoreType.DMA((2, fan, n // fan)),
            pltpu.SemaphoreType.DMA((2, fan, n // fan)),
            pltpu.SemaphoreType.DMA((2, group_count, n)),
            pltpu.SemaphoreType.DMA((2, group_count, n)),
            pltpu.SemaphoreType.DMA((2, dom_count, group_count, n)),
            pltpu.SemaphoreType.DMA((2, dom_count, group_count, n)),
        ],
        compiler_params=pltpu.CompilerParams(
            collective_id=0, has_side_effects=True, vmem_limit_bytes=60 * 1024 * 1024
        ),
        name="attention",
    )(*operands, embed_weight, up_weight)
    if not aligned:
        out = out.reshape(n, tokens, per_device, head_width).transpose(0, 2, 1, 3)
        out = out.reshape(particles, HEADS, tokens, head_width).transpose(0, 2, 1, 3)
    return out.reshape(particles * tokens, model_width), embed_full, up_full


def reward_kernel(n, doms, particles, x_ref, o_ref, held, send_sem, recv_sem):
    me = lax.axis_index("dom") * n + lax.axis_index("seq")
    members = n * doms

    def target(step):
        other = lax.rem(me + step, members)
        return other, {"dom": other // n, "seq": other % n}

    def copy(step, slot):
        other, device = target(step)
        return pltpu.make_async_remote_copy(
            src_ref=x_ref,
            dst_ref=held.at[me],
            send_sem=send_sem.at[other],
            recv_sem=recv_sem.at[slot],
            device_id=device,
            device_id_type=MESH,
        )

    barrier = pltpu.get_barrier_semaphore()

    @pl.loop(1, members)
    def _(step):
        _, device = target(step)
        pl.semaphore_signal(barrier, inc=1, device_id=device, device_id_type=MESH)

    pl.semaphore_wait(barrier, members - 1)

    @pl.loop(1, members)
    def _(step):
        copy(step, me).start()

    held[me] = x_ref[...]

    @pl.loop(1, members)
    def _(step):
        copy(step, lax.rem(me + step, members)).wait_recv()

    logits = []
    for dom in range(doms):
        rewards = jnp.sum(held[dom * n : (dom + 1) * n], axis=0)[:1]
        value = held[dom * n][1:2] + potential_scale * rewards
        used = lax.broadcasted_iota(jnp.int32, value.shape, 1) < particles
        logits.append(jnp.where(used, value, -jnp.inf))
    highest = functools.reduce(jnp.maximum, [jnp.max(v, axis=1, keepdims=True) for v in logits])
    total = sum(jnp.sum(jnp.exp(v - highest), axis=1, keepdims=True) for v in logits)
    own = logits[0]
    for dom in range(1, doms):
        own = jnp.where(lax.axis_index("dom") == dom, logits[dom], own)
    o_ref[...] = jnp.broadcast_to(own - (highest + jnp.log(total)), o_ref.shape)

    @pl.loop(1, members)
    def _(step):
        copy(step, me).wait_send()


def weigh(partial_value, prev_logw, n, doms):
    particles = partial_value.shape[0]
    rows = jnp.stack([partial_value, prev_logw])
    padded = jnp.pad(rows, ((0, 8 - 2), (0, LANES - particles)))
    vmem = pl.BlockSpec(memory_space=pltpu.VMEM)
    out = pl.pallas_call(
        functools.partial(reward_kernel, n, doms, particles),
        out_shape=jax.ShapeDtypeStruct((8, LANES), jnp.float32),
        in_specs=[vmem],
        out_specs=vmem,
        scratch_shapes=[
            pltpu.VMEM((n * doms, 8, LANES), jnp.float32),
            pltpu.SemaphoreType.DMA((n * doms,)),
            pltpu.SemaphoreType.DMA((n * doms,)),
        ],
        compiler_params=pltpu.CompilerParams(collective_id=1, has_side_effects=True),
        name="rewards",
    )(padded)
    return out[0, :particles]


def part_sum(block, rows):
    parts = [
        jnp.sum(block[at : at + rows], axis=0, keepdims=True)
        for at in range(0, block.shape[0], rows)
    ]
    return jnp.concatenate(parts, axis=0)


def fused_kernel(
    n, fan, group_count, dom_count, rounds, groups, chunks, head_width, row_block, tile,
    q_ref, k_ref, v_ref, lat_ref, wo_ref, step_in, embed_ref, gain_in, up_ref, head_in,
    prev_in, anc_in, out_ref, logw_ref,
    step_ref, gain_ref, head_ref, prev_ref, anc_ref, picked,
    qb, kb, vb, ob, mixed, embed_full, up_full, wo, lat, velocity, clean, embedded, features,
    cand, score, mine, held,
    send_sem, recv_sem, back_send, back_recv,
    shard_own, line_send, line_recv, fan_send, fan_recv, group_send, group_recv, dom_send, dom_recv,
    load_sem, step_send, step_recv, score_send, score_recv,
):
    me = lax.axis_index("seq")
    my_group = lax.axis_index("groups")
    my_dom = lax.axis_index("dom")
    particles, tokens, model_width = q_ref.shape
    rows = particles * tokens
    share = particles // rounds
    share_rows = share * tokens
    total_tokens = n * tokens
    inputs = ((q_ref, qb), (k_ref, kb), (v_ref, vb))
    members = n * dom_count
    member = my_dom * n + me

    def other_member(step):
        other = lax.rem(member + step, members)
        return other, {"dom": other // n, "seq": other % n}

    small = (
        (wo_ref, wo), (lat_ref, lat), (step_in, step_ref), (gain_in, gain_ref),
        (head_in, head_ref), (prev_in, prev_ref), (anc_in, anc_ref),
    )
    loads = [
        pltpu.make_async_copy(source, target, load_sem.at[at])
        for at, (source, target) in enumerate(small)
    ]

    barrier = pltpu.get_barrier_semaphore()

    @pl.loop(1, members)
    def _(step):
        _, device = other_member(step)
        pl.semaphore_signal(barrier, inc=1, device_id=device, device_id_type=MESH)

    for step in range(1, group_count):
        peer = {"groups": lax.rem(my_group + step, group_count)}
        pl.semaphore_signal(barrier, inc=1, device_id=peer, device_id_type=MESH)
    for load in loads:
        load.start()
    pl.semaphore_wait(barrier, members - 1 + group_count - 1)

    line_start, line_step, fan_step, group_step, finish_weights, length = shared_weight_exchange(
        n, fan, group_count, dom_count, embed_ref, up_ref, embed_full, up_full,
        shard_own, line_send, line_recv, fan_send, fan_recv, group_send, group_recv,
        dom_send, dom_recv,
    )

    cols = model_width // groups

    def source_of(ref, item, chunk):
        turn, start, width = chunks[chunk]
        offset = pl.multiple_of(groups * start + (item % groups) * width, LANES)
        return ref.at[turn * share + item // groups, :, pl.ds(offset, width)]

    def mixed_of(item, chunk):
        turn, start, width = chunks[chunk]
        offset = pl.multiple_of(groups * start + (item % groups) * width, LANES)
        row = pl.multiple_of((turn * share + item // groups) * tokens, 16)
        return mixed.at[pl.ds(row, tokens), pl.ds(offset, width)]

    def rows_of(ref, owner, chunk):
        turn, start, width = chunks[chunk]
        row = pl.ds(pl.multiple_of(owner * tokens, 16), tokens)
        return ref.at[row, pl.ds(turn * cols + start, width)]

    def outgoing(index, chunk, target):
        source, buffer = inputs[index]
        return pltpu.make_async_remote_copy(
            src_ref=source_of(source, target, chunk),
            dst_ref=rows_of(buffer, me, chunk),
            send_sem=send_sem.at[index, chunk],
            recv_sem=recv_sem.at[index, chunk],
            device_id={"seq": target},
            device_id_type=MESH,
        )

    def own_copy(index, chunk):
        source, buffer = inputs[index]
        return pltpu.make_async_copy(
            source_of(source, me, chunk), rows_of(buffer, me, chunk), recv_sem.at[index, chunk]
        )

    def returned(chunk, target):
        return pltpu.make_async_remote_copy(
            src_ref=rows_of(ob, target, chunk),
            dst_ref=mixed_of(me, chunk),
            send_sem=back_send.at[chunk],
            recv_sem=back_recv.at[chunk],
            device_id={"seq": target},
            device_id_type=MESH,
        )

    def own_return(chunk):
        return pltpu.make_async_copy(
            rows_of(ob, me, chunk), mixed_of(me, chunk), back_recv.at[chunk]
        )

    count = len(chunks)
    blocks = total_tokens // row_block
    owners = row_block // tokens

    def issue(chunk):
        for index in range(3):
            own_copy(index, chunk).start()

            @pl.loop(1, n)
            def _(step, index=index):
                outgoing(index, chunk, lax.rem(me + step, n)).start()

    def attend(chunk):
        turn, start, width = chunks[chunk]
        first = turn * cols + start
        for at in range(1, blocks + 1):
            block = lax.rem(lax.div(me, owners) + at, blocks)
            row = pl.multiple_of(block * row_block, row_block)

            @pl.loop(0, width // LANES)
            def _(unit, row=row):
                attend_pair(
                    qb, kb, vb, ob, row, row_block, first + unit * LANES, head_width
                )

            @pl.loop(0 if at < blocks else 1, owners)
            def _(step, block=block):
                target = block * owners + lax.rem(me + step, owners)
                returned(chunk, target).start()

        own_return(chunk).start()

    def arrive(chunk):
        turn, start, width = chunks[chunk]
        for index in range(3):
            buffer = inputs[index][1]
            first = turn * cols + start
            take(recv_sem.at[index, chunk], buffer.at[:, first : first + width])

    def project(chunk):
        if chunk == 0:
            for load in loads:
                load.wait()
        sigma = step_ref[0].astype(jnp.float32) / STEPS
        turn, start, width = chunks[chunk]
        inner = pl.ds(groups * start, groups * width)
        own_rows = pl.ds(turn * share_rows, share_rows)
        final = chunk + 1 == count or chunks[chunk + 1][0] != turn
        take(back_recv.at[chunk], mixed.at[own_rows, inner])

        @pl.loop(0, model_width // tile, unroll=model_width // tile)
        def _(step):
            columns = pl.ds(pl.multiple_of(step * tile, tile), tile)
            part = jnp.dot(
                mixed[own_rows, inner], wo[inner, columns], preferred_element_type=jnp.float32
            )
            if start > 0:
                part = velocity[own_rows, columns] + part
            if not final:
                velocity[own_rows, columns] = part
                return
            for item in range(share):
                at = slice(item * tokens, (item + 1) * tokens)
                spot = turn * share + item
                flat = lat[spot, :, columns].astype(jnp.float32)
                moved = flat + part[at]
                clean[spot * tokens : (spot + 1) * tokens, columns] = (
                    flat - sigma * moved
                ).astype(jnp.bfloat16)
                cand[my_dom * particles + spot, :, columns] = (flat - moved / STEPS).astype(
                    jnp.bfloat16
                )

    def step_copy(turn, shift, incoming):
        source = lax.rem(my_dom - shift + dom_count, dom_count) if incoming else my_dom
        block = cand.at[pl.ds(source * particles + turn * share, share)]
        return pltpu.make_async_remote_copy(
            src_ref=block,
            dst_ref=block,
            send_sem=step_send.at[turn, shift - 1],
            recv_sem=step_recv.at[turn, shift - 1],
            device_id={"dom": lax.rem(my_dom + shift, dom_count)},
            device_id_type=MESH,
        )

    def embed(turn):
        if turn == 0:
            finish_weights((0,))
        own_rows = pl.ds(turn * share_rows, share_rows)

        @pl.loop(0, embedded.shape[1] // tile, unroll=embedded.shape[1] // tile)
        def _(step):
            columns = pl.ds(pl.multiple_of(step * tile, tile), tile)
            embedded[own_rows, columns] = jnp.dot(
                clean[own_rows, :], embed_full[:, columns], preferred_element_type=jnp.float32
            )

        for shift in range(1, dom_count):
            step_copy(turn, shift, False).start()

        @pl.loop(turn * share, (turn + 1) * share, unroll=share)
        def _(item):
            item_rows = pl.ds(pl.multiple_of(item * tokens, tokens), tokens)
            block = embedded[item_rows, :]
            centered = block - jnp.mean(block, axis=1, keepdims=True)
            variance = jnp.mean(centered * centered, axis=1, keepdims=True)
            normed = centered * lax.rsqrt(variance + norm_eps) * gain_ref[...]
            features[item_rows, :] = jax.nn.gelu(normed).astype(jnp.bfloat16)

    def judge(turn):
        if turn == 0:
            finish_weights((1,))
        own_rows = pl.ds(turn * share_rows, share_rows)

        @pl.loop(0, up_full.shape[1] // tile, unroll=min(8, up_full.shape[1] // tile))
        def _(step):
            columns = pl.ds(pl.multiple_of(step * tile, tile), tile)
            hidden = jnp.dot(
                features[own_rows, :], up_full[:, columns], preferred_element_type=jnp.float32
            )
            score[turn * share : (turn + 1) * share, :] += (
                part_sum(jax.nn.gelu(hidden), tokens) * head_ref[:, columns]
            )

    actions = {
        "issue": issue, "arrive": arrive, "attend": attend,
        "line": line_step, "fan": fan_step, "group": group_step, "start": lambda _: line_start(),
        "project": project, "embed": embed, "judge": judge,
    }
    score[...] = jnp.zeros_like(score)
    for name, at in plan(chunks, length):
        actions[name](at)

    partial_value = jnp.sum(score[...], axis=1, keepdims=True) / math.sqrt(total_tokens)
    lane = lax.broadcasted_iota(jnp.int32, (particles, LANES), 1)
    row = lax.broadcasted_iota(jnp.int32, (particles, LANES), 0)
    before = jnp.zeros((particles, LANES), jnp.float32)
    for item in range(particles):
        before = jnp.where(row == item, prev_ref[item], before)
    half = LANES // 2
    own_block = jnp.where(lane < half, partial_value, before)
    mine[0:particles, :] = own_block
    held[member, 0:particles, :] = own_block

    def score_copy(step):
        _, device = other_member(step)
        return pltpu.make_async_remote_copy(
            src_ref=mine,
            dst_ref=held.at[member],
            send_sem=score_send.at[0],
            recv_sem=score_recv.at[0],
            device_id=device,
            device_id_type=MESH,
        )

    @pl.loop(1, members)
    def _(step):
        score_copy(step).start()

    for turn in range(rounds):
        for shift in range(1, dom_count):
            step_copy(turn, shift, True).wait_recv()
    for item in range(particles):
        picked[item] = cand[anc_ref[item]]
    write = pltpu.make_async_copy(picked, out_ref, load_sem.at[0])
    write.start()

    for chunk in range(count):
        sent = qb.at[0 : (n - 1) * tokens, 0 : chunks[chunk][2]]
        for index in range(3):
            take(send_sem.at[index, chunk], sent)
        take(back_send.at[chunk], sent)

    for turn in range(rounds):
        for shift in range(1, dom_count):
            step_copy(turn, shift, False).wait_send()

    take(score_recv.at[0], held.at[0 : members - 1])

    logits = []
    for dom in range(dom_count):
        reward = jnp.sum(held[dom * n : (dom + 1) * n, 0:particles, :], axis=0)[:, 0:1]
        logits.append(held[dom * n, 0:particles, :][:, half : half + 1] + potential_scale * reward)
    highest = functools.reduce(
        jnp.maximum, [jnp.max(value, axis=0, keepdims=True) for value in logits]
    )
    total = sum(jnp.sum(jnp.exp(value - highest), axis=0, keepdims=True) for value in logits)
    own = logits[0]
    for dom in range(1, dom_count):
        own = jnp.where(my_dom == dom, logits[dom], own)
    result = jnp.broadcast_to(own - (highest + jnp.log(total)), (particles, LANES))
    result = jnp.sum(jnp.where(row == lane, result, 0.0), axis=0, keepdims=True)
    logw_ref[...] = result[:, 0:particles]

    take(score_send.at[0], held.at[0 : members - 1])
    write.wait()


def plan(chunks, length):
    count = len(chunks)
    last = chunks[-1][0]
    early = [chunk for chunk in range(count) if chunks[chunk][0] < last]
    late = [chunk for chunk in range(count) if chunks[chunk][0] == last]
    lines = list(range(2, length))
    fans = list(range(1, length))
    steps = [("start", 0), ("issue", 0), ("line", 1), ("fan", 0)]
    if length == 1:
        steps = [("start", 0), ("issue", 0), ("fan", 0)]
    steps += [("issue", chunk) for chunk in range(1, min(2, count))]
    for chunk in range(count):
        if chunk == count - 1:
            steps += [("line", step) for step in lines] + [("fan", step) for step in fans]
            steps += [("group", step) for step in range(length)]
            steps += [("project", part) for part in early]
        elif chunk == 0:
            steps += [("line", step) for step in lines[:1]] + [("fan", step) for step in fans[:1]]
            lines, fans = lines[1:], fans[1:]
        steps += [("arrive", chunk), ("attend", chunk)]
        if chunk + 2 < count:
            steps.append(("issue", chunk + 2))
        if chunk < count - 1:
            steps += [("line", step) for step in lines[:1]] + [("fan", step) for step in fans[:1]]
            lines, fans = lines[1:], fans[1:]
    for turn in range(last):
        steps += [("embed", turn), ("judge", turn)]
    return steps + [("project", part) for part in late] + [("embed", last), ("judge", last)]


def chunk_list(rounds, cols):
    chunks = []
    for turn in range(rounds):
        widths = [2 * LANES] * (cols // (2 * LANES)) + [LANES] * (cols % (2 * LANES) // LANES)
        if turn == 0:
            widths.reverse()
        start = 0
        for width in widths:
            chunks.append((turn, start, width))
            start += width
    return tuple(chunks)


def in_place(array):
    return pltpu.with_memory_space_constraint(array, pltpu.HBM)


def fused(
    latents, queries, keys, values, out_weight, step_index, embed_weight, norm_gain, up_weight,
    head_weight, prev_logw, ancestors,
):
    n = lax.axis_size("seq")
    group_count = lax.axis_size("groups")
    dom_count = lax.axis_size("dom")
    fan = 2 if n % 2 == 0 else 1
    particles, tokens, model_width = queries.shape
    head_width = model_width // HEADS
    rounds = round_count(n, particles, model_width)
    cols = particles * model_width // (n * rounds)
    groups = model_width // cols
    chunks = chunk_list(rounds, cols)
    count = len(chunks)
    rows = particles * tokens
    total_tokens = n * tokens
    members = n * dom_count
    fan_steps, group_steps, dom_steps = (max(x - 1, 1) for x in (fan, group_count, dom_count))
    tile = 512
    embed_shape = (n * embed_weight.shape[0], embed_weight.shape[1])
    up_shape = (up_weight.shape[0], n * up_weight.shape[1])
    hbm = pl.BlockSpec(memory_space=pl.ANY)
    vmem = pl.BlockSpec(memory_space=pltpu.VMEM)
    bf16 = jnp.bfloat16
    dma = pltpu.SemaphoreType.DMA
    resampled, logw = pl.pallas_call(
        functools.partial(
            fused_kernel, n, fan, group_count, dom_count, rounds, groups, chunks, head_width,
            min(256, total_tokens), tile,
        ),
        out_shape=(
            jax.ShapeDtypeStruct(latents.shape, bf16),
            jax.ShapeDtypeStruct((1, particles), jnp.float32),
        ),
        in_specs=[hbm] * 12,
        out_specs=(hbm, vmem),
        scratch_shapes=[
            pltpu.SMEM(step_index.shape, jnp.int32),
            pltpu.VMEM((1, norm_gain.shape[0]), jnp.float32),
            pltpu.VMEM((1, head_weight.shape[0]), jnp.float32),
            pltpu.SMEM(prev_logw.shape, jnp.float32),
            pltpu.SMEM(ancestors.shape, jnp.int32),
            pltpu.VMEM(latents.shape, bf16),
        ]
        + [pltpu.VMEM((total_tokens, rounds * cols), bf16)] * 4
        + [
            pltpu.VMEM((rows, model_width), bf16),
            pltpu.VMEM(embed_shape, bf16),
            pltpu.VMEM(up_shape, bf16),
            pltpu.VMEM(out_weight.shape, bf16),
            pltpu.VMEM(latents.shape, bf16),
            pltpu.VMEM((rows, model_width), jnp.float32),
            pltpu.VMEM((rows, model_width), bf16),
            pltpu.VMEM((rows, embed_shape[1]), jnp.float32),
            pltpu.VMEM((rows, embed_shape[1]), bf16),
            pltpu.VMEM((dom_count * particles, tokens, model_width), bf16),
            pltpu.VMEM((particles, tile), jnp.float32),
            pltpu.VMEM((8, LANES), jnp.float32),
            pltpu.VMEM((members, 8, LANES), jnp.float32),
            dma((3, count)),
            dma((3, count)),
            dma((count,)),
            dma((count,)),
            dma((2,)),
            dma((2, 2, max(n // fan - 1, 1))),
            dma((2, 2, max(n // fan - 1, 1))),
            dma((2, fan_steps)),
            dma((2, fan_steps, n // fan)),
            dma((2, group_steps)),
            dma((2, group_steps, n)),
            dma((2, dom_steps)),
            dma((2, dom_steps)),
            dma((7,)),
            dma((rounds, dom_steps)),
            dma((rounds, dom_steps)),
            dma((1,)),
            dma((1,)),
        ],
        compiler_params=pltpu.CompilerParams(
            collective_id=0, has_side_effects=True, vmem_limit_bytes=44 * 1024 * 1024
        ),
        name="step",
    )(
        *map(
            in_place,
            (queries, keys, values, latents, out_weight),
        ),
        step_index,
        *map(
            in_place,
            (
                embed_weight, norm_gain.reshape(1, -1), up_weight, head_weight.reshape(1, -1),
                prev_logw, ancestors,
            ),
        ),
    )
    return resampled, logw[0]


def round_count(n, particles, model_width):
    for rounds in (2, 1):
        if particles % rounds or (particles * HEADS) % (n * rounds):
            continue
        cols = particles * model_width // (n * rounds)
        if cols % LANES == 0 and model_width % cols == 0:
            return rounds
    return 0


def tiles_evenly(queries, embed_weight, up_weight):
    n = lax.axis_size("seq")
    particles, tokens, model_width = queries.shape
    if 2 * (model_width // HEADS) != LANES or not round_count(n, particles, model_width):
        return False
    if 256 % tokens or n * tokens % 256:
        return False
    return model_width % 512 == 0 and embed_weight.shape[1] % 512 == 0


def on_device(
    latents,
    queries,
    keys,
    values,
    out_weight,
    step_index,
    embed_weight,
    norm_gain,
    up_weight,
    head_weight,
    prev_logw,
    ancestors,
):
    seq_count = lax.axis_size("seq")
    dom_count = lax.axis_size("dom")
    local_particles, local_tokens, model_width = latents.shape
    local_rows = local_particles * local_tokens
    total_tokens = local_tokens * seq_count
    dom = lax.axis_index("dom")

    if tiles_evenly(queries, embed_weight, up_weight):
        return fused(
            latents, queries, keys, values, out_weight, step_index, embed_weight, norm_gain,
            up_weight, head_weight, prev_logw, ancestors,
        )
    attended, embed_full, up_full = attention(
        queries, keys, values, embed_weight, up_weight
    )
    flat = latents.reshape(local_rows, model_width).astype(jnp.float32)
    velocity = flat + jnp.dot(attended, out_weight, preferred_element_type=jnp.float32)
    sigma = step_index[0].astype(jnp.float32) / STEPS
    clean = (flat - sigma * velocity).astype(jnp.bfloat16)
    stepped = (flat - velocity / STEPS).astype(jnp.bfloat16)
    stepped = stepped.reshape(local_particles, local_tokens, model_width)
    candidates = [stepped]
    for shift in range(1, dom_count):
        pairs = [((to + shift) % dom_count, to) for to in range(dom_count)]
        candidates.append(lax.ppermute(stepped, "dom", pairs))
    embedded = jnp.dot(
        clean,
        embed_full,
        preferred_element_type=jnp.float32,
    )
    centre = jnp.mean(embedded, axis=1, keepdims=True)
    centered = embedded - centre
    variance = jnp.mean(centered * centered, axis=1, keepdims=True)
    features = jax.nn.gelu(centered * lax.rsqrt(variance + norm_eps) * norm_gain[None, :]).astype(
        jnp.bfloat16
    )
    scored = (
        jax.nn.gelu(
            jnp.dot(
                features,
                up_full,
                preferred_element_type=jnp.float32,
            )
        )
        * head_weight[None, :]
    )
    partial_value = jnp.sum(jnp.sum(scored, axis=1).reshape(local_particles, local_tokens), axis=1)
    partial_value = partial_value / math.sqrt(total_tokens)
    log_weights = weigh(partial_value, prev_logw, seq_count, dom_count)
    slot = lax.rem(ancestors // local_particles - dom + dom_count, dom_count)
    row = slot * local_particles + lax.rem(ancestors, local_particles)
    resampled = jnp.take(jnp.concatenate(candidates), row, axis=0, mode="clip")
    return (resampled, log_weights)


def solution(mesh):
    in_specs = (
        P(("groups", "dom"), "seq", None),
        P(("groups", "dom"), "seq", None),
        P(("groups", "dom"), "seq", None),
        P(("groups", "dom"), "seq", None),
        P(),
        P("groups"),
        P("seq", None),
        P(),
        P(None, "seq"),
        P(),
        P(("groups", "dom")),
        P(("groups", "dom")),
    )
    out_specs = (P(("groups", "dom"), "seq", None), P(("groups", "dom")))
    return jax.shard_map(
        on_device, mesh=mesh, in_specs=in_specs, out_specs=out_specs, check_vma=False
    )
```

```python
import functools
import math

import jax
import jax.numpy as jnp
from jax import lax
from jax.experimental import pallas as pl
from jax.experimental.pallas import tpu as pltpu
from jax.sharding import PartitionSpec as P

HEADS = 24
STEPS = 28
LANES = 128
MESH = pl.DeviceIdType.MESH

potential_scale = 4.0
norm_eps = 1e-05


def attend_plain(qb, kb, vb, ob, row, rows, column, head_width):
    cols = pl.ds(column, head_width)
    rescale = math.log2(math.e) / math.sqrt(head_width)
    scores = lax.dot_general(
        qb[pl.ds(row, rows), cols],
        kb[:, cols],
        (((1,), (1,)), ((), ())),
        preferred_element_type=jnp.float32,
    )
    highest = jnp.max(scores, axis=-1, keepdims=True)
    expanded = jnp.exp2((scores - highest) * rescale)
    total = jnp.sum(expanded, axis=-1, keepdims=True)
    mixed = jnp.dot(
        expanded.astype(jnp.bfloat16), vb[:, cols], preferred_element_type=jnp.float32
    )
    ob[pl.ds(row, rows), cols] = (mixed / total).astype(ob.dtype)


def attend_pair(qb, kb, vb, ob, row, rows, column, head_width):
    cols = pl.ds(pl.multiple_of(column, LANES), LANES)
    rescale = math.log2(math.e) / math.sqrt(head_width)
    query = qb[pl.ds(row, rows), cols]
    key = kb[:, cols]
    value = vb[:, cols]
    query_low = lax.broadcasted_iota(jnp.int32, query.shape, 1) < head_width
    value_low = lax.broadcasted_iota(jnp.int32, value.shape, 1) < head_width
    results = []
    for head in range(2):
        own_query = query_low if head == 0 else jnp.logical_not(query_low)
        own_value = value_low if head == 0 else jnp.logical_not(value_low)
        scores = lax.dot_general(
            jnp.where(own_query, query, jnp.zeros_like(query)),
            key,
            (((1,), (1,)), ((), ())),
            preferred_element_type=jnp.float32,
        )
        highest = jnp.max(scores, axis=-1, keepdims=True)
        expanded = jnp.exp2((scores - highest) * rescale).astype(jnp.bfloat16)
        results.append(
            jnp.dot(
                expanded,
                jnp.where(own_value, value, jnp.ones_like(value)),
                preferred_element_type=jnp.float32,
            )
        )
    first, second = results
    low = lax.broadcasted_iota(jnp.int32, first.shape, 1) < head_width
    mixed = jnp.where(low, first, second)
    total = pltpu.roll(jnp.where(low, second, first), head_width, 1)
    ob[pl.ds(row, rows), cols] = (mixed / total).astype(ob.dtype)


def piece(ref, item, groups, cols, start, width):
    if groups == 0:
        return ref.at[item]
    offset = pl.multiple_of((item % groups) * cols + start, LANES)
    return ref.at[item // groups, :, pl.ds(offset, width)]


def weight_exchange(
    n, fan, group_count, dom_count, embed_ref, up_ref, embed_full, up_full,
    shard_own, line_send, line_recv, fan_send, fan_recv, group_send, group_recv, dom_send, dom_recv,
):
    me = lax.axis_index("seq")
    my_group = lax.axis_index("groups")
    my_dom = lax.axis_index("dom")
    share_count = group_count * dom_count
    embed_rows, embed_cols = embed_ref.shape
    up_rows, up_cols = up_ref.shape
    embed_part = embed_cols // share_count
    up_part = up_rows // share_count

    def share(which, owner, group, dom, own=False):
        part = group * dom_count + dom
        if which == 0:
            columns = pl.ds(pl.multiple_of(part * embed_part, LANES), embed_part)
            if own:
                return embed_ref.at[:, columns]
            return embed_full.at[
                pl.ds(pl.multiple_of(owner * embed_rows, 16), embed_rows), columns
            ]
        rows = pl.ds(pl.multiple_of(part * up_part, 16), up_part)
        if own:
            return up_ref.at[rows, :]
        return up_full.at[rows, pl.ds(pl.multiple_of(owner * up_cols, LANES), up_cols)]

    def shard_copy(which):
        if which == 0:
            target = embed_full.at[pl.ds(pl.multiple_of(me * embed_rows, 16), embed_rows), :]
            return pltpu.make_async_copy(embed_ref, target, shard_own.at[0])
        target = up_full.at[:, pl.ds(pl.multiple_of(me * up_cols, LANES), up_cols)]
        return pltpu.make_async_copy(up_ref, target, shard_own.at[1])

    place = lax.div(me, fan)
    lane = lax.rem(me, fan)
    length = n // fan
    signs = (1, -1)

    def line_copy(which, direction, step, incoming):
        sign = signs[direction]
        origin = place - sign * (step if incoming else step - 1)
        owner = lax.rem(origin + n, length) * fan + lane
        to = lax.rem(place + sign + n, length) * fan + lane
        return pltpu.make_async_remote_copy(
            src_ref=share(which, owner, my_group, my_dom, own=step == 1 and not incoming),
            dst_ref=share(which, owner, my_group, my_dom),
            send_sem=line_send.at[which, direction, step - 1],
            recv_sem=line_recv.at[which, direction, step - 1],
            device_id={"seq": to},
            device_id_type=MESH,
        )

    def receives(direction, step):
        return place >= step if direction == 0 else place + step < length

    def sends(direction, step):
        if direction == 0:
            return jnp.logical_and(place >= step - 1, place + 1 < length)
        return jnp.logical_and(place + step - 1 < length, place >= 1)

    def fan_copy(which, spot, shift, incoming, own=False):
        to = lax.rem(lane + shift, fan)
        source = lax.rem(lane - shift + fan, fan) if incoming else lane
        owner = spot * fan + source
        return pltpu.make_async_remote_copy(
            src_ref=share(which, owner, my_group, my_dom, own=own),
            dst_ref=share(which, owner, my_group, my_dom),
            send_sem=fan_send.at[which, shift, spot],
            recv_sem=fan_recv.at[which, shift, spot],
            device_id={"seq": place * fan + to},
            device_id_type=MESH,
        )

    def group_copy(which, owner, shift, incoming):
        other = lax.rem(my_group + shift, group_count)
        source = lax.rem(my_group - shift + group_count, group_count) if incoming else my_group
        return pltpu.make_async_remote_copy(
            src_ref=share(which, owner, source, my_dom),
            dst_ref=share(which, owner, source, my_dom),
            send_sem=group_send.at[which, shift, owner],
            recv_sem=group_recv.at[which, shift, owner],
            device_id={"groups": other},
            device_id_type=MESH,
        )

    def dom_copy(which, owner, shift, group_shift, incoming):
        other = lax.rem(my_dom + shift, dom_count)
        source = lax.rem(my_dom - shift + dom_count, dom_count) if incoming else my_dom
        group = lax.rem(my_group - group_shift + group_count, group_count)
        return pltpu.make_async_remote_copy(
            src_ref=share(which, owner, group, source),
            dst_ref=share(which, owner, group, source),
            send_sem=dom_send.at[which, shift, group_shift, owner],
            recv_sem=dom_recv.at[which, shift, group_shift, owner],
            device_id={"dom": other},
            device_id_type=MESH,
        )

    def spread(which, owner):
        for shift in range(1, group_count):
            group_copy(which, owner, shift, False).start()
        for shift in range(1, dom_count):
            dom_copy(which, owner, shift, 0, False).start()

    def each_arrival(step, action):
        for direction in range(2):

            @pl.when(receives(direction, step))
            def _(direction=direction):
                for which in range(2):
                    action(which, direction, place - signs[direction] * step)

    def line_start():
        for which in range(2):
            for direction in range(2):

                @pl.when(sends(direction, 1))
                def _(which=which, direction=direction):
                    line_copy(which, direction, 1, False).start()

            for shift in range(1, fan):
                fan_copy(which, place, shift, False, own=True).start()
            shard_copy(which).start()

    def line_step(step):
        def action(which, direction, spot):
            line_copy(which, direction, step, True).wait_recv()
            if step + 1 < length:

                @pl.when(sends(direction, step + 1))
                def _():
                    line_copy(which, direction, step + 1, False).start()

            for shift in range(1, fan):
                fan_copy(which, spot, shift, False).start()
            spread(which, spot * fan + lane)

        each_arrival(step, action)

    def fan_step(step):
        def action(which, direction, spot):
            for shift in range(1, fan):
                fan_copy(which, spot, shift, True).wait_recv()
                spread(which, spot * fan + lax.rem(lane - shift + fan, fan))

        if step == 0:
            for which in range(2):
                action(which, 0, place)
        else:
            each_arrival(step, action)

    def group_block(which, owner):
        for group_shift in range(1, group_count):
            group_copy(which, owner, group_shift, True).wait_recv()
            for shift in range(1, dom_count):
                dom_copy(which, owner, shift, group_shift, False).start()

    def group_step(step):
        def action(which, direction, spot):
            if step > 0:
                group_block(which, spot * fan + lane)
            for shift in range(1, fan):
                group_block(which, spot * fan + lax.rem(lane - shift + fan, fan))

        if step == 0:
            for which in range(2):
                action(which, 0, place)
        else:
            each_arrival(step, action)

    def move_step(step):
        if 1 <= step < length:
            line_step(step)
        if 0 <= step - 1 < length:
            fan_step(step - 1)


    def finish_weights(parts=(0, 1)):
        for which in parts:
            shard_copy(which).wait()
            for direction in range(2):
                for step in range(1, length):

                    @pl.when(sends(direction, step))
                    def _(which=which, direction=direction, step=step):
                        line_copy(which, direction, step, False).wait_send()

            @pl.loop(0, length)
            def _(spot, which=which):
                for shift in range(1, fan):
                    fan_copy(which, spot, shift, False).wait_send()

            @pl.loop(1, n)
            def _(step, which=which):
                owner = lax.rem(me + step, n)
                for shift in range(1, group_count):
                    group_copy(which, owner, shift, False).wait_send()
                for shift in range(1, dom_count):
                    for group_shift in range(group_count):
                        dom_copy(which, owner, shift, group_shift, True).wait_recv()
                        dom_copy(which, owner, shift, group_shift, False).wait_send()

    return line_start, move_step, group_step, finish_weights, length


def take(semaphore, region):
    pltpu.make_async_copy(region, region, semaphore).wait()


def shared_weight_exchange(
    n, fan, group_count, dom_count, embed_ref, up_ref, embed_full, up_full,
    shard_own, line_send, line_recv, fan_send, fan_recv, group_send, group_recv, dom_send, dom_recv,
):
    me = lax.axis_index("seq")
    my_group = lax.axis_index("groups")
    my_dom = lax.axis_index("dom")
    share_count = group_count * dom_count
    embed_rows, embed_cols = embed_ref.shape
    up_rows, up_cols = up_ref.shape
    embed_part = embed_cols // share_count
    up_part = up_rows // share_count

    def share(which, owner, group, dom, own=False):
        part = group * dom_count + dom
        if which == 0:
            columns = pl.ds(pl.multiple_of(part * embed_part, LANES), embed_part)
            if own:
                return embed_ref.at[:, columns]
            return embed_full.at[
                pl.ds(pl.multiple_of(owner * embed_rows, 16), embed_rows), columns
            ]
        rows = pl.ds(pl.multiple_of(part * up_part, 16), up_part)
        if own:
            return up_ref.at[rows, :]
        return up_full.at[rows, pl.ds(pl.multiple_of(owner * up_cols, LANES), up_cols)]

    def shard_copy(which):
        if which == 0:
            target = embed_full.at[pl.ds(pl.multiple_of(me * embed_rows, 16), embed_rows), :]
            return pltpu.make_async_copy(embed_ref, target, shard_own.at[0])
        target = up_full.at[:, pl.ds(pl.multiple_of(me * up_cols, LANES), up_cols)]
        return pltpu.make_async_copy(up_ref, target, shard_own.at[1])

    place = lax.div(me, fan)
    lane = lax.rem(me, fan)
    length = n // fan
    signs = (1, -1)

    def line_copy(which, direction, step, incoming):
        sign = signs[direction]
        origin = place - sign * (step if incoming else step - 1)
        owner = lax.rem(origin + n, length) * fan + lane
        to = lax.rem(place + sign + n, length) * fan + lane
        return pltpu.make_async_remote_copy(
            src_ref=share(which, owner, my_group, my_dom, own=step == 1 and not incoming),
            dst_ref=share(which, owner, my_group, my_dom),
            send_sem=line_send.at[which, direction, step - 1],
            recv_sem=line_recv.at[which, direction, step - 1],
            device_id={"seq": to},
            device_id_type=MESH,
        )

    def receives(direction, step):
        return place >= step if direction == 0 else place + step < length

    def sends(direction, step):
        if direction == 0:
            return jnp.logical_and(place >= step - 1, place + 1 < length)
        return jnp.logical_and(place + step - 1 < length, place >= 1)

    def fan_copy(which, spot, shift, incoming, own=False):
        to = lax.rem(lane + shift, fan)
        source = lax.rem(lane - shift + fan, fan) if incoming else lane
        owner = spot * fan + source
        return pltpu.make_async_remote_copy(
            src_ref=share(which, owner, my_group, my_dom, own=own),
            dst_ref=share(which, owner, my_group, my_dom),
            send_sem=fan_send.at[which, shift - 1],
            recv_sem=fan_recv.at[which, shift - 1, spot],
            device_id={"seq": place * fan + to},
            device_id_type=MESH,
        )

    def group_copy(which, owner, shift, incoming):
        other = lax.rem(my_group + shift, group_count)
        source = lax.rem(my_group - shift + group_count, group_count) if incoming else my_group
        return pltpu.make_async_remote_copy(
            src_ref=share(which, owner, source, my_dom),
            dst_ref=share(which, owner, source, my_dom),
            send_sem=group_send.at[which, shift - 1],
            recv_sem=group_recv.at[which, shift - 1, owner],
            device_id={"groups": other},
            device_id_type=MESH,
        )

    def dom_copy(which, owner, shift, group_shift, incoming):
        other = lax.rem(my_dom + shift, dom_count)
        source = lax.rem(my_dom - shift + dom_count, dom_count) if incoming else my_dom
        group = lax.rem(my_group - group_shift + group_count, group_count)
        return pltpu.make_async_remote_copy(
            src_ref=share(which, owner, group, source),
            dst_ref=share(which, owner, group, source),
            send_sem=dom_send.at[which, shift - 1],
            recv_sem=dom_recv.at[which, shift - 1],
            device_id={"dom": other},
            device_id_type=MESH,
        )

    def spread(which, owner):
        for shift in range(1, group_count):
            group_copy(which, owner, shift, False).start()
        for shift in range(1, dom_count):
            dom_copy(which, owner, shift, 0, False).start()

    def each_arrival(step, action):
        for direction in range(2):

            @pl.when(receives(direction, step))
            def _(direction=direction):
                for which in range(2):
                    action(which, direction, place - signs[direction] * step)

    def line_start():
        for which in range(2):
            for direction in range(2):

                @pl.when(sends(direction, 1))
                def _(which=which, direction=direction):
                    line_copy(which, direction, 1, False).start()

            for shift in range(1, fan):
                fan_copy(which, place, shift, False, own=True).start()
            shard_copy(which).start()

    def line_step(step):
        def action(which, direction, spot):
            line_copy(which, direction, step, True).wait_recv()
            if step + 1 < length:

                @pl.when(sends(direction, step + 1))
                def _():
                    line_copy(which, direction, step + 1, False).start()

            for shift in range(1, fan):
                fan_copy(which, spot, shift, False).start()
            spread(which, spot * fan + lane)

        each_arrival(step, action)

    def fan_step(step):
        def action(which, direction, spot):
            for shift in range(1, fan):
                fan_copy(which, spot, shift, True).wait_recv()
                spread(which, spot * fan + lax.rem(lane - shift + fan, fan))

        if step == 0:
            for which in range(2):
                action(which, 0, place)
        else:
            each_arrival(step, action)

    def group_block(which, owner):
        for group_shift in range(1, group_count):
            group_copy(which, owner, group_shift, True).wait_recv()
            for shift in range(1, dom_count):
                dom_copy(which, owner, shift, group_shift, False).start()

    def group_step(step):
        def action(which, direction, spot):
            if step > 0:
                group_block(which, spot * fan + lane)
            for shift in range(1, fan):
                group_block(which, spot * fan + lax.rem(lane - shift + fan, fan))

        if step == 0:
            for which in range(2):
                action(which, 0, place)
        else:
            each_arrival(step, action)

    def parts_of(which, amount):
        if which == 0:
            wide = math.gcd(amount, share_count)
            return embed_full.at[0 : amount // wide * embed_rows, 0 : wide * embed_part]
        wide = math.gcd(amount, share_count)
        return up_full.at[0 : wide * up_part, 0 : amount // wide * up_cols]

    def finish_weights(parts=(0, 1)):
        for which in parts:
            shard_copy(which).wait()
            for direction in range(2):
                for step in range(1, length):

                    @pl.when(sends(direction, step))
                    def _(which=which, direction=direction, step=step):
                        line_copy(which, direction, step, False).wait_send()

            for shift in range(1, fan):
                take(fan_send.at[which, shift - 1], parts_of(which, length))
            for shift in range(1, group_count):
                take(group_send.at[which, shift - 1], parts_of(which, n - 1))
            for shift in range(1, dom_count):
                take(dom_recv.at[which, shift - 1], parts_of(which, (n - 1) * group_count))
                take(dom_send.at[which, shift - 1], parts_of(which, (n - 1) * group_count))

    return line_start, line_step, fan_step, group_step, finish_weights, length


def attention_kernel(
    n, fan, group_count, dom_count, groups, cols, width, head_width, row_block,
    q_ref, k_ref, v_ref, embed_ref, up_ref, o_ref, embed_full, up_full,
    qb, kb, vb, ob, send_sem, recv_sem, own_sem, back_send, back_recv, back_own,
    shard_own, line_send, line_recv, fan_send, fan_recv, group_send, group_recv, dom_send, dom_recv,
):
    me = lax.axis_index("seq")
    my_group = lax.axis_index("groups")
    my_dom = lax.axis_index("dom")
    tokens = q_ref.shape[1]
    total_tokens = n * tokens
    chunks = cols // width
    inputs = ((q_ref, qb), (k_ref, kb), (v_ref, vb))

    barrier = pltpu.get_barrier_semaphore()

    @pl.loop(1, n)
    def _(step):
        pl.semaphore_signal(
            barrier, inc=1, device_id={"seq": lax.rem(me + step, n)}, device_id_type=MESH
        )

    for step in range(1, group_count):
        peer = {"groups": lax.rem(my_group + step, group_count)}
        pl.semaphore_signal(barrier, inc=1, device_id=peer, device_id_type=MESH)
    for step in range(1, dom_count):
        peer = {"dom": lax.rem(my_dom + step, dom_count)}
        pl.semaphore_signal(barrier, inc=1, device_id=peer, device_id_type=MESH)
    pl.semaphore_wait(barrier, n - 1 + group_count - 1 + dom_count - 1)

    line_start, move_step, group_step, finish_weights, length = weight_exchange(
        n, fan, group_count, dom_count, embed_ref, up_ref, embed_full, up_full,
        shard_own, line_send, line_recv, fan_send, fan_recv, group_send, group_recv,
        dom_send, dom_recv,
    )

    def rows_of(ref, owner, chunk):
        row = pl.ds(pl.multiple_of(owner * tokens, 16), tokens)
        return ref.at[row, pl.ds(chunk * width, width)]

    def outgoing(index, chunk, target, slot):
        source, buffer = inputs[index]
        return pltpu.make_async_remote_copy(
            src_ref=piece(source, target, groups, cols, chunk * width, width),
            dst_ref=rows_of(buffer, me, chunk),
            send_sem=send_sem.at[index, chunk, target],
            recv_sem=recv_sem.at[index, chunk, slot],
            device_id={"seq": target},
            device_id_type=MESH,
        )

    def own_copy(index, chunk):
        source, buffer = inputs[index]
        return pltpu.make_async_copy(
            piece(source, me, groups, cols, chunk * width, width),
            rows_of(buffer, me, chunk),
            own_sem.at[index, chunk],
        )

    def returned(chunk, target, slot):
        return pltpu.make_async_remote_copy(
            src_ref=rows_of(ob, target, chunk),
            dst_ref=piece(o_ref, me, groups, cols, chunk * width, width),
            send_sem=back_send.at[chunk, target],
            recv_sem=back_recv.at[chunk, slot],
            device_id={"seq": target},
            device_id_type=MESH,
        )

    def own_return(chunk):
        return pltpu.make_async_copy(
            rows_of(ob, me, chunk),
            piece(o_ref, me, groups, cols, chunk * width, width),
            back_own.at[chunk],
        )

    weight_steps = length + 2

    def weight_step(step):
        move_step(step)
        if 0 <= step - 2 < length:
            group_step(step - 2)

    ready = 1
    for chunk in range(chunks):
        if chunk == 0:
            line_start()
        elif ready < weight_steps:
            weight_step(ready)
            ready += 1
        for index in range(3):
            own_copy(index, chunk).start()

            @pl.loop(1, n)
            def _(step, index=index, chunk=chunk):
                outgoing(index, chunk, lax.rem(me + step, n), me).start()

    paired = 2 * head_width == LANES and width % LANES == 0
    unit = LANES if paired else head_width
    blocks = total_tokens // row_block

    for chunk in range(chunks):
        for index in range(3):
            own_copy(index, chunk).wait()

            @pl.loop(1, n)
            def _(step, index=index, chunk=chunk):
                other = lax.rem(me + step, n)
                outgoing(index, chunk, other, other).wait_recv()

        if paired:

            @pl.loop(0, (width // unit) * blocks)
            def _(step, chunk=chunk):
                attend_pair(
                    qb, kb, vb, ob,
                    pl.multiple_of((step % blocks) * row_block, row_block), row_block,
                    chunk * width + (step // blocks) * unit, head_width,
                )
        else:
            for head in range(width // unit):

                @pl.loop(0, blocks)
                def _(step, head=head, chunk=chunk):
                    attend_plain(
                        qb, kb, vb, ob,
                        pl.multiple_of(step * row_block, row_block), row_block,
                        chunk * width + head * unit, head_width,
                    )

        own_return(chunk).start()

        @pl.loop(1, n)
        def _(step, chunk=chunk):
            returned(chunk, lax.rem(me + step, n), me).start()

        if ready < weight_steps and chunk < chunks - 1:
            weight_step(ready)
            ready += 1

    for step in range(ready, weight_steps):
        weight_step(step)
    finish_weights()

    for chunk in range(chunks):
        own_return(chunk).wait()
        for index in range(3):

            @pl.loop(1, n)
            def _(step, index=index, chunk=chunk):
                outgoing(index, chunk, lax.rem(me + step, n), me).wait_send()

        @pl.loop(1, n)
        def _(step, chunk=chunk):
            other = lax.rem(me + step, n)
            returned(chunk, other, other).wait_recv()
            returned(chunk, other, me).wait_send()


def attention(queries, keys, values, embed_weight, up_weight):
    n = lax.axis_size("seq")
    group_count = lax.axis_size("groups")
    dom_count = lax.axis_size("dom")
    fan = 2 if n % 2 == 0 else 1
    particles, tokens, model_width = queries.shape
    head_width = model_width // HEADS
    per_device = particles * HEADS // n
    cols = per_device * head_width
    aligned = model_width % cols == 0 and cols % LANES == 0
    groups = model_width // cols if aligned else 0
    width = 2 * LANES if aligned and cols % (2 * LANES) == 0 else cols
    chunks = cols // width
    total_tokens = n * tokens

    def to_items(array):
        if aligned:
            return array
        split = array.reshape(particles, tokens, HEADS, head_width).transpose(0, 2, 1, 3)
        split = split.reshape(n, per_device, tokens, head_width).transpose(0, 2, 1, 3)
        return split.reshape(n, tokens, cols)

    operands = tuple(to_items(a) for a in (queries, keys, values))
    any_spec = pl.BlockSpec(memory_space=pl.ANY)
    embed_shape = (n * embed_weight.shape[0], embed_weight.shape[1])
    up_shape = (up_weight.shape[0], n * up_weight.shape[1])
    out, embed_full, up_full = pl.pallas_call(
        functools.partial(
            attention_kernel, n, fan, group_count, dom_count, groups, cols, width, head_width,
            min(256, total_tokens),
        ),
        out_shape=(
            jax.ShapeDtypeStruct(operands[0].shape, jnp.bfloat16),
            jax.ShapeDtypeStruct(embed_shape, jnp.bfloat16),
            jax.ShapeDtypeStruct(up_shape, jnp.bfloat16),
        ),
        in_specs=[any_spec] * 5,
        out_specs=(any_spec,) * 3,
        scratch_shapes=[pltpu.VMEM((total_tokens, cols), jnp.bfloat16)] * 4
        + [
            pltpu.SemaphoreType.DMA((3, chunks, n)),
            pltpu.SemaphoreType.DMA((3, chunks, n)),
            pltpu.SemaphoreType.DMA((3, chunks)),
            pltpu.SemaphoreType.DMA((chunks, n)),
            pltpu.SemaphoreType.DMA((chunks, n)),
            pltpu.SemaphoreType.DMA((chunks,)),
            pltpu.SemaphoreType.DMA((2,)),
            pltpu.SemaphoreType.DMA((2, 2, n // fan)),
            pltpu.SemaphoreType.DMA((2, 2, n // fan)),
            pltpu.SemaphoreType.DMA((2, fan, n // fan)),
            pltpu.SemaphoreType.DMA((2, fan, n // fan)),
            pltpu.SemaphoreType.DMA((2, group_count, n)),
            pltpu.SemaphoreType.DMA((2, group_count, n)),
            pltpu.SemaphoreType.DMA((2, dom_count, group_count, n)),
            pltpu.SemaphoreType.DMA((2, dom_count, group_count, n)),
        ],
        compiler_params=pltpu.CompilerParams(
            collective_id=0, has_side_effects=True, vmem_limit_bytes=60 * 1024 * 1024
        ),
        name="attention",
    )(*operands, embed_weight, up_weight)
    if not aligned:
        out = out.reshape(n, tokens, per_device, head_width).transpose(0, 2, 1, 3)
        out = out.reshape(particles, HEADS, tokens, head_width).transpose(0, 2, 1, 3)
    return out.reshape(particles * tokens, model_width), embed_full, up_full


def reward_kernel(n, doms, particles, x_ref, o_ref, held, send_sem, recv_sem):
    me = lax.axis_index("dom") * n + lax.axis_index("seq")
    members = n * doms

    def target(step):
        other = lax.rem(me + step, members)
        return other, {"dom": other // n, "seq": other % n}

    def copy(step, slot):
        other, device = target(step)
        return pltpu.make_async_remote_copy(
            src_ref=x_ref,
            dst_ref=held.at[me],
            send_sem=send_sem.at[other],
            recv_sem=recv_sem.at[slot],
            device_id=device,
            device_id_type=MESH,
        )

    barrier = pltpu.get_barrier_semaphore()

    @pl.loop(1, members)
    def _(step):
        _, device = target(step)
        pl.semaphore_signal(barrier, inc=1, device_id=device, device_id_type=MESH)

    pl.semaphore_wait(barrier, members - 1)

    @pl.loop(1, members)
    def _(step):
        copy(step, me).start()

    held[me] = x_ref[...]

    @pl.loop(1, members)
    def _(step):
        copy(step, lax.rem(me + step, members)).wait_recv()

    logits = []
    for dom in range(doms):
        rewards = jnp.sum(held[dom * n : (dom + 1) * n], axis=0)[:1]
        value = held[dom * n][1:2] + potential_scale * rewards
        used = lax.broadcasted_iota(jnp.int32, value.shape, 1) < particles
        logits.append(jnp.where(used, value, -jnp.inf))
    highest = functools.reduce(jnp.maximum, [jnp.max(v, axis=1, keepdims=True) for v in logits])
    total = sum(jnp.sum(jnp.exp(v - highest), axis=1, keepdims=True) for v in logits)
    own = logits[0]
    for dom in range(1, doms):
        own = jnp.where(lax.axis_index("dom") == dom, logits[dom], own)
    o_ref[...] = jnp.broadcast_to(own - (highest + jnp.log(total)), o_ref.shape)

    @pl.loop(1, members)
    def _(step):
        copy(step, me).wait_send()


def weigh(partial_value, prev_logw, n, doms):
    particles = partial_value.shape[0]
    rows = jnp.stack([partial_value, prev_logw])
    padded = jnp.pad(rows, ((0, 8 - 2), (0, LANES - particles)))
    vmem = pl.BlockSpec(memory_space=pltpu.VMEM)
    out = pl.pallas_call(
        functools.partial(reward_kernel, n, doms, particles),
        out_shape=jax.ShapeDtypeStruct((8, LANES), jnp.float32),
        in_specs=[vmem],
        out_specs=vmem,
        scratch_shapes=[
            pltpu.VMEM((n * doms, 8, LANES), jnp.float32),
            pltpu.SemaphoreType.DMA((n * doms,)),
            pltpu.SemaphoreType.DMA((n * doms,)),
        ],
        compiler_params=pltpu.CompilerParams(collective_id=1, has_side_effects=True),
        name="rewards",
    )(padded)
    return out[0, :particles]


def part_sum(block, rows):
    parts = [
        jnp.sum(block[at : at + rows], axis=0, keepdims=True)
        for at in range(0, block.shape[0], rows)
    ]
    return jnp.concatenate(parts, axis=0)


def fused_kernel(
    n, fan, group_count, dom_count, rounds, groups, chunks, head_width, row_block, tile,
    q_ref, k_ref, v_ref, lat_ref, wo_ref, step_in, embed_ref, gain_in, up_ref, head_in,
    prev_in, anc_in, out_ref, logw_ref,
    step_ref, gain_ref, head_ref, prev_ref, anc_ref, picked,
    qb, kb, vb, ob, mixed, embed_full, up_full, wo, lat, velocity, clean, embedded, features,
    cand, score, mine, held,
    send_sem, recv_sem, back_send, back_recv,
    shard_own, line_send, line_recv, fan_send, fan_recv, group_send, group_recv, dom_send, dom_recv,
    load_sem, step_send, step_recv, score_send, score_recv,
):
    me = lax.axis_index("seq")
    my_group = lax.axis_index("groups")
    my_dom = lax.axis_index("dom")
    particles, tokens, model_width = q_ref.shape
    rows = particles * tokens
    share = particles // rounds
    share_rows = share * tokens
    total_tokens = n * tokens
    inputs = ((q_ref, qb), (k_ref, kb), (v_ref, vb))
    members = n * dom_count
    member = my_dom * n + me

    def other_member(step):
        other = lax.rem(member + step, members)
        return other, {"dom": other // n, "seq": other % n}

    small = (
        (wo_ref, wo), (lat_ref, lat), (step_in, step_ref), (gain_in, gain_ref),
        (head_in, head_ref), (prev_in, prev_ref), (anc_in, anc_ref),
    )
    loads = [
        pltpu.make_async_copy(source, target, load_sem.at[at])
        for at, (source, target) in enumerate(small)
    ]

    barrier = pltpu.get_barrier_semaphore()

    @pl.loop(1, members)
    def _(step):
        _, device = other_member(step)
        pl.semaphore_signal(barrier, inc=1, device_id=device, device_id_type=MESH)

    for step in range(1, group_count):
        peer = {"groups": lax.rem(my_group + step, group_count)}
        pl.semaphore_signal(barrier, inc=1, device_id=peer, device_id_type=MESH)
    for load in loads:
        load.start()
    pl.semaphore_wait(barrier, members - 1 + group_count - 1)

    line_start, line_step, fan_step, group_step, finish_weights, length = shared_weight_exchange(
        n, fan, group_count, dom_count, embed_ref, up_ref, embed_full, up_full,
        shard_own, line_send, line_recv, fan_send, fan_recv, group_send, group_recv,
        dom_send, dom_recv,
    )

    cols = model_width // groups

    def source_of(ref, item, chunk):
        turn, start, width = chunks[chunk]
        offset = pl.multiple_of(groups * start + (item % groups) * width, LANES)
        return ref.at[turn * share + item // groups, :, pl.ds(offset, width)]

    def mixed_of(item, chunk):
        turn, start, width = chunks[chunk]
        offset = pl.multiple_of(groups * start + (item % groups) * width, LANES)
        row = pl.multiple_of((turn * share + item // groups) * tokens, 16)
        return mixed.at[pl.ds(row, tokens), pl.ds(offset, width)]

    def rows_of(ref, owner, chunk):
        turn, start, width = chunks[chunk]
        row = pl.ds(pl.multiple_of(owner * tokens, 16), tokens)
        return ref.at[row, pl.ds(turn * cols + start, width)]

    def outgoing(index, chunk, target):
        source, buffer = inputs[index]
        return pltpu.make_async_remote_copy(
            src_ref=source_of(source, target, chunk),
            dst_ref=rows_of(buffer, me, chunk),
            send_sem=send_sem.at[index, chunk],
            recv_sem=recv_sem.at[index, chunk],
            device_id={"seq": target},
            device_id_type=MESH,
        )

    def own_copy(index, chunk):
        source, buffer = inputs[index]
        return pltpu.make_async_copy(
            source_of(source, me, chunk), rows_of(buffer, me, chunk), recv_sem.at[index, chunk]
        )

    def returned(chunk, target):
        return pltpu.make_async_remote_copy(
            src_ref=rows_of(ob, target, chunk),
            dst_ref=mixed_of(me, chunk),
            send_sem=back_send.at[chunk],
            recv_sem=back_recv.at[chunk],
            device_id={"seq": target},
            device_id_type=MESH,
        )

    def own_return(chunk):
        return pltpu.make_async_copy(
            rows_of(ob, me, chunk), mixed_of(me, chunk), back_recv.at[chunk]
        )

    count = len(chunks)
    blocks = total_tokens // row_block
    owners = row_block // tokens

    def issue(chunk):
        for index in range(3):
            own_copy(index, chunk).start()

            @pl.loop(1, n)
            def _(step, index=index):
                outgoing(index, chunk, lax.rem(me + step, n)).start()

    def attend(chunk):
        turn, start, width = chunks[chunk]
        first = turn * cols + start
        for at in range(1, blocks + 1):
            block = lax.rem(lax.div(me, owners) + at, blocks)
            row = pl.multiple_of(block * row_block, row_block)

            @pl.loop(0, width // LANES)
            def _(unit, row=row):
                attend_pair(
                    qb, kb, vb, ob, row, row_block, first + unit * LANES, head_width
                )

            @pl.loop(0 if at < blocks else 1, owners)
            def _(step, block=block):
                target = block * owners + lax.rem(me + step, owners)
                returned(chunk, target).start()

        own_return(chunk).start()

    def arrive(chunk):
        turn, start, width = chunks[chunk]
        for index in range(3):
            buffer = inputs[index][1]
            first = turn * cols + start
            take(recv_sem.at[index, chunk], buffer.at[:, first : first + width])

    def project(chunk):
        if chunk == 0:
            for load in loads:
                load.wait()
        sigma = step_ref[0].astype(jnp.float32) / STEPS
        turn, start, width = chunks[chunk]
        inner = pl.ds(groups * start, groups * width)
        own_rows = pl.ds(turn * share_rows, share_rows)
        final = chunk + 1 == count or chunks[chunk + 1][0] != turn
        take(back_recv.at[chunk], mixed.at[own_rows, inner])

        @pl.loop(0, model_width // tile, unroll=model_width // tile)
        def _(step):
            columns = pl.ds(pl.multiple_of(step * tile, tile), tile)
            part = jnp.dot(
                mixed[own_rows, inner], wo[inner, columns], preferred_element_type=jnp.float32
            )
            if start > 0:
                part = velocity[own_rows, columns] + part
            if not final:
                velocity[own_rows, columns] = part
                return
            for item in range(share):
                at = slice(item * tokens, (item + 1) * tokens)
                spot = turn * share + item
                flat = lat[spot, :, columns].astype(jnp.float32)
                moved = flat + part[at]
                clean[spot * tokens : (spot + 1) * tokens, columns] = (
                    flat - sigma * moved
                ).astype(jnp.bfloat16)
                cand[my_dom * particles + spot, :, columns] = (flat - moved / STEPS).astype(
                    jnp.bfloat16
                )

    def step_copy(turn, shift, incoming):
        source = lax.rem(my_dom - shift + dom_count, dom_count) if incoming else my_dom
        block = cand.at[pl.ds(source * particles + turn * share, share)]
        return pltpu.make_async_remote_copy(
            src_ref=block,
            dst_ref=block,
            send_sem=step_send.at[turn, shift - 1],
            recv_sem=step_recv.at[turn, shift - 1],
            device_id={"dom": lax.rem(my_dom + shift, dom_count)},
            device_id_type=MESH,
        )

    def embed(turn):
        if turn == 0:
            finish_weights((0,))
        own_rows = pl.ds(turn * share_rows, share_rows)

        @pl.loop(0, embedded.shape[1] // tile, unroll=embedded.shape[1] // tile)
        def _(step):
            columns = pl.ds(pl.multiple_of(step * tile, tile), tile)
            embedded[own_rows, columns] = jnp.dot(
                clean[own_rows, :], embed_full[:, columns], preferred_element_type=jnp.float32
            )

        for shift in range(1, dom_count):
            step_copy(turn, shift, False).start()

        @pl.loop(turn * share, (turn + 1) * share, unroll=share)
        def _(item):
            item_rows = pl.ds(pl.multiple_of(item * tokens, tokens), tokens)
            block = embedded[item_rows, :]
            centered = block - jnp.mean(block, axis=1, keepdims=True)
            variance = jnp.mean(centered * centered, axis=1, keepdims=True)
            normed = centered * lax.rsqrt(variance + norm_eps) * gain_ref[...]
            features[item_rows, :] = jax.nn.gelu(normed).astype(jnp.bfloat16)

    def judge(turn):
        if turn == 0:
            finish_weights((1,))
        own_rows = pl.ds(turn * share_rows, share_rows)

        @pl.loop(0, up_full.shape[1] // tile, unroll=min(8, up_full.shape[1] // tile))
        def _(step):
            columns = pl.ds(pl.multiple_of(step * tile, tile), tile)
            hidden = jnp.dot(
                features[own_rows, :], up_full[:, columns], preferred_element_type=jnp.float32
            )
            score[turn * share : (turn + 1) * share, :] += (
                part_sum(jax.nn.gelu(hidden), tokens) * head_ref[:, columns]
            )

    actions = {
        "issue": issue, "arrive": arrive, "attend": attend,
        "line": line_step, "fan": fan_step, "group": group_step, "start": lambda _: line_start(),
        "project": project, "embed": embed, "judge": judge,
    }
    score[...] = jnp.zeros_like(score)
    for name, at in plan(chunks, length):
        actions[name](at)

    partial_value = jnp.sum(score[...], axis=1, keepdims=True) / math.sqrt(total_tokens)
    lane = lax.broadcasted_iota(jnp.int32, (particles, LANES), 1)
    row = lax.broadcasted_iota(jnp.int32, (particles, LANES), 0)
    before = jnp.zeros((particles, LANES), jnp.float32)
    for item in range(particles):
        before = jnp.where(row == item, prev_ref[item], before)
    half = LANES // 2
    own_block = jnp.where(lane < half, partial_value, before)
    mine[0:particles, :] = own_block
    held[member, 0:particles, :] = own_block

    def score_copy(step):
        _, device = other_member(step)
        return pltpu.make_async_remote_copy(
            src_ref=mine,
            dst_ref=held.at[member],
            send_sem=score_send.at[0],
            recv_sem=score_recv.at[0],
            device_id=device,
            device_id_type=MESH,
        )

    @pl.loop(1, members)
    def _(step):
        score_copy(step).start()

    for turn in range(rounds):
        for shift in range(1, dom_count):
            step_copy(turn, shift, True).wait_recv()
    for item in range(particles):
        picked[item] = cand[anc_ref[item]]
    write = pltpu.make_async_copy(picked, out_ref, load_sem.at[0])
    write.start()

    for chunk in range(count):
        sent = qb.at[0 : (n - 1) * tokens, 0 : chunks[chunk][2]]
        for index in range(3):
            take(send_sem.at[index, chunk], sent)
        take(back_send.at[chunk], sent)

    for turn in range(rounds):
        for shift in range(1, dom_count):
            step_copy(turn, shift, False).wait_send()

    take(score_recv.at[0], held.at[0 : members - 1])

    logits = []
    for dom in range(dom_count):
        reward = jnp.sum(held[dom * n : (dom + 1) * n, 0:particles, :], axis=0)[:, 0:1]
        logits.append(held[dom * n, 0:particles, :][:, half : half + 1] + potential_scale * reward)
    highest = functools.reduce(
        jnp.maximum, [jnp.max(value, axis=0, keepdims=True) for value in logits]
    )
    total = sum(jnp.sum(jnp.exp(value - highest), axis=0, keepdims=True) for value in logits)
    own = logits[0]
    for dom in range(1, dom_count):
        own = jnp.where(my_dom == dom, logits[dom], own)
    result = jnp.broadcast_to(own - (highest + jnp.log(total)), (particles, LANES))
    result = jnp.sum(jnp.where(row == lane, result, 0.0), axis=0, keepdims=True)
    logw_ref[...] = result[:, 0:particles]

    take(score_send.at[0], held.at[0 : members - 1])
    write.wait()


def plan(chunks, length):
    count = len(chunks)
    last = chunks[-1][0]
    early = [chunk for chunk in range(count) if chunks[chunk][0] < last]
    late = [chunk for chunk in range(count) if chunks[chunk][0] == last]
    lines = list(range(2, length))
    fans = list(range(1, length))
    steps = [("start", 0), ("issue", 0), ("line", 1), ("fan", 0)]
    if length == 1:
        steps = [("start", 0), ("issue", 0), ("fan", 0)]
    steps += [("issue", chunk) for chunk in range(1, min(2, count))]
    for chunk in range(count):
        if chunk == count - 1:
            steps += [("line", step) for step in lines] + [("fan", step) for step in fans]
            steps += [("group", step) for step in range(length)]
            steps += [("project", part) for part in early]
            steps += [("embed", turn) for turn in range(last)]
        elif chunk == 0:
            steps += [("line", step) for step in lines[:1]] + [("fan", step) for step in fans[:1]]
            lines, fans = lines[1:], fans[1:]
        steps += [("arrive", chunk), ("attend", chunk)]
        if chunk + 2 < count:
            steps.append(("issue", chunk + 2))
        if chunk < count - 1:
            steps += [("line", step) for step in lines[:1]] + [("fan", step) for step in fans[:1]]
            lines, fans = lines[1:], fans[1:]
    for turn in range(last):
        steps.append(("judge", turn))
    return steps + [("project", part) for part in late] + [("embed", last), ("judge", last)]


def chunk_list(rounds, cols):
    chunks = []
    for turn in range(rounds):
        widths = [2 * LANES] * (cols // (2 * LANES)) + [LANES] * (cols % (2 * LANES) // LANES)
        if turn == 0:
            widths.reverse()
        start = 0
        for width in widths:
            chunks.append((turn, start, width))
            start += width
    return tuple(chunks)


def in_place(array):
    return pltpu.with_memory_space_constraint(array, pltpu.HBM)


def fused(
    latents, queries, keys, values, out_weight, step_index, embed_weight, norm_gain, up_weight,
    head_weight, prev_logw, ancestors,
):
    n = lax.axis_size("seq")
    group_count = lax.axis_size("groups")
    dom_count = lax.axis_size("dom")
    fan = 2 if n % 2 == 0 else 1
    particles, tokens, model_width = queries.shape
    head_width = model_width // HEADS
    rounds = round_count(n, particles, model_width)
    cols = particles * model_width // (n * rounds)
    groups = model_width // cols
    chunks = chunk_list(rounds, cols)
    count = len(chunks)
    rows = particles * tokens
    total_tokens = n * tokens
    members = n * dom_count
    fan_steps, group_steps, dom_steps = (max(x - 1, 1) for x in (fan, group_count, dom_count))
    tile = 512
    embed_shape = (n * embed_weight.shape[0], embed_weight.shape[1])
    up_shape = (up_weight.shape[0], n * up_weight.shape[1])
    hbm = pl.BlockSpec(memory_space=pl.ANY)
    vmem = pl.BlockSpec(memory_space=pltpu.VMEM)
    bf16 = jnp.bfloat16
    dma = pltpu.SemaphoreType.DMA
    resampled, logw = pl.pallas_call(
        functools.partial(
            fused_kernel, n, fan, group_count, dom_count, rounds, groups, chunks, head_width,
            min(256, total_tokens), tile,
        ),
        out_shape=(
            jax.ShapeDtypeStruct(latents.shape, bf16),
            jax.ShapeDtypeStruct((1, particles), jnp.float32),
        ),
        in_specs=[hbm] * 12,
        out_specs=(hbm, vmem),
        scratch_shapes=[
            pltpu.SMEM(step_index.shape, jnp.int32),
            pltpu.VMEM((1, norm_gain.shape[0]), jnp.float32),
            pltpu.VMEM((1, head_weight.shape[0]), jnp.float32),
            pltpu.SMEM(prev_logw.shape, jnp.float32),
            pltpu.SMEM(ancestors.shape, jnp.int32),
            pltpu.VMEM(latents.shape, bf16),
        ]
        + [pltpu.VMEM((total_tokens, rounds * cols), bf16)] * 4
        + [
            pltpu.VMEM((rows, model_width), bf16),
            pltpu.VMEM(embed_shape, bf16),
            pltpu.VMEM(up_shape, bf16),
            pltpu.VMEM(out_weight.shape, bf16),
            pltpu.VMEM(latents.shape, bf16),
            pltpu.VMEM((rows, model_width), jnp.float32),
            pltpu.VMEM((rows, model_width), bf16),
            pltpu.VMEM((rows, embed_shape[1]), jnp.float32),
            pltpu.VMEM((rows, embed_shape[1]), bf16),
            pltpu.VMEM((dom_count * particles, tokens, model_width), bf16),
            pltpu.VMEM((particles, tile), jnp.float32),
            pltpu.VMEM((8, LANES), jnp.float32),
            pltpu.VMEM((members, 8, LANES), jnp.float32),
            dma((3, count)),
            dma((3, count)),
            dma((count,)),
            dma((count,)),
            dma((2,)),
            dma((2, 2, max(n // fan - 1, 1))),
            dma((2, 2, max(n // fan - 1, 1))),
            dma((2, fan_steps)),
            dma((2, fan_steps, n // fan)),
            dma((2, group_steps)),
            dma((2, group_steps, n)),
            dma((2, dom_steps)),
            dma((2, dom_steps)),
            dma((7,)),
            dma((rounds, dom_steps)),
            dma((rounds, dom_steps)),
            dma((1,)),
            dma((1,)),
        ],
        compiler_params=pltpu.CompilerParams(
            collective_id=0, has_side_effects=True, vmem_limit_bytes=44 * 1024 * 1024
        ),
        name="step",
    )(
        *map(
            in_place,
            (queries, keys, values, latents, out_weight),
        ),
        step_index,
        *map(
            in_place,
            (
                embed_weight, norm_gain.reshape(1, -1), up_weight, head_weight.reshape(1, -1),
                prev_logw, ancestors,
            ),
        ),
    )
    return resampled, logw[0]


def round_count(n, particles, model_width):
    for rounds in (2, 1):
        if particles % rounds or (particles * HEADS) % (n * rounds):
            continue
        cols = particles * model_width // (n * rounds)
        if cols % LANES == 0 and model_width % cols == 0:
            return rounds
    return 0


def tiles_evenly(queries, embed_weight, up_weight):
    n = lax.axis_size("seq")
    particles, tokens, model_width = queries.shape
    if 2 * (model_width // HEADS) != LANES or not round_count(n, particles, model_width):
        return False
    if 256 % tokens or n * tokens % 256:
        return False
    return model_width % 512 == 0 and embed_weight.shape[1] % 512 == 0


def on_device(
    latents,
    queries,
    keys,
    values,
    out_weight,
    step_index,
    embed_weight,
    norm_gain,
    up_weight,
    head_weight,
    prev_logw,
    ancestors,
):
    seq_count = lax.axis_size("seq")
    dom_count = lax.axis_size("dom")
    local_particles, local_tokens, model_width = latents.shape
    local_rows = local_particles * local_tokens
    total_tokens = local_tokens * seq_count
    dom = lax.axis_index("dom")

    if tiles_evenly(queries, embed_weight, up_weight):
        return fused(
            latents, queries, keys, values, out_weight, step_index, embed_weight, norm_gain,
            up_weight, head_weight, prev_logw, ancestors,
        )
    attended, embed_full, up_full = attention(
        queries, keys, values, embed_weight, up_weight
    )
    flat = latents.reshape(local_rows, model_width).astype(jnp.float32)
    velocity = flat + jnp.dot(attended, out_weight, preferred_element_type=jnp.float32)
    sigma = step_index[0].astype(jnp.float32) / STEPS
    clean = (flat - sigma * velocity).astype(jnp.bfloat16)
    stepped = (flat - velocity / STEPS).astype(jnp.bfloat16)
    stepped = stepped.reshape(local_particles, local_tokens, model_width)
    candidates = [stepped]
    for shift in range(1, dom_count):
        pairs = [((to + shift) % dom_count, to) for to in range(dom_count)]
        candidates.append(lax.ppermute(stepped, "dom", pairs))
    embedded = jnp.dot(
        clean,
        embed_full,
        preferred_element_type=jnp.float32,
    )
    centre = jnp.mean(embedded, axis=1, keepdims=True)
    centered = embedded - centre
    variance = jnp.mean(centered * centered, axis=1, keepdims=True)
    features = jax.nn.gelu(centered * lax.rsqrt(variance + norm_eps) * norm_gain[None, :]).astype(
        jnp.bfloat16
    )
    scored = (
        jax.nn.gelu(
            jnp.dot(
                features,
                up_full,
                preferred_element_type=jnp.float32,
            )
        )
        * head_weight[None, :]
    )
    partial_value = jnp.sum(jnp.sum(scored, axis=1).reshape(local_particles, local_tokens), axis=1)
    partial_value = partial_value / math.sqrt(total_tokens)
    log_weights = weigh(partial_value, prev_logw, seq_count, dom_count)
    slot = lax.rem(ancestors // local_particles - dom + dom_count, dom_count)
    row = slot * local_particles + lax.rem(ancestors, local_particles)
    resampled = jnp.take(jnp.concatenate(candidates), row, axis=0, mode="clip")
    return (resampled, log_weights)


def solution(mesh):
    in_specs = (
        P(("groups", "dom"), "seq", None),
        P(("groups", "dom"), "seq", None),
        P(("groups", "dom"), "seq", None),
        P(("groups", "dom"), "seq", None),
        P(),
        P("groups"),
        P("seq", None),
        P(),
        P(None, "seq"),
        P(),
        P(("groups", "dom")),
        P(("groups", "dom")),
    )
    out_specs = (P(("groups", "dom"), "seq", None), P(("groups", "dom")))
    return jax.shard_map(
        on_device, mesh=mesh, in_specs=in_specs, out_specs=out_specs, check_vma=False
    )
```
